32 devices in a mesh: rep: 4 (over y, x), seq: 8 (over z, core).
Axes of the slice: x: 2, y: 2, z: 4, core: 2. Of those that a mesh axis runs over, the one named last changes fastest.
Arguments:
- inputs: bfloat16 [4, 2048, 1536], P('rep', 'seq'), may hold values from -13 to 13
- segment_ids: int32 [4, 2048], P('rep'), may hold values from 0 to 7, as said below
- valid_mask: int32 [4, 2048], P('rep'), may hold values from 0 to 1, as said below
- input_weight: bfloat16 [1536, 4608], P('seq'), may hold values from -0.15625 to 0.15625
- output_weight: bfloat16 [1536, 1536], P('seq'), may hold values from -0.15625 to 0.15625
- conv_kernel: float32 [16, 6, 11], replicated, may hold values from -1.2 to 1.2
- head_mix: float32 [8, 2, 2], replicated, may hold values from 0.2 to 1
- first_gain: float32 [1536], replicated, may hold values from 0.5 to 1.5
- second_gain: float32 [1536], replicated, may hold values from 0.5 to 1.5
- group_gain: float32 [1536], replicated, may hold values from 0.5 to 1.5
- gate_weight: bfloat16 [1536, 4096], P(None, 'seq'), may hold values from -0.15625 to 0.15625
- up_weight: bfloat16 [1536, 4096], P(None, 'seq'), may hold values from -0.15625 to 0.15625
- down_weight: bfloat16 [4096, 1536], P('seq'), may hold values from -0.09375 to 0.09375
- cotangent: bfloat16 [4, 2048, 1536], P('rep', 'seq'), may hold values from -17 to 17
Outputs:
- output: bfloat16 [4, 2048, 1536], P('rep', 'seq')
- grad_inputs: bfloat16 [4, 2048, 1536], P('rep', 'seq')
- grad_input_weight: float32 [1536, 4608], P('seq')
- grad_output_weight: float32 [1536, 1536], P('seq')
- grad_kernel: float32 [16, 6, 11], replicated
- grad_mix: float32 [8, 2, 2], replicated
- grad_first_gain: float32 [1536], replicated
- grad_second_gain: float32 [1536], replicated
- grad_group_gain: float32 [1536], replicated
- grad_gate: float32 [1536, 4096], P(None, 'seq')
- grad_up: float32 [1536, 4096], P(None, 'seq')
- grad_down: float32 [4096, 1536], P('seq')
The draws below stay inside these ranges and needn't reach their ends.
Inputs may be any that keep to these rules, and one draw needn't show every extreme that they name: `segment_ids`: segment ids never fall along a sequence and start at 0. The positions k * 1024 to (k + 1) * 1024 - 1 form frame k; every document lies inside one frame, a frame holds one to four documents, the first frame of the first sequence is a single document of exactly 1024 positions, and every frame of the last sequence holds four documents. `valid_mask`: in each frame the positions with 0 form its tail, at most 256 of them; the first frame of the first sequence has none.
All inputs are finite; a program needn't handle non-finite values.
Results may differ from the reference program's by a relative error of at most 0.02.
Values may be sent and summed in bfloat16 or wider, within the bound.
A program may use at most 384 MiB of HBM per device.

```python
import jax
import jax.numpy as jnp
from jax import lax

D = 1536
HEADS = 16
HEAD_DIM = 96
FF = 4096
QCONV = 6
KCONV = 11
MAXDOC = 1024
SEQLEN = 2048
REPS = 4


def document_layout(key):
    frames = SEQLEN // MAXDOC
    base = jax.random.fold_in(key, 7)
    key_pad, key_cut, key_full = jax.random.split(base, 3)
    position = jnp.arange(SEQLEN, dtype=jnp.int32)
    within = position % MAXDOC
    frame_index = position // MAXDOC
    padding = jax.random.randint(key_pad, (REPS, frames), 0, MAXDOC // 4 + 1)
    cut_points = jax.random.randint(key_cut, (REPS, frames, 3), 1, MAXDOC)
    quarter = MAXDOC // 4
    spread_cuts = jax.random.randint(key_full, (REPS, frames, 3), 1, quarter + 1)
    spread_cuts = spread_cuts + jnp.arange(3, dtype=jnp.int32)[None, None, :] * quarter
    last_row = (jnp.arange(REPS, dtype=jnp.int32) == REPS - 1)[:, None, None]
    cut_points = jnp.where(last_row, spread_cuts, cut_points)
    leading = (jnp.arange(REPS, dtype=jnp.int32)[:, None] == 0) & (jnp.arange(frames, dtype=jnp.int32)[None, :] == 0)
    padding = jnp.where(leading, 0, padding)
    frame_cuts = cut_points[:, frame_index, :]
    marked = jnp.any(frame_cuts == within[None, :, None], axis=-1) & jnp.logical_not(leading[:, frame_index])
    boundary = (within[None, :] == 0) | marked
    segment = jnp.cumsum(boundary.astype(jnp.int32), axis=1) - 1
    live = (within[None, :] < MAXDOC - padding[:, frame_index]).astype(jnp.int32)
    return (segment.astype(jnp.int32), live)


def draw_segment_ids(key, part):
    return document_layout(key)[0]


def draw_valid_mask(key, part):
    return document_layout(key)[1]


def draw_inputs(key, part):
    base = jax.random.fold_in(key, 11)
    key_rows, key_cols, key_vals = jax.random.split(base, 3)
    col_scale = jnp.exp(jax.random.uniform(key_cols, (D,), jnp.float32, -0.58, 0.58))
    row_scale = jnp.exp(jax.random.uniform(key_rows, (REPS, SEQLEN, 1), jnp.float32, -0.58, 0.58))
    values = jax.random.normal(key_vals, (REPS, SEQLEN, D), jnp.float32)
    values = jnp.clip(values, -4.0, 4.0)
    return (values * col_scale * row_scale).astype(jnp.bfloat16)


def draw_cotangent(key, part):
    base = jax.random.fold_in(key, 13)
    key_cols, key_vals = jax.random.split(base, 2)
    col_scale = jnp.exp(jax.random.uniform(key_cols, (D,), jnp.float32, -0.35, 0.35))
    ramp = 1.0 + 2.0 * jnp.arange(SEQLEN, dtype=jnp.float32) / (SEQLEN - 1)
    values = jax.random.normal(key_vals, (REPS, SEQLEN, D), jnp.float32)
    values = jnp.clip(values, -4.0, 4.0)
    return (values * col_scale * ramp[None, :, None]).astype(jnp.bfloat16)


def shard_levels(rng, extent, shards, smallest, high):
    level, own = 1.0, jax.random.fold_in(rng, 6)
    for dim, parts in shards:
        steps = jnp.exp(jax.random.uniform(jax.random.fold_in(own, dim), (parts,), jnp.float32, smallest / len(shards), high / len(shards)))
        level = level * jnp.repeat(steps, extent[dim] // parts).reshape([-1 if axis == dim else 1 for axis in range(len(extent))])
    return level


def normal_values(stream_key, shape, scale, most, cuts=(), held_as=jnp.bfloat16):
    entries = scale * jax.random.normal(stream_key, shape, jnp.float32)
    if cuts:
        entries = entries * shard_levels(stream_key, shape, cuts, -0.22, 0.18)
    return jnp.clip(entries, -most, most).astype(held_as)


def setup_inputs(seed: int = 0) -> dict:
    arg_keys = jax.random.split(jax.random.key(seed), 15)
    inputs = draw_inputs(jax.random.fold_in(arg_keys[14], 71), 0)
    segment_ids = draw_segment_ids(jax.random.fold_in(arg_keys[14], 71), 0)
    valid_mask = draw_valid_mask(jax.random.fold_in(arg_keys[14], 71), 0)
    input_weight = normal_values(arg_keys[3], (D, 3 * D), D ** -0.5, 0.15625, ((0, 8),))
    output_weight = normal_values(arg_keys[4], (D, D), D ** -0.5, 0.15625, ((0, 8),))
    conv_kernel = normal_values(arg_keys[5], (HEADS, QCONV, KCONV), 0.3, 1.2, (), jnp.float32)
    head_mix = jnp.clip(jax.random.uniform(arg_keys[6], (HEADS // 2, 2, 2), jnp.float32, 0.2, 1.0), 0.2, 1.0)
    first_gain = jnp.clip(1.0 + 0.1 * jax.random.normal(arg_keys[7], (D,), jnp.float32), 0.5, 1.5)
    second_gain = jnp.clip(1.0 + 0.1 * jax.random.normal(arg_keys[8], (D,), jnp.float32), 0.5, 1.5)
    group_gain = jnp.clip(1.0 + 0.1 * jax.random.normal(arg_keys[9], (D,), jnp.float32), 0.5, 1.5)
    gate_weight = normal_values(arg_keys[10], (D, FF), D ** -0.5, 0.15625, ((1, 8),))
    up_weight = normal_values(arg_keys[11], (D, FF), D ** -0.5, 0.15625, ((1, 8),))
    down_weight = normal_values(arg_keys[12], (FF, D), FF ** -0.5, 0.09375, ((0, 8),))
    cotangent = draw_cotangent(jax.random.fold_in(arg_keys[14], 71), 0)
    return {"inputs": inputs, "segment_ids": segment_ids, "valid_mask": valid_mask, "input_weight": input_weight, "output_weight": output_weight, "conv_kernel": conv_kernel, "head_mix": head_mix, "first_gain": first_gain, "second_gain": second_gain, "group_gain": group_gain, "gate_weight": gate_weight, "up_weight": up_weight, "down_weight": down_weight, "cotangent": cotangent}


EPS = 1e-06
HIGHEST = lax.Precision.HIGHEST

@jax.custom_vjp
def low(v):
    return lax.optimization_barrier(v.astype(jnp.bfloat16)).astype(jnp.float32)

@jax.custom_vjp
def low_back(v):
    return v

def low_keep(v):
    return (low(v), None)

def low_pass(kept, grad):
    return (grad,)

def back_keep(v):
    return (v, None)

def back_low(kept, grad):
    return (low(grad),)
low.defvjp(low_keep, low_pass)
low_back.defvjp(back_keep, back_low)

def rms_norm(values, gain):
    return values * lax.rsqrt(lax.optimization_barrier(jnp.mean(values * values, axis=-1, keepdims=True)) + EPS) * gain

def group_norm(values, gain):
    shaped = values.reshape(values.shape[:-1] + (HEADS, HEAD_DIM))
    centred = shaped - lax.optimization_barrier(jnp.mean(shaped, axis=-1, keepdims=True))
    unit = centred * lax.rsqrt(lax.optimization_barrier(jnp.mean(centred * centred, axis=-1, keepdims=True)) + EPS)
    return unit.reshape(values.shape) * gain

def convolve(logits, kernel, rows, columns):
    rim_rows = kernel.shape[1] - 1
    key_span = kernel.shape[2] - 1
    result = jnp.zeros((logits.shape[0], rows, columns), jnp.float32)
    for row_tap in range(kernel.shape[1]):
        for col_tap in range(kernel.shape[2]):
            weight = kernel[:, row_tap, col_tap][:, None, None]
            result = result + weight * logits[:, rim_rows - row_tap:rim_rows - row_tap + rows, key_span - col_tap:key_span - col_tap + columns]
    return result

def attend(query, keys, values, segment_ids, valid_mask, conv_kernel, head_mix):
    rim_rows = QCONV - 1
    half_span = KCONV // 2
    frames = SEQLEN // MAXDOC
    score_scale = HEAD_DIM ** (-0.5)
    padding = ((0, 0), (half_span, half_span), (0, 0))
    query_pad = jnp.pad(query, padding)
    keys_pad = jnp.pad(keys, padding)
    values_pad = jnp.pad(values, padding)
    segment_pad = jnp.pad(segment_ids, ((0, 0), (half_span, half_span)), constant_values=-1)
    valid_pad = jnp.pad(valid_mask, ((0, 0), (half_span, half_span)))
    position_pad = jnp.arange(SEQLEN + 2 * half_span, dtype=jnp.int32) - half_span

    def block(index):
        zero = jnp.zeros((), jnp.int32)
        row_index = (index // frames).astype(jnp.int32)
        first = (index % frames * MAXDOC).astype(jnp.int32)
        query_first = (first + (half_span - rim_rows)).astype(jnp.int32)
        value_first = (first + half_span).astype(jnp.int32)
        query_rows = lax.dynamic_slice(query_pad, (row_index, query_first, zero), (1, MAXDOC + rim_rows, D))[0]
        key_rows = lax.dynamic_slice(keys_pad, (row_index, first, zero), (1, MAXDOC + 2 * half_span, D))[0]
        value_rows = lax.dynamic_slice(values_pad, (row_index, value_first, zero), (1, MAXDOC, D))[0]
        query_seg = lax.dynamic_slice(segment_pad, (row_index, query_first), (1, MAXDOC + rim_rows))[0]
        key_seg = lax.dynamic_slice(segment_pad, (row_index, first), (1, MAXDOC + 2 * half_span))[0]
        query_live = lax.dynamic_slice(valid_pad, (row_index, query_first), (1, MAXDOC + rim_rows))[0]
        key_live = lax.dynamic_slice(valid_pad, (row_index, first), (1, MAXDOC + 2 * half_span))[0]
        query_pos = lax.dynamic_slice(position_pad, (query_first,), (MAXDOC + rim_rows,))
        key_pos = lax.dynamic_slice(position_pad, (first,), (MAXDOC + 2 * half_span,))
        mask_ext = ((query_seg[:, None] == key_seg[None, :]) & (key_pos[None, :] <= query_pos[:, None]) & (query_live[:, None] > 0) & (key_live[None, :] > 0)).astype(jnp.float32)
        mask_own = mask_ext[rim_rows:, half_span:half_span + MAXDOC]
        row_valid = query_live[rim_rows:].astype(jnp.float32)[:, None]

        def head_pair(pair):
            width_pair = 2 * HEAD_DIM
            pair_first = (pair * width_pair).astype(jnp.int32)
            kernel_first = (pair * 2).astype(jnp.int32)
            query_g = lax.dynamic_slice_in_dim(query_rows, pair_first, width_pair, 1).reshape(-1, 2, HEAD_DIM)
            key_g = lax.dynamic_slice_in_dim(key_rows, pair_first, width_pair, 1).reshape(-1, 2, HEAD_DIM)
            value_g = lax.dynamic_slice_in_dim(value_rows, pair_first, width_pair, 1).reshape(-1, 2, HEAD_DIM)
            kernel_g = lax.dynamic_slice_in_dim(conv_kernel, kernel_first, 2, 0)
            mixing_g = lax.dynamic_index_in_dim(head_mix, pair.astype(jnp.int32), 0, keepdims=False)
            raw = jnp.einsum('qhd,khd->hqk', query_g, key_g, precision=HIGHEST)
            logits = raw * score_scale * mask_ext
            conv = convolve(logits, kernel_g, MAXDOC, MAXDOC)
            allowed = mask_own > 0
            peak = lax.optimization_barrier(jnp.max(jnp.where(allowed, conv, -1e+30), axis=-1, keepdims=True))
            peak = jnp.where(row_valid > 0, peak, 0.0)
            expo = jnp.where(allowed, jnp.exp(jnp.where(allowed, conv - peak, -80.0)), 0.0)
            prob = expo / (lax.optimization_barrier(jnp.sum(expo, axis=-1, keepdims=True)) + 1.0 - row_valid)
            mixed = low(jnp.einsum('gh,hqk->gqk', mixing_g, prob, precision=HIGHEST))
            result = jnp.einsum('hqk,khd->qhd', mixed, value_g, precision=HIGHEST)
            return result.reshape(MAXDOC, width_pair)
        pairs = lax.map(jax.checkpoint(head_pair), jnp.arange(HEADS // 2, dtype=jnp.int32))
        return pairs.transpose(1, 0, 2).reshape(MAXDOC, D)
    blocks = lax.map(jax.checkpoint(block), jnp.arange(REPS * frames, dtype=jnp.int32))
    return blocks.reshape(REPS, SEQLEN, D)

def forward(inputs, input_weight, output_weight, conv_kernel, head_mix, first_gain, second_gain, group_gain, gate_weight, up_weight, down_weight, segment_ids, valid_mask):
    live = valid_mask.astype(jnp.float32)[..., None]
    normed_in = low(rms_norm(inputs, first_gain))
    projected = low_back(low(jnp.einsum('rtd,de->rte', normed_in, input_weight, precision=HIGHEST)))
    query = projected[..., :D]
    keys = projected[..., D:2 * D]
    values = projected[..., 2 * D:]
    attended = low_back(attend(query, keys, values, segment_ids, valid_mask, conv_kernel, head_mix))
    normed = low(group_norm(attended, group_gain))
    branch = low_back(jnp.einsum('rtd,de->rte', normed, output_weight, precision=HIGHEST))
    resid = inputs + live * branch
    normed_mid = low(rms_norm(resid, second_gain))
    gate = low_back(jnp.einsum('rtd,df->rtf', normed_mid, gate_weight, precision=HIGHEST))
    up_proj = low_back(jnp.einsum('rtd,df->rtf', normed_mid, up_weight, precision=HIGHEST))
    hidden = low(jax.nn.silu(gate) * up_proj)
    mlp = low_back(jnp.einsum('rtf,fd->rtd', hidden, down_weight, precision=HIGHEST))
    return resid + live * mlp

def reference(inputs, segment_ids, valid_mask, input_weight, output_weight, conv_kernel, head_mix, first_gain, second_gain, group_gain, gate_weight, up_weight, down_weight, cotangent):
    params = (inputs.astype(jnp.float32), input_weight.astype(jnp.float32), output_weight.astype(jnp.float32), conv_kernel.astype(jnp.float32), head_mix.astype(jnp.float32), first_gain.astype(jnp.float32), second_gain.astype(jnp.float32), group_gain.astype(jnp.float32), gate_weight.astype(jnp.float32), up_weight.astype(jnp.float32), down_weight.astype(jnp.float32))

    def closed(*values):
        return forward(*values, segment_ids, valid_mask)
    result, pullback = jax.vjp(closed, *params)
    grads = pullback(cotangent.astype(jnp.float32))
    return (result.astype(jnp.bfloat16), grads[0].astype(jnp.bfloat16), grads[1], grads[2], grads[3], grads[4], grads[5], grads[6], grads[7], grads[8], grads[9], grads[10])
```

```python
import functools
import jax
import jax.numpy as jnp
from jax import lax
from jax.experimental import pallas as pl
from jax.experimental.pallas import tpu as pltpu
from jax.sharding import PartitionSpec as P

FRAME = 1024


EPS = 1e-06
LANES = 128
ROWS = 256
EDGE = 64
HEADER = 16
NEG = -1e30
PROB = jnp.float32

NT = (((1,), (1,)), ((), ()))
NN = (((1,), (0,)), ((), ()))


def dot(a, b, dims=NN):
    return lax.dot_general(a, b, dims, preferred_element_type=jnp.float32)


def toeplitz(kernel, scale):
    heads, taps, span = kernel.shape
    shape = (heads, 2 * LANES, taps * LANES)
    lane = lax.broadcasted_iota(jnp.int32, shape, 2)
    tap = lax.broadcasted_iota(jnp.int32, shape, 1)
    diff = lane % LANES + EDGE + span // 2 - tap
    total = jnp.zeros(shape, jnp.float32)
    for b in range(span):
        weight = jnp.repeat(kernel[:, :, b] * scale, LANES, axis=1)[:, None, :]
        total = total + jnp.where(diff == b, weight, 0.0)
    return total


def split_toeplitz(full):
    kept = lax.reduce_precision(full, exponent_bits=8, mantissa_bits=7)
    high = kept.astype(jnp.bfloat16)
    low = (full - kept).astype(jnp.bfloat16)
    return high, jnp.concatenate([high, high, low], axis=1)


def toeplitz_grad(grads, taps, span, scale):
    heads = grads.shape[0]
    shape = grads.shape
    lane = lax.broadcasted_iota(jnp.int32, shape, 2)
    tap = lax.broadcasted_iota(jnp.int32, shape, 1)
    diff = lane % LANES + EDGE + span // 2 - tap
    cols = []
    for b in range(span):
        part = jnp.sum(jnp.where(diff == b, grads, 0.0), axis=1)
        cols.append(jnp.sum(part.reshape(heads, taps, LANES), axis=-1) * scale)
    return jnp.stack(cols, axis=-1)


def lane_mask(dim):
    return lax.broadcasted_iota(jnp.int32, (ROWS, LANES), 1) < dim


def group_stats(att, dim):
    mean = jnp.sum(att, axis=-1, keepdims=True) / dim
    centred = jnp.where(lane_mask(dim), att - mean, 0.0)
    var = jnp.sum(centred * centred, axis=-1, keepdims=True) / dim
    inv = lax.rsqrt(var + EPS)
    return centred * inv, inv


def forward_kernel(
    dim, taps, q_ref, k_ref, v_ref, t_ref, rowc_ref, colp_ref, colc_ref, gain_ref, mix_ref,
    normed_ref, att_ref, prob_ref, lm_ref, lo_ref, p_ref, cv_ref, mx_ref, sm_ref, acc_ref,
):
    step = pl.program_id(1)
    first = step * ROWS
    top = pl.multiple_of(first + EDGE - HEADER, 16)
    tall = ROWS + HEADER
    codes = rowc_ref[pl.ds(top, tall), :]
    ipos = first - HEADER + lax.broadcasted_iota(jnp.int32, (tall, LANES), 0)
    lane = lax.broadcasted_iota(jnp.int32, (tall, LANES), 1)
    live = codes[HEADER:] >= 0

    def logits(c, carry):
        at = pl.multiple_of(c * LANES, LANES)
        keep = (codes == colp_ref[:, pl.ds(at, LANES)]) & (at - EDGE + lane <= ipos)
        for h in range(2):
            cols = slice(h * LANES, (h + 1) * LANES)
            raw = dot(q_ref[pl.ds(top, tall), cols], k_ref[pl.ds(at, LANES), cols], NT)
            raw = jnp.where(keep, raw, 0.0)
            high = raw.astype(jnp.bfloat16)
            lm_ref[h, :, pl.ds(at, LANES)] = high
            lo_ref[h, :, pl.ds(at, LANES)] = (raw - high.astype(jnp.float32)).astype(jnp.bfloat16)
        return carry

    lax.fori_loop(0, 2 * step + 3, logits, 0)
    mx_ref[...] = jnp.full(mx_ref.shape, NEG, jnp.float32)
    blocks = 2 * step + 2

    def convolve(c, carry):
        at = pl.multiple_of(c * LANES, LANES)
        keep = (codes[HEADER:] == colc_ref[:, pl.ds(at, LANES)]) & (at + lane[HEADER:] <= ipos[HEADER:])
        for h in range(2):
            high = lm_ref[h, :, pl.ds(at, 2 * LANES)]
            p_ref[h] = dot(jnp.concatenate([high, lo_ref[h, :, pl.ds(at, 2 * LANES)], high], axis=1), t_ref[h])
            conv = p_ref[h, HEADER:, :LANES]
            for a in range(1, taps):
                conv = conv + p_ref[h, HEADER - a : tall - a, a * LANES : (a + 1) * LANES]
            conv = jnp.where(keep, conv, NEG)
            cv_ref[h, :, pl.ds(at, LANES)] = conv
            mx_ref[h] = jnp.maximum(mx_ref[h], conv)
        return carry

    lax.fori_loop(0, blocks, convolve, 0)
    sm_ref[...] = jnp.zeros(sm_ref.shape, jnp.float32)
    for h in range(2):
        peak = jnp.max(mx_ref[h], axis=-1, keepdims=True)
        mx_ref[h] = jnp.where(live, jnp.broadcast_to(peak, (ROWS, LANES)), 0.0)

    def exponents(c, carry):
        at = pl.multiple_of(c * LANES, LANES)
        for h in range(2):
            value = jnp.exp(cv_ref[h, :, pl.ds(at, LANES)] - mx_ref[h])
            cv_ref[h, :, pl.ds(at, LANES)] = value
            sm_ref[h] = sm_ref[h] + value
        return carry

    lax.fori_loop(0, blocks, exponents, 0)
    for h in range(2):
        total = jnp.sum(sm_ref[h], axis=-1, keepdims=True)
        total = jnp.where(live, jnp.broadcast_to(total, (ROWS, LANES)), 1.0)
        sm_ref[h] = 1.0 / total
    acc_ref[...] = jnp.zeros(acc_ref.shape, jnp.float32)
    pair = pl.program_id(0)
    mix = [[mix_ref[pair, 2 * g + h] for h in range(2)] for g in range(2)]

    def mixing(c, carry):
        at = pl.multiple_of(c * LANES, LANES)
        prob = [cv_ref[h, :, pl.ds(at, LANES)] * sm_ref[h] for h in range(2)]
        for g in range(2):
            cols = slice(g * LANES, (g + 1) * LANES)
            prob_ref[g, :, pl.ds(at, LANES)] = prob[g].astype(prob_ref.dtype)
            mixed = (mix[g][0] * prob[0] + mix[g][1] * prob[1]).astype(jnp.bfloat16)
            acc_ref[g] += dot(mixed, v_ref[pl.ds(at + EDGE, LANES), cols])
        return carry

    lax.fori_loop(0, blocks, mixing, 0)
    for g in range(2):
        att = acc_ref[g]
        att_ref[:, g * LANES : (g + 1) * LANES] = att
        unit, _ = group_stats(att, dim)
        normed = unit * gain_ref[0:1, g * LANES : (g + 1) * LANES]
        normed_ref[:, g * LANES : (g + 1) * LANES] = normed.astype(jnp.bfloat16)


def backward_kernel(
    dim, taps, q_ref, k_ref, v_ref, t_ref, rowc_ref, colp_ref, colt_ref, rowt_ref, prob_ref, att_ref, dn_ref,
    gain_ref, mix_ref, dq_ref, dk_ref, dv_ref, g_ref, dmix_ref, dgain_ref,
    dp_ref, dc_ref, dl_ref, lt_ref, dkt_ref, dvt_ref, datt_ref, dattt_ref, qt_ref, rs_ref, dqa_ref, dm_ref, ahead_ref,
):
    pair = pl.program_id(0)
    turn = pl.program_id(1)
    step = pl.num_programs(1) - 1 - turn
    first = pl.multiple_of(step * ROWS, ROWS)
    own = pl.multiple_of(first + EDGE, 16)
    codes = rowc_ref[pl.ds(own, ROWS), :]
    ipos = first + lax.broadcasted_iota(jnp.int32, (ROWS, LANES), 0)
    lane = lax.broadcasted_iota(jnp.int32, (ROWS, LANES), 1)
    blocks = 2 * step + 2
    mix = [[mix_ref[pair, 2 * g + h] for h in range(2)] for g in range(2)]

    @pl.when(turn == 0)
    def _():
        dc_ref[...] = jnp.zeros(dc_ref.shape, jnp.float32)
        dkt_ref[...] = jnp.zeros(dkt_ref.shape, jnp.float32)
        dvt_ref[...] = jnp.zeros(dvt_ref.shape, jnp.float32)
        g_ref[...] = jnp.zeros(g_ref.shape, jnp.float32)
        dmix_ref[...] = jnp.zeros(dmix_ref.shape, jnp.float32)
        dgain_ref[...] = jnp.zeros(dgain_ref.shape, jnp.float32)
        for ref in (dq_ref, dv_ref):
            ref[:EDGE, :] = jnp.zeros((EDGE, 2 * LANES), jnp.bfloat16)
            ref[ref.shape[0] - EDGE :, :] = jnp.zeros((EDGE, 2 * LANES), jnp.bfloat16)

    @pl.when(turn > 0)
    def _():
        for h in range(2):
            dc_ref[h, ROWS:, :] = dc_ref[h, :8, :]

    for g in range(2):
        cols = slice(g * LANES, (g + 1) * LANES)
        unit, inv = group_stats(att_ref[:, cols], dim)
        grad = dn_ref[:, cols]
        dgain_ref[0:1, cols] += jnp.sum(grad * unit, axis=0, keepdims=True)
        scaled = grad * gain_ref[0:1, cols]
        mean = jnp.sum(scaled, axis=-1, keepdims=True) / dim
        inner = jnp.sum(scaled * unit, axis=-1, keepdims=True) / dim
        datt = inv * (scaled - mean - unit * inner)
        datt = jnp.where(lane_mask(dim), datt, 0.0)
        high = datt.astype(jnp.bfloat16)
        datt_ref[g, :, :LANES] = high
        datt_ref[g, :, LANES:] = (datt - high.astype(jnp.float32)).astype(jnp.bfloat16)
        dattt_ref[g] = datt.T.astype(jnp.bfloat16)
        qt_ref[g] = q_ref[pl.ds(own, ROWS), cols].astype(jnp.float32).T.astype(jnp.bfloat16)
    rs_ref[...] = jnp.zeros(rs_ref.shape, jnp.float32)
    dm_ref[...] = jnp.zeros(dm_ref.shape, jnp.float32)

    def probs(c, carry):
        at = pl.multiple_of(c * LANES, LANES)
        prob = [prob_ref[h, :, pl.ds(at, LANES)].astype(jnp.float32) for h in range(2)]
        dmixed = []
        for g in range(2):
            cols = slice(g * LANES, (g + 1) * LANES)
            value = v_ref[pl.ds(at + EDGE, LANES), cols]
            dmixed.append(dot(datt_ref[g], jnp.concatenate([value, value], axis=1), NT))
            mixed = (mix[g][0] * prob[0] + mix[g][1] * prob[1]).astype(jnp.bfloat16)
            dvt_ref[g, :, pl.ds(at, LANES)] += dot(dattt_ref[g], mixed)
            for h in range(2):
                dm_ref[2 * g + h] += dmixed[g] * prob[h]
        for h in range(2):
            dprob = mix[0][h] * dmixed[0] + mix[1][h] * dmixed[1]
            dp_ref[h, :, pl.ds(at, LANES)] = dprob
            rs_ref[h] += prob[h] * dprob
        return carry

    lax.fori_loop(0, blocks, probs, 0)
    for h in range(2):
        rs_ref[h] = jnp.broadcast_to(jnp.sum(rs_ref[h], axis=-1, keepdims=True), (ROWS, LANES))
    for n in range(4):
        dmix_ref[0, n : n + 1, :] += jnp.sum(dm_ref[n], axis=0, keepdims=True)

    tlane = lax.broadcasted_iota(jnp.int32, (LANES, ROWS), 1)
    trow = lax.broadcasted_iota(jnp.int32, (LANES, ROWS), 0)

    def transposed_logits(c, carry):
        at = pl.multiple_of(c * LANES, LANES)
        wide = jnp.concatenate([colt_ref[pl.ds(at, LANES), :]] * 2, axis=1)
        keep = (wide == rowt_ref[:, pl.ds(first, ROWS)]) & (at - EDGE + trow <= first + tlane)
        for h in range(2):
            cols = slice(h * LANES, (h + 1) * LANES)
            raw = dot(k_ref[pl.ds(at, LANES), cols], q_ref[pl.ds(own, ROWS), cols], NT)
            lt_ref[h, pl.ds(at, LANES), :] = jnp.where(keep, raw, 0.0).astype(jnp.bfloat16)
            dl_ref[h, :, pl.ds(at, LANES)] = jnp.zeros((ROWS, LANES), jnp.float32)
        return carry

    lax.fori_loop(0, blocks + 1, transposed_logits, 0)

    def convolve(c, carry):
        at = pl.multiple_of(c * LANES, LANES)
        for h in range(2):
            prob = prob_ref[h, :, pl.ds(at, LANES)].astype(jnp.float32)
            dc_ref[h, :ROWS, pl.ds(at, LANES)] = prob * (dp_ref[h, :, pl.ds(at, LANES)] - rs_ref[h])
            shifted = jnp.concatenate(
                [dc_ref[h, a : a + ROWS, pl.ds(at, LANES)].astype(jnp.bfloat16) for a in range(taps)], axis=1
            )
            g_ref[h] += dot(lt_ref[h, pl.ds(at, 2 * LANES), :], shifted)
            dl_ref[h, :, pl.ds(at, 2 * LANES)] += dot(shifted, t_ref[h], NT)
        return carry

    lax.fori_loop(0, blocks, convolve, 0)
    dqa_ref[...] = jnp.zeros(dqa_ref.shape, jnp.float32)

    def logits(c, carry):
        at = pl.multiple_of(c * LANES, LANES)
        keep = (codes == colp_ref[:, pl.ds(at, LANES)]) & (at - EDGE + lane <= ipos)
        for h in range(2):
            cols = slice(h * LANES, (h + 1) * LANES)
            dl = jnp.where(keep, dl_ref[h, :, pl.ds(at, LANES)], 0.0).astype(jnp.bfloat16)
            dqa_ref[h] += dot(dl, k_ref[pl.ds(at, LANES), cols])
            dkt_ref[h, :, pl.ds(at, LANES)] += dot(qt_ref[h], dl)
        return carry

    lax.fori_loop(0, blocks + 1, logits, 0)
    for h in range(2):
        dq_ref[pl.ds(own, ROWS), h * LANES : (h + 1) * LANES] = dqa_ref[h].astype(jnp.bfloat16)

    @pl.when(step == 0)
    def _():
        head = slice(EDGE - HEADER, EDGE)
        wide = (HEADER, 2 * LANES)
        keep = jnp.concatenate([rowc_ref[head, :]] * 2, axis=1) == colp_ref[:, : 2 * LANES]
        keep = keep & (
            lax.broadcasted_iota(jnp.int32, wide, 1) - EDGE <= lax.broadcasted_iota(jnp.int32, wide, 0) - HEADER
        )
        for h in range(2):
            cols = slice(h * LANES, (h + 1) * LANES)
            ahead_ref[:HEADER, :] = jnp.zeros((HEADER, LANES), jnp.float32)
            ahead_ref[HEADER:, :] = dc_ref[h, :HEADER, :LANES]
            shifted = jnp.concatenate(
                [ahead_ref[a : a + HEADER, :].astype(jnp.bfloat16) for a in range(taps)], axis=1
            )
            near = k_ref[: 2 * LANES, cols]
            query = q_ref[head, cols]
            raw = jnp.where(keep, dot(query, near, NT), 0.0)
            g_ref[h] += dot(raw.T.astype(jnp.bfloat16), shifted)
            dl = jnp.where(keep, dot(shifted, t_ref[h], NT), 0.0).astype(jnp.bfloat16)
            dq_ref[head, cols] = dot(dl, near).astype(jnp.bfloat16)
            dkt_ref[h, :, : 2 * LANES] += dot(query.astype(jnp.float32).T.astype(jnp.bfloat16), dl)
            dk_ref[:, cols] = dkt_ref[h].T.astype(jnp.bfloat16)
            dv_ref[pl.ds(EDGE, dvt_ref.shape[2]), cols] = dvt_ref[h].T.astype(jnp.bfloat16)


def attention_forward(proj, toep, codes, gain, mix, dim, taps):
    tall = proj.shape[0]
    frame = tall - 2 * EDGE
    pairs = mix.shape[0]
    steps = frame // ROWS
    whole = lambda off: pl.BlockSpec((tall, 2 * LANES), lambda p, r: (0, off * pairs + p))
    wide = pairs * 2 * LANES
    return pl.pallas_call(
        functools.partial(forward_kernel, dim, taps),
        grid=(pairs, steps),
        in_specs=[
            whole(0), whole(1), whole(2),
            pl.BlockSpec((2, 6 * LANES, taps * LANES), lambda p, r: (p, 0, 0)),
            pl.BlockSpec((tall, LANES), lambda p, r: (0, 0)),
            pl.BlockSpec((1, tall), lambda p, r: (0, 0)),
            pl.BlockSpec((1, frame), lambda p, r: (0, 0)),
            pl.BlockSpec((1, 2 * LANES), lambda p, r: (0, p)),
            pl.BlockSpec(memory_space=pltpu.SMEM),
        ],
        out_specs=[
            pl.BlockSpec((ROWS, 2 * LANES), lambda p, r: (r, p)),
            pl.BlockSpec((ROWS, 2 * LANES), lambda p, r: (r, p)),
            pl.BlockSpec((2, ROWS, frame), lambda p, r: (p, r, 0)),
        ],
        out_shape=[
            jax.ShapeDtypeStruct((frame, wide), jnp.bfloat16),
            jax.ShapeDtypeStruct((frame, wide), jnp.float32),
            jax.ShapeDtypeStruct((2 * pairs, frame, frame), PROB),
        ],
        scratch_shapes=[
            pltpu.VMEM((2, ROWS + HEADER, tall), jnp.bfloat16),
            pltpu.VMEM((2, ROWS + HEADER, tall), jnp.bfloat16),
            pltpu.VMEM((2, ROWS + HEADER, taps * LANES), jnp.float32),
            pltpu.VMEM((2, ROWS, frame), jnp.float32),
            pltpu.VMEM((2, ROWS, LANES), jnp.float32),
            pltpu.VMEM((2, ROWS, LANES), jnp.float32),
            pltpu.VMEM((2, ROWS, LANES), jnp.float32),
        ],
        cost_estimate=pl.CostEstimate(flops=60_000_000_000, bytes_accessed=40_000_000, transcendentals=0),
        compiler_params=pltpu.CompilerParams(vmem_limit_bytes=48 << 20),
        name="attend",
    )(proj, proj, proj, toep, codes["row"], codes["colp"], codes["col"], gain, mix)


def attention_backward(proj, toep, codes, prob, att, dnormed, gain, mix, dim, taps):
    tall = proj.shape[0]
    frame = tall - 2 * EDGE
    pairs = mix.shape[0]
    steps = frame // ROWS
    whole = lambda off: pl.BlockSpec((tall, 2 * LANES), lambda p, r: (0, off * pairs + p))
    wide = pairs * 2 * LANES
    back = lambda r: steps - 1 - r
    return pl.pallas_call(
        functools.partial(backward_kernel, dim, taps),
        grid=(pairs, steps),
        in_specs=[
            whole(0), whole(1), whole(2),
            pl.BlockSpec((2, 2 * LANES, taps * LANES), lambda p, r: (p, 0, 0)),
            pl.BlockSpec((tall, LANES), lambda p, r: (0, 0)),
            pl.BlockSpec((1, tall), lambda p, r: (0, 0)),
            pl.BlockSpec((tall, LANES), lambda p, r: (0, 0)),
            pl.BlockSpec((1, frame), lambda p, r: (0, 0)),
            pl.BlockSpec((2, ROWS, frame), lambda p, r: (p, back(r), 0)),
            pl.BlockSpec((ROWS, 2 * LANES), lambda p, r: (back(r), p)),
            pl.BlockSpec((ROWS, 2 * LANES), lambda p, r: (back(r), p)),
            pl.BlockSpec((1, 2 * LANES), lambda p, r: (0, p)),
            pl.BlockSpec(memory_space=pltpu.SMEM),
        ],
        out_specs=[
            pl.BlockSpec((tall, 2 * LANES), lambda p, r: (0, p)),
            pl.BlockSpec((tall, 2 * LANES), lambda p, r: (0, p)),
            pl.BlockSpec((tall, 2 * LANES), lambda p, r: (0, p)),
            pl.BlockSpec((2, 2 * LANES, taps * LANES), lambda p, r: (p, 0, 0)),
            pl.BlockSpec((1, 8, LANES), lambda p, r: (p, 0, 0)),
            pl.BlockSpec((1, 2 * LANES), lambda p, r: (0, p)),
        ],
        out_shape=[
            jax.ShapeDtypeStruct((tall, wide), jnp.bfloat16),
            jax.ShapeDtypeStruct((tall, wide), jnp.bfloat16),
            jax.ShapeDtypeStruct((tall, wide), jnp.bfloat16),
            jax.ShapeDtypeStruct((2 * pairs, 2 * LANES, taps * LANES), jnp.float32),
            jax.ShapeDtypeStruct((pairs, 8, LANES), jnp.float32),
            jax.ShapeDtypeStruct((1, wide), jnp.float32),
        ],
        scratch_shapes=[
            pltpu.VMEM((2, ROWS, frame), jnp.float32),
            pltpu.VMEM((2, ROWS + 8, frame), jnp.float32),
            pltpu.VMEM((2, ROWS, tall), jnp.float32),
            pltpu.VMEM((2, tall, ROWS), jnp.bfloat16),
            pltpu.VMEM((2, LANES, tall), jnp.float32),
            pltpu.VMEM((2, LANES, frame), jnp.float32),
            pltpu.VMEM((2, ROWS, 2 * LANES), jnp.bfloat16),
            pltpu.VMEM((2, LANES, ROWS), jnp.bfloat16),
            pltpu.VMEM((2, LANES, ROWS), jnp.bfloat16),
            pltpu.VMEM((2, ROWS, LANES), jnp.float32),
            pltpu.VMEM((2, ROWS, LANES), jnp.float32),
            pltpu.VMEM((4, ROWS, LANES), jnp.float32),
            pltpu.VMEM((2 * HEADER, LANES), jnp.float32),
        ],
        cost_estimate=pl.CostEstimate(flops=70_000_000_000, bytes_accessed=40_000_000, transcendentals=0),
        compiler_params=pltpu.CompilerParams(vmem_limit_bytes=48 << 20),
        name="attend_back",
    )(proj, proj, proj, toep, codes["row"], codes["colp"], codes["colt"], codes["rowt"], prob, att, dnormed, gain, mix)


def make_codes(segment, valid):
    row = jnp.where(valid > 0, segment, -1)
    col = jnp.where(valid > 0, segment, -2)
    rowp = jnp.pad(row, (EDGE - HEADER, EDGE), constant_values=-1)
    colp = jnp.pad(col, (EDGE - HEADER, EDGE), constant_values=-2)
    tall = rowp.shape[0]
    return {
        "row": jnp.broadcast_to(rowp[:, None], (tall, LANES)),
        "colt": jnp.broadcast_to(colp[:, None], (tall, LANES)),
        "colp": colp[None],
        "col": col[None, HEADER:],
        "rowt": row[None, HEADER:],
    }


MESH = pl.DeviceIdType.MESH


def meet(peers):
    barrier = pltpu.get_barrier_semaphore()
    for peer in peers:
        pl.semaphore_signal(barrier, inc=1, device_id=peer, device_id_type=MESH)
    pl.semaphore_wait(barrier, len(peers))


def send(src, dst, send_sem, recv_sem, peer):
    return pltpu.make_async_remote_copy(
        src_ref=src, dst_ref=dst, send_sem=send_sem, recv_sem=recv_sem, device_id=peer, device_id_type=MESH
    )


def gather_kernel(
    reps, count, w_ref, x_ref, z_ref, wc_ref, f_ref, own_sem, side_send, side_recv, far_send, far_recv, rep_send, rep_recv,
    tok_send, tok_recv, head_send, head_recv,
):
    rep = lax.axis_index("rep")
    me = lax.axis_index("seq")
    chips = count // 2
    chip, core = me // 2, me % 2
    rows = w_ref.shape[0]
    part = rows // reps
    full = w_ref.shape[1] // 3
    cols = wc_ref.shape[1] // 3
    tokens = x_ref.shape[0]
    place = me % 4
    sibling = chip * 2 + 1 - core
    far_ids = [((chip + k) % chips) * 2 + e for k in range(1, chips) for e in range(2)]
    rep_ids = [(rep + k) % reps for k in range(1, reps)]
    at = lambda r, s: (r, s)
    meet([at(rep, s) for s in far_ids + [sibling]] + [at(r, me) for r in rep_ids])

    def source(first, size, who, t):
        left = pl.multiple_of(t * full + (who % 4) * cols, LANES)
        return w_ref.at[pl.ds(first, size), pl.ds(left, cols)]

    def target(first, size, t):
        return wc_ref.at[pl.ds(first, size), pl.ds(t * cols, cols)]

    def spot(who, r):
        return pl.multiple_of(who * rows + r * part, 16)

    def token_rows(who, half):
        return f_ref.at[pl.ds(pl.multiple_of(EDGE + (who % 4) * tokens + half * (tokens // 2), 16), tokens // 2), :]

    waits = []
    quarter = pl.multiple_of(rep * part, 16)
    for n, who in enumerate(far_ids):
        for t in range(3):
            copy = send(
                source(quarter, part, who, t), target(spot(me, rep), part, t), far_send.at[n, t], far_recv.at[me, t],
                at(rep, who),
            )
            copy.start()
            waits.append(copy)
    for t in range(3):
        copy = send(
            source(0, rows, sibling, t), target(spot(me, 0), rows, t), side_send.at[t], side_recv.at[t], at(rep, sibling)
        )
        copy.start()
        waits.append(copy)
    partner = (chip ^ 1) * 2 + core
    for half in range(2):
        mine = x_ref.at[pl.ds(half * (tokens // 2), tokens // 2), :]
        copy = send(mine, token_rows(me, half), tok_send.at[0, half], tok_recv.at[0, half], at(rep, partner))
        copy.start()
        waits.append(copy)
        copy = send(mine, token_rows(me, half), tok_send.at[1, half], tok_recv.at[1, half], at(rep, sibling))
        copy.start()
        waits.append(copy)
    local = [
        pltpu.make_async_copy(source(0, rows, me, t), target(spot(me, 0), rows, t), own_sem.at[t]) for t in range(3)
    ]
    lead = EDGE - HEADER
    local.append(pltpu.make_async_copy(z_ref.at[pl.ds(0, lead), :], f_ref.at[pl.ds(0, lead), :], own_sem.at[4]))
    local.append(
        pltpu.make_async_copy(z_ref, f_ref.at[pl.ds(f_ref.shape[0] - EDGE, EDGE), :], own_sem.at[5])
    )
    local.append(pltpu.make_async_copy(
        x_ref, f_ref.at[pl.ds(pl.multiple_of(EDGE + place * tokens, 16), tokens), :], own_sem.at[3]
    ))
    for copy in local:
        copy.start()
    head = f_ref.at[pl.ds(lead, HEADER), :]
    fill = pltpu.make_async_copy(z_ref.at[pl.ds(0, HEADER), :], head, own_sem.at[6])
    sends_on = (place == 3) & (me < count - 4)
    after = [
        send(x_ref.at[pl.ds(tokens - HEADER, HEADER), :], head, head_send.at[v], head_recv.at[0],
             at(rep, lax.rem(me + 1 + v, count)))
        for v in range(4)
    ]

    @pl.when(sends_on)
    def _():
        for copy in after:
            copy.start()

    @pl.when(me < 4)
    def _():
        fill.start()

    for n, who in enumerate(far_ids):
        for t in range(3):
            got = target(spot(who, rep), part, t)
            send(got, got, far_send.at[n, t], far_recv.at[who, t], at(rep, who)).wait_recv()
        block = wc_ref.at[pl.ds(spot(who, rep), part), :]
        for m, r in enumerate(rep_ids):
            copy = send(block, block, rep_send.at[n, m], rep_recv.at[n, m], at(r, me))
            copy.start()
            waits.append(copy)
    for half in range(2):
        got = token_rows(partner, half)
        send(got, got, tok_send.at[0, half], tok_recv.at[0, half], at(rep, partner)).wait_recv()
        copy = send(got, got, tok_send.at[2, half], tok_recv.at[2, half], at(rep, sibling))
        copy.start()
        waits.append(copy)
    for copy in local:
        copy.wait()

    @pl.when(me < 4)
    def _():
        fill.wait()

    @pl.when(me >= 4)
    def _():
        after[0].wait_recv()

    @pl.when(sends_on)
    def _():
        for copy in after:
            copy.wait_send()

    for t in range(3):
        got = target(spot(sibling, 0), rows, t)
        send(got, got, side_send.at[t], side_recv.at[t], at(rep, sibling)).wait_recv()
    for half in range(2):
        for kind, who in ((1, sibling), (2, partner ^ 1)):
            got = token_rows(who, half)
            send(got, got, tok_send.at[kind, half], tok_recv.at[kind, half], at(rep, sibling)).wait_recv()
    for n, who in enumerate(far_ids):
        for m in range(reps - 1):
            block = wc_ref.at[pl.ds(spot(who, (rep + reps - 1 - m) % reps), part), :]
            send(block, block, rep_send.at[n, m], rep_recv.at[n, m], at(rep_ids[m], me)).wait_recv()
    for copy in waits:
        copy.wait_send()


def gather_weight(weight, tokens, reps, count):
    rows, full = weight.shape
    own = full // 4
    far = count - 2
    dma = pltpu.SemaphoreType.DMA
    return pl.pallas_call(
        functools.partial(gather_kernel, reps, count),
        in_specs=[pl.BlockSpec(memory_space=pl.ANY)] * 3,
        out_specs=[pl.BlockSpec(memory_space=pl.ANY)] * 2,
        out_shape=[
            jax.ShapeDtypeStruct((rows * count, own), weight.dtype),
            jax.ShapeDtypeStruct((tokens.shape[0] * 4 + 2 * EDGE, tokens.shape[1]), tokens.dtype),
        ],
        scratch_shapes=[
            dma((7,)), dma((3,)), dma((3,)), dma((far, 3)), dma((count, 3)), dma((far, reps - 1)), dma((far, reps - 1)),
            dma((3, 2)), dma((3, 2)), dma((4,)), dma((1,)),
        ],
        cost_estimate=pl.CostEstimate(flops=40_000_000_000, bytes_accessed=20_000_000, transcendentals=0),
        compiler_params=pltpu.CompilerParams(collective_id=1, has_side_effects=True),
        name="gather_weight",
    )(weight, tokens, jnp.zeros((EDGE, tokens.shape[1]), tokens.dtype))


def frame_gather_kernel(x_ref, f_ref, own_sem, send_sem, recv_sem):
    rep = lax.axis_index("rep")
    me = lax.axis_index("seq")
    chip, core = me // 2, me % 2
    half_rows = x_ref.shape[0] // 2
    sibling = (rep, chip * 2 + 1 - core)
    partner = (rep, (chip ^ 1) * 2 + core)
    meet([sibling, partner])

    def rows(who, half):
        return f_ref.at[pl.ds(pl.multiple_of((who % 4) * 2 * half_rows + half * half_rows, 16), half_rows), :]

    waits = []

    def push(src, dst, kind, half, peer):
        copy = send(src, dst, send_sem.at[kind, half], recv_sem.at[kind, half], peer)
        copy.start()
        waits.append(copy)

    for half in range(2):
        push(x_ref.at[pl.ds(half * half_rows, half_rows), :], rows(me, half), 0, half, partner)
    for half in range(2):
        push(x_ref.at[pl.ds(half * half_rows, half_rows), :], rows(me, half), 1, half, sibling)
    local = pltpu.make_async_copy(
        x_ref, f_ref.at[pl.ds(pl.multiple_of((me % 4) * 2 * half_rows, 16), 2 * half_rows), :], own_sem.at[0]
    )
    local.start()

    def arrived(kind, half, who):
        got = rows(who, half)
        send(got, got, send_sem.at[kind, half], recv_sem.at[kind, half], sibling).wait_recv()
        return got

    for half in range(2):
        got = arrived(0, half, partner[1])
        push(got, got, 2, half, sibling)
    local.wait()
    for half in range(2):
        arrived(1, half, sibling[1])
        arrived(2, half, partner[1] ^ 1)
    for copy in waits:
        copy.wait_send()


def frame_gather(values):
    dma = pltpu.SemaphoreType.DMA
    return pl.pallas_call(
        frame_gather_kernel,
        in_specs=[pl.BlockSpec(memory_space=pl.ANY)],
        out_specs=pl.BlockSpec(memory_space=pl.ANY),
        out_shape=jax.ShapeDtypeStruct((values.shape[0] * 4, values.shape[1]), values.dtype),
        scratch_shapes=[dma((1,)), dma((3, 2)), dma((3, 2))],
        cost_estimate=pl.CostEstimate(flops=20_000_000_000, bytes_accessed=8_000_000, transcendentals=0),
        compiler_params=pltpu.CompilerParams(collective_id=2, has_side_effects=True),
        name="frame_gather",
    )(values)


def frame_swap_kernel(h_ref, r_ref, own_sem, send_sem, recv_sem):
    rep = lax.axis_index("rep")
    me = lax.axis_index("seq")
    base, place = me // 4 * 4, me % 4
    rows = r_ref.shape[0]
    cols = h_ref.shape[1]
    peers = [base + (place ^ n) for n in (2, 3, 1)]
    meet([(rep, who) for who in peers])

    def block(who):
        return h_ref.at[pl.ds(pl.multiple_of((who % 4) * rows, 16), rows), :]

    def spot(who):
        return r_ref.at[:, pl.ds(pl.multiple_of((who % 4) * cols, LANES), cols)]

    copies = [
        send(block(who), spot(me), send_sem.at[n], recv_sem.at[n], (rep, who)) for n, who in enumerate(peers)
    ]
    for copy in copies:
        copy.start()
    local = pltpu.make_async_copy(block(me), spot(me), own_sem.at[0])
    local.start()
    local.wait()
    for n, who in enumerate(peers):
        send(block(who), spot(who), send_sem.at[n], recv_sem.at[n], (rep, who)).wait_recv()
    for copy in copies:
        copy.wait_send()


def frame_swap(values):
    dma = pltpu.SemaphoreType.DMA
    return pl.pallas_call(
        frame_swap_kernel,
        in_specs=[pl.BlockSpec(memory_space=pl.ANY)],
        out_specs=pl.BlockSpec(memory_space=pl.ANY),
        out_shape=jax.ShapeDtypeStruct((values.shape[0] // 4, values.shape[1] * 4), values.dtype),
        scratch_shapes=[dma((1,)), dma((3,)), dma((3,))],
        cost_estimate=pl.CostEstimate(flops=10_000_000_000, bytes_accessed=2_000_000, transcendentals=0),
        compiler_params=pltpu.CompilerParams(collective_id=3, has_side_effects=True),
        name="frame_swap",
    )(values)


def small_sum_kernel(reps, count, v_ref, o_ref, one_ref, two_ref, sum_ref, send1, recv1, send2, recv2):
    rep = lax.axis_index("rep")
    me = lax.axis_index("seq")
    rep_ids = [(rep + k) % reps for k in range(1, reps)]
    seq_ids = [(me + k) % count for k in range(1, count)]
    meet([(r, me) for r in rep_ids] + [(rep, s) for s in seq_ids])
    waits = []
    for m, r in enumerate(rep_ids):
        copy = send(v_ref, one_ref.at[rep], send1.at[m], recv1.at[rep], (r, me))
        copy.start()
        waits.append(copy)
    one_ref[rep] = v_ref[...]
    for m, r in enumerate(rep_ids):
        send(v_ref, one_ref.at[r], send1.at[m], recv1.at[r], (r, me)).wait_recv()
    total = one_ref[0]
    for r in range(1, reps):
        total = total + one_ref[r]
    sum_ref[...] = total
    for m, s in enumerate(seq_ids):
        copy = send(sum_ref, two_ref.at[me], send2.at[m], recv2.at[me], (rep, s))
        copy.start()
        waits.append(copy)
    two_ref[me] = total
    for m, s in enumerate(seq_ids):
        send(sum_ref, two_ref.at[s], send2.at[m], recv2.at[s], (rep, s)).wait_recv()
    total = two_ref[0]
    for s in range(1, count):
        total = total + two_ref[s]
    o_ref[...] = total
    for copy in waits:
        copy.wait_send()


def small_sum(values, reps, count):
    size = values.shape[0]
    rows = -(-size // (8 * LANES)) * 8
    shaped = jnp.pad(values, (0, rows * LANES - size)).reshape(rows, LANES)
    dma = pltpu.SemaphoreType.DMA
    vmem = pl.BlockSpec(memory_space=pltpu.VMEM)
    out = pl.pallas_call(
        functools.partial(small_sum_kernel, reps, count),
        in_specs=[vmem],
        out_specs=vmem,
        out_shape=jax.ShapeDtypeStruct(shaped.shape, jnp.float32),
        scratch_shapes=[
            pltpu.VMEM((reps, rows, LANES), jnp.float32), pltpu.VMEM((count, rows, LANES), jnp.float32),
            pltpu.VMEM((rows, LANES), jnp.float32),
            dma((reps - 1,)), dma((reps,)), dma((count - 1,)), dma((count,)),
        ],
        compiler_params=pltpu.CompilerParams(collective_id=4, has_side_effects=True),
        name="small_sum",
    )(shaped)
    return out.reshape(-1)[:size]


def reduce_kernel(
    reps, count, gi_ref, go_ref, dn_ref, oi_ref, oo_ref, od_ref,
    li_ref, ri_ref, zi_ref, qi_ref, lo_ref, ro_ref, zo_ref, qo_ref, ld_ref, bd_ref, hd_ref,
    load_sem, one_send, one_recv, two_send, two_recv, three_send, three_recv, tok_send, tok_recv,
    head_send, head_recv,
):
    rep = lax.axis_index("rep")
    me = lax.axis_index("seq")
    chip, core = me // 2, me % 2
    base, place = me // 4 * 4, me % 4
    sibling = chip * 2 + 1 - core
    partner = (chip ^ 1) * 2 + core
    rep_ids = [(rep + k) % reps for k in range(1, reps)]
    seq_ids = [(me + k) % count for k in range(1, count)]
    part = li_ref.shape[1]
    rows = part * reps
    halves = lo_ref.shape[0]
    cols = gi_ref.shape[1] // 3
    width = cols * 4
    tokens = od_ref.shape[0]
    meet([(r, me) for r in rep_ids] + [(rep, s) for s in seq_ids])
    waits = []

    def push(src, dst, send_sem, recv_sem, peer):
        copy = send(src, dst, send_sem, recv_sem, peer)
        copy.start()
        waits.append(copy)

    def arrived(dst, send_sem, recv_sem):
        send(dst, dst, send_sem, recv_sem, (rep, sibling)).wait_recv()

    def quarter(ref, who, r):
        return ref.at[pl.ds(pl.multiple_of(who * rows + r * part, 16), part), :]

    def token_rows(who):
        return dn_ref.at[pl.ds(pl.multiple_of(EDGE + (who % 4) * tokens, 16), tokens), :]

    ahead = send(
        dn_ref.at[pl.ds(EDGE - HEADER, HEADER), :], hd_ref.at[place], head_send.at[0], head_recv.at[place],
        (rep, lax.rem(base + count - 1, count)),
    )

    @pl.when(me >= 4)
    def _():
        ahead.start()

    push(token_rows(partner ^ 1), bd_ref.at[0], tok_send.at[0], tok_recv.at[0], (rep, sibling))
    push(token_rows(sibling), bd_ref.at[1], tok_send.at[1], tok_recv.at[1], (rep, sibling))
    loads = [
        pltpu.make_async_copy(token_rows(partner), ld_ref.at[0], load_sem.at[0]),
        pltpu.make_async_copy(token_rows(me), ld_ref.at[1], load_sem.at[1]),
    ]
    for copy in loads:
        copy.start()
    order = seq_ids + [me]
    for h in range(halves):
        for m, r in enumerate(rep_ids):
            push(quarter(go_ref, h, r), ro_ref.at[m, h], one_send.at[count + h, m], one_recv.at[count + h, m], (r, me))
    for n, who in enumerate(order):
        for m, r in enumerate(rep_ids):
            push(quarter(gi_ref, who, r), ri_ref.at[m, n], one_send.at[n, m], one_recv.at[n, m], (r, me))
    own = [pltpu.make_async_copy(quarter(gi_ref, who, rep), li_ref.at[n], load_sem.at[2 + n]) for n, who in enumerate(order)]
    own += [
        pltpu.make_async_copy(quarter(go_ref, h, rep), lo_ref.at[h], load_sem.at[2 + count + h]) for h in range(halves)
    ]
    for copy in own:
        copy.start()

    loads[0].wait()
    arrived(bd_ref.at[0], tok_send.at[0], tok_recv.at[0])
    wide = jnp.float32
    ld_ref[0] = (ld_ref[0].astype(wide) + bd_ref[0].astype(wide)).astype(jnp.bfloat16)
    push(ld_ref.at[0], bd_ref.at[2], tok_send.at[2], tok_recv.at[2], (rep, partner))

    def over_reps(local_ref, rest_ref, n, sems):
        total = local_ref[n].astype(wide)
        for m in range(reps - 1):
            arrived(rest_ref.at[m, n], one_send.at[sems, m], one_recv.at[sems, m])
            total = total + rest_ref[m, n].astype(wide)
        local_ref[n] = total.astype(jnp.bfloat16)

    frames = count // 4
    for h in range(halves):
        own[count + h].wait()
        over_reps(lo_ref, ro_ref, h, count + h)
        owner = place * halves + h

        @pl.when(owner == me)
        def _():
            zo_ref[me // 4] = lo_ref[h]

        @pl.when(owner != me)
        def _():
            send(lo_ref.at[h], zo_ref.at[me // 4], two_send.at[count + h], two_recv.at[count + me // 4], (rep, owner)).start()

    for n, who in enumerate(order):
        own[n].wait()
        over_reps(li_ref, ri_ref, n, n)
        if n < count - 1:
            push(li_ref.at[n], zi_ref.at[me], two_send.at[n], two_recv.at[me], (rep, who))
        else:
            zi_ref[me] = li_ref[n]

    loads[1].wait()
    arrived(bd_ref.at[1], tok_send.at[1], tok_recv.at[1])
    arrived(bd_ref.at[2], tok_send.at[2], tok_recv.at[2])
    od_ref[...] = ld_ref[1].astype(wide) + bd_ref[1].astype(wide) + bd_ref[2].astype(wide)

    @pl.when((place == 3) & (me < count - 4))
    def _():
        total = od_ref[tokens - HEADER :, :]
        for v in range(4):
            arrived(hd_ref.at[v], head_send.at[0], head_recv.at[v])
            total = total + hd_ref[v].astype(wide)
        od_ref[tokens - HEADER :, :] = total

    @pl.when(me >= 4)
    def _():
        ahead.wait_send()

    for f in range(frames):
        source = f * 4 + me // halves

        @pl.when(source != me)
        def _():
            arrived(zo_ref.at[f], two_send.at[count], two_recv.at[count + f])

    total = zo_ref[0].astype(wide)
    for f in range(1, frames):
        total = total + zo_ref[f].astype(wide)
    qo_ref[...] = total.astype(jnp.bfloat16)
    for m, r in enumerate(rep_ids):
        push(qo_ref, oo_ref.at[pl.ds(pl.multiple_of(rep * part, 16), part), :], three_send.at[0, m], three_recv.at[0, m], (r, me))
    for n, who in enumerate(seq_ids):
        arrived(zi_ref.at[who], two_send.at[n], two_recv.at[who])
    for u in range(4):
        total = zi_ref[u].astype(wide)
        for f in range(1, frames):
            total = total + zi_ref[f * 4 + u].astype(wide)
        for t in range(3):
            qi_ref[:, t * width + u * cols : t * width + (u + 1) * cols] = total[:, t * cols : (t + 1) * cols].astype(
                jnp.bfloat16
            )
    for m, r in enumerate(rep_ids):
        push(qi_ref, oi_ref.at[pl.ds(pl.multiple_of(rep * part, 16), part), :], three_send.at[1, m], three_recv.at[1, m], (r, me))
    final = [
        pltpu.make_async_copy(qo_ref, oo_ref.at[pl.ds(pl.multiple_of(rep * part, 16), part), :], load_sem.at[0]),
        pltpu.make_async_copy(qi_ref, oi_ref.at[pl.ds(pl.multiple_of(rep * part, 16), part), :], load_sem.at[1]),
    ]
    for copy in final:
        copy.start()
    for h in range(halves):
        owner = place * halves + h

        @pl.when(owner != me)
        def _():
            send(lo_ref.at[h], zo_ref.at[me // 4], two_send.at[count + h], two_recv.at[count + me // 4], (rep, owner)).wait_send()

    for copy in final:
        copy.wait()
    for m in range(reps - 1):
        r = (rep + reps - 1 - m) % reps
        for n, ref in ((0, oo_ref), (1, oi_ref)):
            arrived(ref.at[pl.ds(pl.multiple_of(r * part, 16), part), :], three_send.at[n, m], three_recv.at[n, m])
    for copy in waits:
        copy.wait_send()


def reduce_weights(grad_in, grad_out, tokens, reps, count):
    width = grad_out.shape[1]
    own = grad_in.shape[1]
    rows = width // count
    part = rows // reps
    halves = grad_out.shape[0] // rows
    frames = count // 4
    each = (tokens.shape[0] - 2 * EDGE) // 4
    dma = pltpu.SemaphoreType.DMA
    low = jnp.bfloat16
    hbm = pl.BlockSpec(memory_space=pl.ANY)
    return pl.pallas_call(
        functools.partial(reduce_kernel, reps, count),
        in_specs=[hbm] * 3,
        out_specs=[hbm, hbm, pl.BlockSpec(memory_space=pltpu.VMEM)],
        out_shape=[
            jax.ShapeDtypeStruct((rows, 3 * width), low),
            jax.ShapeDtypeStruct((rows, width), low),
            jax.ShapeDtypeStruct((each, width), jnp.float32),
        ],
        scratch_shapes=[
            pltpu.VMEM((count, part, own), low), pltpu.VMEM((reps - 1, count, part, own), low),
            pltpu.VMEM((count, part, own), low), pltpu.VMEM((part, 3 * width), low),
            pltpu.VMEM((halves, part, width), low), pltpu.VMEM((reps - 1, halves, part, width), low),
            pltpu.VMEM((frames, part, width), low), pltpu.VMEM((part, width), low),
            pltpu.VMEM((2, each, width), low), pltpu.VMEM((3, each, width), low),
            pltpu.VMEM((4, HEADER, width), low),
            dma((2 + count + halves,)), dma((count + halves, reps - 1)), dma((count + halves, reps - 1)),
            dma((count + halves,)), dma((count + frames,)), dma((2, reps - 1)), dma((2, reps - 1)), dma((3,)), dma((3,)),
            dma((1,)), dma((4,)),
        ],
        cost_estimate=pl.CostEstimate(flops=70_000_000_000, bytes_accessed=20_000_000, transcendentals=0),
        compiler_params=pltpu.CompilerParams(collective_id=5, has_side_effects=True, vmem_limit_bytes=40 << 20),
        name="reduce_weights",
    )(grad_in, grad_out, tokens)


def rms_scale(values):
    return lax.rsqrt(jnp.mean(values * values, axis=-1, keepdims=True) + EPS)


def norm_back(grad_out, values, inv_scale, gain):
    scaled_grad = grad_out * gain
    inner = jnp.mean(scaled_grad * values, axis=-1, keepdims=True)
    return inv_scale * scaled_grad - values * inv_scale**3 * inner


def pad_heads(values, dim):
    shaped = values.reshape(values.shape[:-1] + (-1, dim))
    shaped = jnp.pad(shaped, [(0, 0)] * (shaped.ndim - 1) + [(0, LANES - dim)])
    return shaped.reshape(values.shape[:-1] + (-1,))


def cut_heads(values, dim):
    shaped = values.reshape(values.shape[:-1] + (-1, LANES))[..., :dim]
    return shaped.reshape(values.shape[:-1] + (-1,))


def on_device(
    inputs, segment_ids, valid_mask, input_weight, output_weight, conv_kernel, head_mix, first_gain, second_gain,
    group_gain, gate_weight, up_weight, down_weight, cotangent,
):
    tokens, width = inputs.shape[1:]
    heads, taps, span = conv_kernel.shape
    dim = width // heads
    scale = dim ** (-0.5)
    count = lax.axis_size("seq")
    team = FRAME // tokens
    own_heads = heads // team
    own_width = own_heads * dim
    own_pairs = own_heads // 2
    groups = [[g * team + i for i in range(team)] for g in range(count // team)]
    seq_rank = lax.axis_index("seq")
    place = seq_rank % team
    frame_first = (seq_rank // team) * FRAME
    row_first = seq_rank * tokens
    contract_rows = (((0,), (0,)), ((), ()))

    resid_in = inputs[0].astype(jnp.float32)
    grad_out = cotangent[0].astype(jnp.float32)
    row_valid = lax.dynamic_slice_in_dim(valid_mask[0], row_first, tokens).astype(jnp.float32)[:, None]
    ahead = lambda values: jnp.pad(values, (HEADER, 0))
    codes = make_codes(
        lax.dynamic_slice_in_dim(ahead(segment_ids[0]), frame_first, FRAME + HEADER),
        lax.dynamic_slice_in_dim(ahead(valid_mask[0]), frame_first, FRAME + HEADER),
    )
    own_kernel = lax.dynamic_slice_in_dim(conv_kernel, place * own_heads, own_heads)
    own_mix = lax.dynamic_slice_in_dim(head_mix, place * own_pairs, own_pairs).reshape(own_pairs, 4)
    own_gain = pad_heads(lax.dynamic_slice_in_dim(group_gain, place * own_width, own_width)[None], dim)
    toep, toep_split = split_toeplitz(toeplitz(own_kernel, scale))

    reps = lax.axis_size("rep")
    direct = team == 4 and (width // count) % (16 * reps) == 0
    first_scale = rms_scale(resid_in)
    normed_in = (resid_in * first_scale * first_gain).astype(jnp.bfloat16)
    if direct:
        own_input, normed_frame = gather_weight(input_weight, normed_in, reps, count)
    else:
        full_input = lax.all_gather(input_weight, "seq", axis=0, tiled=True)
        own_input = lax.dynamic_slice_in_dim(full_input.reshape(width, 3, width), place * own_width, own_width, axis=2)
        own_input = own_input.reshape(width, 3 * own_width)
        normed_frame = lax.all_gather(normed_in, "seq", axis=0, tiled=True, axis_index_groups=groups)
        ends = lax.all_gather(normed_in[tokens - HEADER :], "seq", axis=0)
        last = jnp.maximum(seq_rank // team * team - 1, 0)
        end = jnp.where(frame_first > 0, lax.dynamic_index_in_dim(ends, last, keepdims=False), 0)
        lead = jnp.zeros((EDGE - HEADER, width), jnp.bfloat16)
        normed_frame = jnp.concatenate([lead, end, normed_frame, jnp.zeros((EDGE, width), jnp.bfloat16)], axis=0)
    dmlp = (row_valid * grad_out).astype(jnp.bfloat16)
    own_input, output_weight, dmlp = lax.optimization_barrier((own_input, output_weight, dmlp))
    full_output = lax.all_gather(output_weight, "seq", axis=0, tiled=True)
    own_input = pad_heads(own_input, dim)
    proj = jnp.dot(normed_frame, own_input, preferred_element_type=jnp.float32).astype(jnp.bfloat16)
    dmlp_all = lax.all_gather(dmlp, "seq", axis=0, tiled=True)
    normed_own, att, prob = attention_forward(proj, toep_split, codes, own_gain, own_mix, dim, taps)
    normed_own, full_output = lax.optimization_barrier((normed_own, full_output))
    normed_own = cut_heads(normed_own, dim)

    def to_rows(values):
        moved = lax.all_to_all(
            values.reshape(team, tokens, own_width), "seq", 0, 0, tiled=True, axis_index_groups=groups
        )
        return moved.transpose(1, 0, 2).reshape(tokens, width)

    normed = frame_swap(normed_own) if direct else to_rows(normed_own)
    branch = jnp.dot(normed, full_output, preferred_element_type=jnp.float32)
    resid = resid_in + row_valid * branch
    second_scale = rms_scale(resid)
    normed_mid = (resid * second_scale * second_gain).astype(jnp.bfloat16)
    normed_mid, dmlp_all = lax.optimization_barrier((normed_mid, dmlp_all))
    inputs_all = lax.all_gather(normed_mid, "seq", axis=0, tiled=True)
    gate = jnp.dot(inputs_all, gate_weight, preferred_element_type=jnp.float32)
    up_proj = jnp.dot(inputs_all, up_weight, preferred_element_type=jnp.float32)
    dhidden = jnp.dot(dmlp_all, down_weight.T, preferred_element_type=jnp.float32)
    sigmoid_gate = jax.nn.sigmoid(gate)
    gate_grad = (dhidden * up_proj * sigmoid_gate * (1.0 + gate * (1.0 - sigmoid_gate))).astype(jnp.bfloat16)
    up_grad = (dhidden * gate * sigmoid_gate).astype(jnp.bfloat16)
    hidden = (jax.nn.silu(gate) * up_proj).astype(jnp.bfloat16)
    dmid_part = (
        jnp.dot(gate_grad, gate_weight.T, preferred_element_type=jnp.float32)
        + jnp.dot(up_grad, up_weight.T, preferred_element_type=jnp.float32)
    ).astype(jnp.bfloat16)
    gate_grad, up_grad, hidden, dmid_part = lax.optimization_barrier((gate_grad, up_grad, hidden, dmid_part))
    dmid_low = lax.psum_scatter(dmid_part, "seq", scatter_dimension=0, tiled=True)
    mlp_part = jnp.dot(hidden, down_weight, preferred_element_type=jnp.float32).astype(jnp.bfloat16)
    mlp_grads = [
        lax.dot_general(left, right, contract_rows, preferred_element_type=jnp.float32).astype(jnp.bfloat16)
        for left, right in ((inputs_all, gate_grad), (inputs_all, up_grad), (hidden, dmlp_all))
    ]
    dmid_low, mlp_part, mlp_grads = lax.optimization_barrier((dmid_low, mlp_part, mlp_grads))
    mlp_low = lax.psum_scatter(mlp_part, "seq", scatter_dimension=0, tiled=True)
    mlp_grads = [lax.psum(value, "rep") for value in mlp_grads]
    dmid = dmid_low.astype(jnp.float32)
    second_part = jnp.sum(dmid * resid * second_scale, axis=0)
    dresid = grad_out + norm_back(dmid, resid, second_scale, second_gain)
    dbranch = (row_valid * dresid).astype(jnp.bfloat16)
    if direct:
        dbranch_frame = frame_gather(dbranch)
    else:
        dbranch_frame = lax.all_gather(dbranch, "seq", axis=0, tiled=True, axis_index_groups=groups)
    own_output = lax.dynamic_slice_in_dim(full_output, place * own_width, own_width, axis=0)
    dnormed_own = lax.dot_general(dbranch_frame, own_output, NT, preferred_element_type=jnp.float32)
    own_output_grad = lax.dot_general(normed_own, dbranch_frame, contract_rows, preferred_element_type=jnp.float32)
    dq, dk, dv, dtoep, dmix, dgain = attention_backward(
        proj, toep, codes, prob, att, pad_heads(dnormed_own, dim), own_gain, own_mix, dim, taps
    )
    dproj = jnp.concatenate([dq, dk, dv], axis=1)
    own_input_grad = lax.dot_general(normed_frame, dproj, contract_rows, preferred_element_type=jnp.float32)
    own_input_grad = cut_heads(own_input_grad.astype(jnp.bfloat16), dim)
    own_output_grad = own_output_grad.astype(jnp.bfloat16)
    dnormin_part = lax.dot_general(dproj, own_input, NT, preferred_element_type=jnp.float32).astype(jnp.bfloat16)
    if direct:
        grad_input_w, grad_output_w, dnormin = reduce_weights(own_input_grad, own_output_grad, dnormin_part, reps, count)
    else:
        dnormin = lax.psum_scatter(
            dnormin_part[EDGE : EDGE + FRAME], "seq", scatter_dimension=0, tiled=True, axis_index_groups=groups
        ).astype(jnp.float32)
        starts = lax.all_gather(dnormin_part[EDGE - HEADER : EDGE], "seq", axis=0).astype(jnp.float32)
        later = lax.dynamic_slice_in_dim(
            jnp.pad(starts, ((0, team), (0, 0), (0, 0))), (seq_rank // team + 1) * team, team
        ).sum(axis=0)
        later = jnp.where(place == team - 1, later, 0.0)
        dnormin = dnormin + jnp.pad(later, ((tokens - HEADER, 0), (0, 0)))
        pieces = lax.all_to_all(own_input_grad.reshape(count, width // count, 3 * own_width), "seq", 0, 0, tiled=True)
        pieces = pieces.reshape(count // team, team, width // count, 3, own_width).astype(jnp.float32).sum(axis=0)
        grad_input_w = pieces.transpose(1, 2, 0, 3).reshape(width // count, 3 * width)
        spots = jnp.zeros((width, width), jnp.bfloat16)
        spots = lax.dynamic_update_slice_in_dim(spots, own_output_grad, place * own_width, 0)
        grad_output_w = lax.psum_scatter(spots, "seq", scatter_dimension=0, tiled=True)
        grad_input_w, grad_output_w = [
            lax.psum(value.astype(jnp.bfloat16), "rep") for value in (grad_input_w, grad_output_w)
        ]
    dnormin, mlp_low, mlp_grads = lax.optimization_barrier((dnormin, mlp_low, mlp_grads))
    result = resid + row_valid * mlp_low.astype(jnp.float32)
    first_part = jnp.sum(dnormin * resid_in * first_scale, axis=0)
    grad_in = dresid + norm_back(dnormin, resid_in, first_scale, first_gain)

    def spread(values, size):
        empty = jnp.zeros((size,) + values.shape[1:], jnp.float32)
        return lax.dynamic_update_slice_in_dim(empty, values, place * values.shape[0], 0)

    kernel_part = spread(toeplitz_grad(dtoep, taps, span, scale), heads)
    mix_part = spread(jnp.sum(dmix[:, :4], axis=-1).reshape(own_pairs, 2, 2), heads // 2)
    group_part = spread(cut_heads(dgain, dim)[0], width)
    parts = (kernel_part, mix_part, first_part, second_part, group_part)
    if direct:
        flat = small_sum(jnp.concatenate([value.reshape(-1) for value in parts]), reps, count)
        summed, start = [], 0
        for value in parts:
            summed.append(flat[start : start + value.size].reshape(value.shape))
            start += value.size
    else:
        summed = lax.psum(parts, ("rep", "seq"))
    grad_kernel, grad_mix, grad_first, grad_second, grad_group = summed
    grads = [value.astype(jnp.float32) for value in (grad_input_w, grad_output_w, *mlp_grads)]
    return (
        result.astype(jnp.bfloat16)[None], grad_in.astype(jnp.bfloat16)[None], grads[0], grads[1], grad_kernel,
        grad_mix, grad_first, grad_second, grad_group, grads[2], grads[3], grads[4],
    )


def solution(mesh):
    in_specs = (
        P("rep", "seq", None), P("rep", None), P("rep", None), P("seq", None), P("seq", None), P(), P(), P(), P(), P(),
        P(None, "seq"), P(None, "seq"), P("seq", None), P("rep", "seq", None),
    )
    out_specs = (
        P("rep", "seq", None), P("rep", "seq", None), P("seq", None), P("seq", None), P(), P(), P(), P(), P(),
        P(None, "seq"), P(None, "seq"), P("seq", None),
    )
    return jax.shard_map(on_device, mesh=mesh, in_specs=in_specs, out_specs=out_specs, check_vma=False)
```

```python
import functools
import jax
import jax.numpy as jnp
from jax import lax
from jax.experimental import pallas as pl
from jax.experimental.pallas import tpu as pltpu
from jax.sharding import PartitionSpec as P

FRAME = 1024


EPS = 1e-06
LANES = 128
ROWS = 256
EDGE = 64
HEADER = 16
NEG = -1e30
PROB = jnp.float32

NT = (((1,), (1,)), ((), ()))
NN = (((1,), (0,)), ((), ()))


def dot(a, b, dims=NN):
    return lax.dot_general(a, b, dims, preferred_element_type=jnp.float32)


def toeplitz(kernel, scale):
    heads, taps, span = kernel.shape
    shape = (heads, 2 * LANES, taps * LANES)
    lane = lax.broadcasted_iota(jnp.int32, shape, 2)
    tap = lax.broadcasted_iota(jnp.int32, shape, 1)
    diff = lane % LANES + EDGE + span // 2 - tap
    total = jnp.zeros(shape, jnp.float32)
    for b in range(span):
        weight = jnp.repeat(kernel[:, :, b] * scale, LANES, axis=1)[:, None, :]
        total = total + jnp.where(diff == b, weight, 0.0)
    return total


def split_toeplitz(full):
    kept = lax.reduce_precision(full, exponent_bits=8, mantissa_bits=7)
    high = kept.astype(jnp.bfloat16)
    low = (full - kept).astype(jnp.bfloat16)
    return high, jnp.concatenate([high, high, low], axis=1)


def tap_grads(sums, taps, span, scale):
    shaped = sums.reshape(sums.shape[0], 16, taps, LANES).sum(axis=-1)
    return shaped[:, :span].transpose(0, 2, 1) * scale


def lane_mask(dim):
    return lax.broadcasted_iota(jnp.int32, (ROWS, LANES), 1) < dim


def group_stats(att, dim):
    mean = jnp.sum(att, axis=-1, keepdims=True) / dim
    centred = jnp.where(lane_mask(dim), att - mean, 0.0)
    var = jnp.sum(centred * centred, axis=-1, keepdims=True) / dim
    inv = lax.rsqrt(var + EPS)
    return centred * inv, inv


def forward_kernel(
    dim, taps, q_ref, k_ref, v_ref, t_ref, rowc_ref, colp_ref, colc_ref, gain_ref, mix_ref,
    normed_ref, att_ref, prob_ref, lm_ref, lo_ref, p_ref, cv_ref, mx_ref, sm_ref, acc_ref,
):
    step = pl.program_id(1)
    first = step * ROWS
    top = pl.multiple_of(first + EDGE - HEADER, 16)
    tall = ROWS + HEADER
    codes = rowc_ref[pl.ds(top, tall), :]
    ipos = first - HEADER + lax.broadcasted_iota(jnp.int32, (tall, LANES), 0)
    lane = lax.broadcasted_iota(jnp.int32, (tall, LANES), 1)
    live = codes[HEADER:] >= 0

    def logits(c, carry):
        at = pl.multiple_of(c * LANES, LANES)
        keep = (codes == colp_ref[:, pl.ds(at, LANES)]) & (at - EDGE + lane <= ipos)
        for h in range(2):
            cols = slice(h * LANES, (h + 1) * LANES)
            raw = dot(q_ref[pl.ds(top, tall), cols], k_ref[pl.ds(at, LANES), cols], NT)
            raw = jnp.where(keep, raw, 0.0)
            high = raw.astype(jnp.bfloat16)
            lm_ref[h, :, pl.ds(at, LANES)] = high
            lo_ref[h, :, pl.ds(at, LANES)] = (raw - high.astype(jnp.float32)).astype(jnp.bfloat16)
        return carry

    lax.fori_loop(0, 2 * step + 3, logits, 0)
    mx_ref[...] = jnp.full(mx_ref.shape, NEG, jnp.float32)

    def convolve(c, carry):
        for n in range(2):
            convolve_block(pl.multiple_of((2 * c + n) * LANES, LANES))
        return carry

    def convolve_block(at):
        keep = (codes[HEADER:] == colc_ref[:, pl.ds(at, LANES)]) & (at + lane[HEADER:] <= ipos[HEADER:])
        for h in range(2):
            high = lm_ref[h, :, pl.ds(at, 2 * LANES)]
            p_ref[h] = dot(jnp.concatenate([high, lo_ref[h, :, pl.ds(at, 2 * LANES)], high], axis=1), t_ref[h])
            conv = p_ref[h, HEADER:, :LANES]
            for a in range(1, taps):
                conv = conv + p_ref[h, HEADER - a : tall - a, a * LANES : (a + 1) * LANES]
            conv = jnp.where(keep, conv, NEG)
            cv_ref[h, :, pl.ds(at, LANES)] = conv
            mx_ref[h] = jnp.maximum(mx_ref[h], conv)

    lax.fori_loop(0, step + 1, convolve, 0)
    sm_ref[...] = jnp.zeros(sm_ref.shape, jnp.float32)
    for h in range(2):
        peak = jnp.max(mx_ref[h], axis=-1, keepdims=True)
        mx_ref[h] = jnp.where(live, jnp.broadcast_to(peak, (ROWS, LANES)), 0.0)

    def exponents(c, carry):
        for h in range(2):
            total = sm_ref[h]
            for n in range(2):
                at = pl.multiple_of((2 * c + n) * LANES, LANES)
                value = jnp.exp(cv_ref[h, :, pl.ds(at, LANES)] - mx_ref[h])
                cv_ref[h, :, pl.ds(at, LANES)] = value
                total = total + value
            sm_ref[h] = total
        return carry

    lax.fori_loop(0, step + 1, exponents, 0)
    for h in range(2):
        total = jnp.sum(sm_ref[h], axis=-1, keepdims=True)
        total = jnp.where(live, jnp.broadcast_to(total, (ROWS, LANES)), 1.0)
        sm_ref[h] = 1.0 / total
    acc_ref[...] = jnp.zeros(acc_ref.shape, jnp.float32)
    pair = pl.program_id(0)
    mix = [[mix_ref[pair, 2 * g + h] for h in range(2)] for g in range(2)]

    def mixing(c, carry):
        at = pl.multiple_of(c * 2 * LANES, 2 * LANES)
        mixed = [[], []]
        for n in range(2):
            spot = pl.ds(pl.multiple_of(at + n * LANES, LANES), LANES)
            prob = [cv_ref[h, :, spot] * sm_ref[h] for h in range(2)]
            for g in range(2):
                prob_ref[g, :, spot] = prob[g].astype(prob_ref.dtype)
                mixed[g].append((mix[g][0] * prob[0] + mix[g][1] * prob[1]).astype(jnp.bfloat16))
        for g in range(2):
            cols = slice(g * LANES, (g + 1) * LANES)
            value = v_ref[pl.ds(pl.multiple_of(at + EDGE, 16), 2 * LANES), cols]
            acc_ref[g] += dot(jnp.concatenate(mixed[g], axis=1), value)
        return carry

    lax.fori_loop(0, step + 1, mixing, 0)
    for g in range(2):
        att = acc_ref[g]
        att_ref[:, g * LANES : (g + 1) * LANES] = att
        unit, _ = group_stats(att, dim)
        normed = unit * gain_ref[0:1, g * LANES : (g + 1) * LANES]
        normed_ref[:, g * LANES : (g + 1) * LANES] = normed.astype(jnp.bfloat16)


def backward_kernel(
    dim, taps, span, q_ref, k_ref, v_ref, t_ref, rowc_ref, colp_ref, colt_ref, rowt_ref, prob_ref, att_ref, dn_ref,
    gain_ref, mix_ref, dq_ref, dk_ref, dv_ref, taps_ref, dmix_ref, dgain_ref,
    dp_ref, dc_ref, dl_ref, lt_ref, dkt_ref, dvt_ref, datt_ref, dattt_ref, qt_ref, rs_ref, dqa_ref, dm_ref, ahead_ref, g_ref,
):
    pair = pl.program_id(0)
    turn = pl.program_id(1)
    step = pl.num_programs(1) - 1 - turn
    first = pl.multiple_of(step * ROWS, ROWS)
    own = pl.multiple_of(first + EDGE, 16)
    codes = rowc_ref[pl.ds(own, ROWS), :]
    ipos = first + lax.broadcasted_iota(jnp.int32, (ROWS, LANES), 0)
    lane = lax.broadcasted_iota(jnp.int32, (ROWS, LANES), 1)
    blocks = 2 * step + 2
    mix = [[mix_ref[pair, 2 * g + h] for h in range(2)] for g in range(2)]

    @pl.when(turn == 0)
    def _():
        dc_ref[...] = jnp.zeros(dc_ref.shape, jnp.float32)
        dkt_ref[...] = jnp.zeros(dkt_ref.shape, jnp.float32)
        dvt_ref[...] = jnp.zeros(dvt_ref.shape, jnp.float32)
        g_ref[...] = jnp.zeros(g_ref.shape, jnp.float32)
        dmix_ref[...] = jnp.zeros(dmix_ref.shape, jnp.float32)
        dgain_ref[...] = jnp.zeros(dgain_ref.shape, jnp.float32)
        for ref in (dq_ref, dv_ref):
            ref[:EDGE, :] = jnp.zeros((EDGE, 2 * LANES), jnp.bfloat16)
            ref[ref.shape[0] - EDGE :, :] = jnp.zeros((EDGE, 2 * LANES), jnp.bfloat16)

    @pl.when(turn > 0)
    def _():
        for h in range(2):
            dc_ref[h, ROWS:, :] = dc_ref[h, :8, :]

    for g in range(2):
        cols = slice(g * LANES, (g + 1) * LANES)
        unit, inv = group_stats(att_ref[:, cols], dim)
        grad = dn_ref[:, cols]
        dgain_ref[0:1, cols] += jnp.sum(grad * unit, axis=0, keepdims=True)
        scaled = grad * gain_ref[0:1, cols]
        mean = jnp.sum(scaled, axis=-1, keepdims=True) / dim
        inner = jnp.sum(scaled * unit, axis=-1, keepdims=True) / dim
        datt = inv * (scaled - mean - unit * inner)
        datt = jnp.where(lane_mask(dim), datt, 0.0)
        high = datt.astype(jnp.bfloat16)
        datt_ref[g, :, :LANES] = high
        datt_ref[g, :, LANES:] = (datt - high.astype(jnp.float32)).astype(jnp.bfloat16)
        dattt_ref[g] = datt.T.astype(jnp.bfloat16)
        qt_ref[g] = q_ref[pl.ds(own, ROWS), cols].astype(jnp.float32).T.astype(jnp.bfloat16)
    rs_ref[...] = jnp.zeros(rs_ref.shape, jnp.float32)
    dm_ref[...] = jnp.zeros(dm_ref.shape, jnp.float32)

    def probs(c, carry):
        for n in range(2):
            probs_block(pl.multiple_of((2 * c + n) * LANES, LANES))
        return carry

    def probs_block(at):
        prob = [prob_ref[h, :, pl.ds(at, LANES)].astype(jnp.float32) for h in range(2)]
        dmixed = []
        for g in range(2):
            cols = slice(g * LANES, (g + 1) * LANES)
            value = v_ref[pl.ds(at + EDGE, LANES), cols]
            dmixed.append(dot(datt_ref[g], jnp.concatenate([value, value], axis=1), NT))
            mixed = (mix[g][0] * prob[0] + mix[g][1] * prob[1]).astype(jnp.bfloat16)
            dvt_ref[g, :, pl.ds(at, LANES)] += dot(dattt_ref[g], mixed)
            for h in range(2):
                dm_ref[2 * g + h] += dmixed[g] * prob[h]
        for h in range(2):
            dprob = mix[0][h] * dmixed[0] + mix[1][h] * dmixed[1]
            dp_ref[h, :, pl.ds(at, LANES)] = dprob
            rs_ref[h] += prob[h] * dprob

    lax.fori_loop(0, step + 1, probs, 0)
    for h in range(2):
        rs_ref[h] = jnp.broadcast_to(jnp.sum(rs_ref[h], axis=-1, keepdims=True), (ROWS, LANES))
    for n in range(4):
        dmix_ref[0, n : n + 1, :] += jnp.sum(dm_ref[n], axis=0, keepdims=True)

    tlane = lax.broadcasted_iota(jnp.int32, (LANES, ROWS), 1)
    trow = lax.broadcasted_iota(jnp.int32, (LANES, ROWS), 0)

    def transposed_logits(c, carry):
        at = pl.multiple_of(c * LANES, LANES)
        wide = jnp.concatenate([colt_ref[pl.ds(at, LANES), :]] * 2, axis=1)
        keep = (wide == rowt_ref[:, pl.ds(first, ROWS)]) & (at - EDGE + trow <= first + tlane)
        for h in range(2):
            cols = slice(h * LANES, (h + 1) * LANES)
            raw = dot(k_ref[pl.ds(at, LANES), cols], q_ref[pl.ds(own, ROWS), cols], NT)
            lt_ref[h, pl.ds(at, LANES), :] = jnp.where(keep, raw, 0.0).astype(jnp.bfloat16)
            dl_ref[h, :, pl.ds(at, LANES)] = jnp.zeros((ROWS, LANES), jnp.float32)
        return carry

    lax.fori_loop(0, blocks + 1, transposed_logits, 0)

    def convolve(c, carry):
        for n in range(2):
            convolve_block(pl.multiple_of((2 * c + n) * LANES, LANES))
        return carry

    def convolve_block(at):
        for h in range(2):
            prob = prob_ref[h, :, pl.ds(at, LANES)].astype(jnp.float32)
            dc_ref[h, :ROWS, pl.ds(at, LANES)] = prob * (dp_ref[h, :, pl.ds(at, LANES)] - rs_ref[h])
            shifted = jnp.concatenate(
                [dc_ref[h, a : a + ROWS, pl.ds(at, LANES)].astype(jnp.bfloat16) for a in range(taps)], axis=1
            )
            g_ref[h] += dot(lt_ref[h, pl.ds(at, 2 * LANES), :], shifted)
            dl_ref[h, :, pl.ds(at, 2 * LANES)] += dot(shifted, t_ref[h], NT)

    lax.fori_loop(0, step + 1, convolve, 0)
    dqa_ref[...] = jnp.zeros(dqa_ref.shape, jnp.float32)

    def logits(c, carry):
        at = pl.multiple_of(c * LANES, LANES)
        keep = (codes == colp_ref[:, pl.ds(at, LANES)]) & (at - EDGE + lane <= ipos)
        for h in range(2):
            cols = slice(h * LANES, (h + 1) * LANES)
            dl = jnp.where(keep, dl_ref[h, :, pl.ds(at, LANES)], 0.0).astype(jnp.bfloat16)
            dqa_ref[h] += dot(dl, k_ref[pl.ds(at, LANES), cols])
            dkt_ref[h, :, pl.ds(at, LANES)] += dot(qt_ref[h], dl)
        return carry

    lax.fori_loop(0, blocks + 1, logits, 0)
    for h in range(2):
        dq_ref[pl.ds(own, ROWS), h * LANES : (h + 1) * LANES] = dqa_ref[h].astype(jnp.bfloat16)

    @pl.when(step == 0)
    def _():
        head = slice(EDGE - HEADER, EDGE)
        wide = (HEADER, 2 * LANES)
        keep = jnp.concatenate([rowc_ref[head, :]] * 2, axis=1) == colp_ref[:, : 2 * LANES]
        keep = keep & (
            lax.broadcasted_iota(jnp.int32, wide, 1) - EDGE <= lax.broadcasted_iota(jnp.int32, wide, 0) - HEADER
        )
        for h in range(2):
            cols = slice(h * LANES, (h + 1) * LANES)
            ahead_ref[:HEADER, :] = jnp.zeros((HEADER, LANES), jnp.float32)
            ahead_ref[HEADER:, :] = dc_ref[h, :HEADER, :LANES]
            shifted = jnp.concatenate(
                [ahead_ref[a : a + HEADER, :].astype(jnp.bfloat16) for a in range(taps)], axis=1
            )
            near = k_ref[: 2 * LANES, cols]
            query = q_ref[head, cols]
            raw = jnp.where(keep, dot(query, near, NT), 0.0)
            g_ref[h] += dot(raw.T.astype(jnp.bfloat16), shifted)
            dl = jnp.where(keep, dot(shifted, t_ref[h], NT), 0.0).astype(jnp.bfloat16)
            dq_ref[head, cols] = dot(dl, near).astype(jnp.bfloat16)
            dkt_ref[h, :, : 2 * LANES] += dot(query.astype(jnp.float32).T.astype(jnp.bfloat16), dl)
            dk_ref[:, cols] = dkt_ref[h].T.astype(jnp.bfloat16)
            dv_ref[pl.ds(EDGE, dvt_ref.shape[2]), cols] = dvt_ref[h].T.astype(jnp.bfloat16)
        shape = (2 * LANES, taps * LANES)
        lanes = lax.broadcasted_iota(jnp.int32, shape, 1) & (LANES - 1)
        diff = lanes + (EDGE + span // 2) - lax.broadcasted_iota(jnp.int32, shape, 0)

        def diagonals(b, carry):
            for h in range(2):
                part = jnp.where(diff == b, g_ref[h], 0.0)
                taps_ref[h, pl.ds(b, 1), :] = jnp.sum(part, axis=0, keepdims=True)
            return carry

        lax.fori_loop(0, span, diagonals, 0)


def attention_forward(proj, toep, codes, gain, mix, dim, taps):
    tall = proj.shape[0]
    frame = tall - 2 * EDGE
    pairs = mix.shape[0]
    steps = frame // ROWS
    whole = lambda off: pl.BlockSpec((tall, 2 * LANES), lambda p, r: (0, off * pairs + p))
    wide = pairs * 2 * LANES
    return pl.pallas_call(
        functools.partial(forward_kernel, dim, taps),
        grid=(pairs, steps),
        in_specs=[
            whole(0), whole(1), whole(2),
            pl.BlockSpec((2, 6 * LANES, taps * LANES), lambda p, r: (p, 0, 0)),
            pl.BlockSpec((tall, LANES), lambda p, r: (0, 0)),
            pl.BlockSpec((1, tall), lambda p, r: (0, 0)),
            pl.BlockSpec((1, frame), lambda p, r: (0, 0)),
            pl.BlockSpec((1, 2 * LANES), lambda p, r: (0, p)),
            pl.BlockSpec(memory_space=pltpu.SMEM),
        ],
        out_specs=[
            pl.BlockSpec((ROWS, 2 * LANES), lambda p, r: (r, p)),
            pl.BlockSpec((ROWS, 2 * LANES), lambda p, r: (r, p)),
            pl.BlockSpec((2, ROWS, frame), lambda p, r: (p, r, 0)),
        ],
        out_shape=[
            jax.ShapeDtypeStruct((frame, wide), jnp.bfloat16),
            jax.ShapeDtypeStruct((frame, wide), jnp.float32),
            jax.ShapeDtypeStruct((2 * pairs, frame, frame), PROB),
        ],
        scratch_shapes=[
            pltpu.VMEM((2, ROWS + HEADER, tall), jnp.bfloat16),
            pltpu.VMEM((2, ROWS + HEADER, tall), jnp.bfloat16),
            pltpu.VMEM((2, ROWS + HEADER, taps * LANES), jnp.float32),
            pltpu.VMEM((2, ROWS, frame), jnp.float32),
            pltpu.VMEM((2, ROWS, LANES), jnp.float32),
            pltpu.VMEM((2, ROWS, LANES), jnp.float32),
            pltpu.VMEM((2, ROWS, LANES), jnp.float32),
        ],
        cost_estimate=pl.CostEstimate(flops=10_000_000_000, bytes_accessed=40_000_000, transcendentals=0),
        compiler_params=pltpu.CompilerParams(vmem_limit_bytes=48 << 20),
        name="attend",
    )(proj, proj, proj, toep, codes["row"], codes["colp"], codes["col"], gain, mix)


def attention_backward(proj, toep, codes, prob, att, dnormed, gain, mix, dim, taps, span):
    tall = proj.shape[0]
    frame = tall - 2 * EDGE
    pairs = mix.shape[0]
    steps = frame // ROWS
    whole = lambda off: pl.BlockSpec((tall, 2 * LANES), lambda p, r: (0, off * pairs + p))
    wide = pairs * 2 * LANES
    back = lambda r: steps - 1 - r
    return pl.pallas_call(
        functools.partial(backward_kernel, dim, taps, span),
        grid=(pairs, steps),
        in_specs=[
            whole(0), whole(1), whole(2),
            pl.BlockSpec((2, 2 * LANES, taps * LANES), lambda p, r: (p, 0, 0)),
            pl.BlockSpec((tall, LANES), lambda p, r: (0, 0)),
            pl.BlockSpec((1, tall), lambda p, r: (0, 0)),
            pl.BlockSpec((tall, LANES), lambda p, r: (0, 0)),
            pl.BlockSpec((1, frame), lambda p, r: (0, 0)),
            pl.BlockSpec((2, ROWS, frame), lambda p, r: (p, back(r), 0)),
            pl.BlockSpec((ROWS, 2 * LANES), lambda p, r: (back(r), p)),
            pl.BlockSpec((ROWS, 2 * LANES), lambda p, r: (back(r), p)),
            pl.BlockSpec((1, 2 * LANES), lambda p, r: (0, p)),
            pl.BlockSpec(memory_space=pltpu.SMEM),
        ],
        out_specs=[
            pl.BlockSpec((tall, 2 * LANES), lambda p, r: (0, p)),
            pl.BlockSpec((tall, 2 * LANES), lambda p, r: (0, p)),
            pl.BlockSpec((tall, 2 * LANES), lambda p, r: (0, p)),
            pl.BlockSpec((2, 16, taps * LANES), lambda p, r: (p, 0, 0)),
            pl.BlockSpec((1, 8, LANES), lambda p, r: (p, 0, 0)),
            pl.BlockSpec((1, 2 * LANES), lambda p, r: (0, p)),
        ],
        out_shape=[
            jax.ShapeDtypeStruct((tall, wide), jnp.bfloat16),
            jax.ShapeDtypeStruct((tall, wide), jnp.bfloat16),
            jax.ShapeDtypeStruct((tall, wide), jnp.bfloat16),
            jax.ShapeDtypeStruct((2 * pairs, 16, taps * LANES), jnp.float32),
            jax.ShapeDtypeStruct((pairs, 8, LANES), jnp.float32),
            jax.ShapeDtypeStruct((1, wide), jnp.float32),
        ],
        scratch_shapes=[
            pltpu.VMEM((2, ROWS, frame), jnp.float32),
            pltpu.VMEM((2, ROWS + 8, frame), jnp.float32),
            pltpu.VMEM((2, ROWS, tall), jnp.float32),
            pltpu.VMEM((2, tall, ROWS), jnp.bfloat16),
            pltpu.VMEM((2, LANES, tall), jnp.float32),
            pltpu.VMEM((2, LANES, frame), jnp.float32),
            pltpu.VMEM((2, ROWS, 2 * LANES), jnp.bfloat16),
            pltpu.VMEM((2, LANES, ROWS), jnp.bfloat16),
            pltpu.VMEM((2, LANES, ROWS), jnp.bfloat16),
            pltpu.VMEM((2, ROWS, LANES), jnp.float32),
            pltpu.VMEM((2, ROWS, LANES), jnp.float32),
            pltpu.VMEM((4, ROWS, LANES), jnp.float32),
            pltpu.VMEM((2 * HEADER, LANES), jnp.float32),
            pltpu.VMEM((2, 2 * LANES, taps * LANES), jnp.float32),
        ],
        cost_estimate=pl.CostEstimate(flops=10_000_000_000, bytes_accessed=40_000_000, transcendentals=0),
        compiler_params=pltpu.CompilerParams(vmem_limit_bytes=48 << 20),
        name="attend_back",
    )(proj, proj, proj, toep, codes["row"], codes["colp"], codes["colt"], codes["rowt"], prob, att, dnormed, gain, mix)


def make_codes(segment, valid):
    row = jnp.where(valid > 0, segment, -1)
    col = jnp.where(valid > 0, segment, -2)
    rowp = jnp.pad(row, (EDGE - HEADER, EDGE), constant_values=-1)
    colp = jnp.pad(col, (EDGE - HEADER, EDGE), constant_values=-2)
    tall = rowp.shape[0]
    return {
        "row": jnp.broadcast_to(rowp[:, None], (tall, LANES)),
        "colt": jnp.broadcast_to(colp[:, None], (tall, LANES)),
        "colp": colp[None],
        "col": col[None, HEADER:],
        "rowt": row[None, HEADER:],
    }


MESH = pl.DeviceIdType.MESH
TOKENS_AFTER = 2


def meet(peers):
    barrier = pltpu.get_barrier_semaphore()
    for peer in peers:
        pl.semaphore_signal(barrier, inc=1, device_id=peer, device_id_type=MESH)
    pl.semaphore_wait(barrier, len(peers))


def send(src, dst, send_sem, recv_sem, peer):
    return pltpu.make_async_remote_copy(
        src_ref=src, dst_ref=dst, send_sem=send_sem, recv_sem=recv_sem, device_id=peer, device_id_type=MESH
    )


def gather_kernel(
    reps, count, w_ref, x_ref, z_ref, wc_ref, f_ref, own_sem, side_send, side_recv, far_send, far_recv, rep_send, rep_recv,
    tok_send, tok_recv, head_send, head_recv,
):
    rep = lax.axis_index("rep")
    me = lax.axis_index("seq")
    chips = count // 2
    chip, core = me // 2, me % 2
    rows = w_ref.shape[0]
    part = rows // reps
    full = w_ref.shape[1] // 3
    cols = wc_ref.shape[1] // 3
    tokens = x_ref.shape[0]
    place = me % 4
    sibling = chip * 2 + 1 - core
    far_ids = [((chip + k) % chips) * 2 + e for k in range(1, chips) for e in range(2)]
    rep_ids = [(rep + k) % reps for k in range(1, reps)]
    at = lambda r, s: (r, s)
    meet([at(rep, s) for s in far_ids + [sibling]] + [at(r, me) for r in rep_ids])

    def source(first, size, who, t):
        left = pl.multiple_of(t * full + (who % 4) * cols, LANES)
        return w_ref.at[pl.ds(first, size), pl.ds(left, cols)]

    def target(first, size, t):
        return wc_ref.at[pl.ds(first, size), pl.ds(t * cols, cols)]

    def spot(who, r):
        return pl.multiple_of(who * rows + r * part, 16)

    def token_rows(who, half):
        return f_ref.at[pl.ds(pl.multiple_of(EDGE + (who % 4) * tokens + half * (tokens // 2), 16), tokens // 2), :]

    waits = []
    quarter = pl.multiple_of(rep * part, 16)
    for n, who in enumerate(far_ids):
        for t in range(3):
            copy = send(
                source(quarter, part, who, t), target(spot(me, rep), part, t), far_send.at[n, t], far_recv.at[me, t],
                at(rep, who),
            )
            copy.start()
            waits.append(copy)
    for t in range(3):
        copy = send(
            source(0, rows, sibling, t), target(spot(me, 0), rows, t), side_send.at[t], side_recv.at[t], at(rep, sibling)
        )
        copy.start()
        waits.append(copy)
    local = [
        pltpu.make_async_copy(source(0, rows, me, t), target(spot(me, 0), rows, t), own_sem.at[t]) for t in range(3)
    ]
    lead = EDGE - HEADER
    local.append(pltpu.make_async_copy(z_ref.at[pl.ds(0, lead), :], f_ref.at[pl.ds(0, lead), :], own_sem.at[4]))
    local.append(
        pltpu.make_async_copy(z_ref, f_ref.at[pl.ds(f_ref.shape[0] - EDGE, EDGE), :], own_sem.at[5])
    )
    local.append(pltpu.make_async_copy(
        x_ref, f_ref.at[pl.ds(pl.multiple_of(EDGE + place * tokens, 16), tokens), :], own_sem.at[3]
    ))
    for copy in local:
        copy.start()
    def send_tokens():
        partner = (chip ^ 1) * 2 + core
        for half in range(2):
            mine = x_ref.at[pl.ds(half * (tokens // 2), tokens // 2), :]
            copy = send(mine, token_rows(me, half), tok_send.at[0, half], tok_recv.at[0, half], at(rep, partner))
            copy.start()
            waits.append(copy)
            copy = send(mine, token_rows(me, half), tok_send.at[1, half], tok_recv.at[1, half], at(rep, sibling))
            copy.start()
            waits.append(copy)

    head = f_ref.at[pl.ds(lead, HEADER), :]
    fill = pltpu.make_async_copy(z_ref.at[pl.ds(0, HEADER), :], head, own_sem.at[6])
    sends_on = (place == 3) & (me < count - 4)
    after = [
        send(x_ref.at[pl.ds(tokens - HEADER, HEADER), :], head, head_send.at[v], head_recv.at[0],
             at(rep, lax.rem(me + 1 + v, count)))
        for v in range(4)
    ]
    partner = (chip ^ 1) * 2 + core
    for n, who in enumerate(far_ids):
        if n == min(TOKENS_AFTER, len(far_ids) - 1):
            send_tokens()

            @pl.when(sends_on)
            def _():
                for copy in after:
                    copy.start()

            @pl.when(me < 4)
            def _():
                fill.start()

        for t in range(3):
            got = target(spot(who, rep), part, t)
            send(got, got, far_send.at[n, t], far_recv.at[who, t], at(rep, who)).wait_recv()
        block = wc_ref.at[pl.ds(spot(who, rep), part), :]
        for m, r in enumerate(rep_ids):
            copy = send(block, block, rep_send.at[n, m], rep_recv.at[n, m], at(r, me))
            copy.start()
            waits.append(copy)
    for half in range(2):
        got = token_rows(partner, half)
        send(got, got, tok_send.at[0, half], tok_recv.at[0, half], at(rep, partner)).wait_recv()
        copy = send(got, got, tok_send.at[2, half], tok_recv.at[2, half], at(rep, sibling))
        copy.start()
        waits.append(copy)
    for copy in local:
        copy.wait()

    @pl.when(me < 4)
    def _():
        fill.wait()

    @pl.when(me >= 4)
    def _():
        after[0].wait_recv()

    @pl.when(sends_on)
    def _():
        for copy in after:
            copy.wait_send()

    for t in range(3):
        got = target(spot(sibling, 0), rows, t)
        send(got, got, side_send.at[t], side_recv.at[t], at(rep, sibling)).wait_recv()
    for half in range(2):
        for kind, who in ((1, sibling), (2, partner ^ 1)):
            got = token_rows(who, half)
            send(got, got, tok_send.at[kind, half], tok_recv.at[kind, half], at(rep, sibling)).wait_recv()
    for n, who in enumerate(far_ids):
        for m in range(reps - 1):
            block = wc_ref.at[pl.ds(spot(who, (rep + reps - 1 - m) % reps), part), :]
            send(block, block, rep_send.at[n, m], rep_recv.at[n, m], at(rep_ids[m], me)).wait_recv()
    for copy in waits:
        copy.wait_send()


def gather_weight(weight, tokens, reps, count):
    rows, full = weight.shape
    own = full // 4
    far = count - 2
    dma = pltpu.SemaphoreType.DMA
    return pl.pallas_call(
        functools.partial(gather_kernel, reps, count),
        in_specs=[pl.BlockSpec(memory_space=pl.ANY)] * 3,
        out_specs=[pl.BlockSpec(memory_space=pl.ANY)] * 2,
        out_shape=[
            jax.ShapeDtypeStruct((rows * count, own), weight.dtype),
            jax.ShapeDtypeStruct((tokens.shape[0] * 4 + 2 * EDGE, tokens.shape[1]), tokens.dtype),
        ],
        scratch_shapes=[
            dma((7,)), dma((3,)), dma((3,)), dma((far, 3)), dma((count, 3)), dma((far, reps - 1)), dma((far, reps - 1)),
            dma((3, 2)), dma((3, 2)), dma((4,)), dma((1,)),
        ],
        cost_estimate=pl.CostEstimate(flops=2_000_000_000, bytes_accessed=20_000_000, transcendentals=0),
        compiler_params=pltpu.CompilerParams(collective_id=1, has_side_effects=True),
        name="gather_weight",
    )(weight, tokens, jnp.zeros((EDGE, tokens.shape[1]), tokens.dtype))


def frame_gather_kernel(x_ref, f_ref, own_sem, send_sem, recv_sem):
    rep = lax.axis_index("rep")
    me = lax.axis_index("seq")
    chip, core = me // 2, me % 2
    half_rows = x_ref.shape[0] // 2
    sibling = (rep, chip * 2 + 1 - core)
    partner = (rep, (chip ^ 1) * 2 + core)
    meet([sibling, partner])

    def rows(who, half):
        return f_ref.at[pl.ds(pl.multiple_of((who % 4) * 2 * half_rows + half * half_rows, 16), half_rows), :]

    waits = []

    def push(src, dst, kind, half, peer):
        copy = send(src, dst, send_sem.at[kind, half], recv_sem.at[kind, half], peer)
        copy.start()
        waits.append(copy)

    for half in range(2):
        push(x_ref.at[pl.ds(half * half_rows, half_rows), :], rows(me, half), 0, half, partner)
    for half in range(2):
        push(x_ref.at[pl.ds(half * half_rows, half_rows), :], rows(me, half), 1, half, sibling)
    local = pltpu.make_async_copy(
        x_ref, f_ref.at[pl.ds(pl.multiple_of((me % 4) * 2 * half_rows, 16), 2 * half_rows), :], own_sem.at[0]
    )
    local.start()

    def arrived(kind, half, who):
        got = rows(who, half)
        send(got, got, send_sem.at[kind, half], recv_sem.at[kind, half], sibling).wait_recv()
        return got

    for half in range(2):
        got = arrived(0, half, partner[1])
        push(got, got, 2, half, sibling)
    local.wait()
    for half in range(2):
        arrived(1, half, sibling[1])
        arrived(2, half, partner[1] ^ 1)
    for copy in waits:
        copy.wait_send()


def frame_gather(values):
    dma = pltpu.SemaphoreType.DMA
    return pl.pallas_call(
        frame_gather_kernel,
        in_specs=[pl.BlockSpec(memory_space=pl.ANY)],
        out_specs=pl.BlockSpec(memory_space=pl.ANY),
        out_shape=jax.ShapeDtypeStruct((values.shape[0] * 4, values.shape[1]), values.dtype),
        scratch_shapes=[dma((1,)), dma((3, 2)), dma((3, 2))],
        cost_estimate=pl.CostEstimate(flops=2_000_000_000, bytes_accessed=8_000_000, transcendentals=0),
        compiler_params=pltpu.CompilerParams(collective_id=2, has_side_effects=True),
        name="frame_gather",
    )(values)


def frame_swap_kernel(h_ref, r_ref, own_sem, send_sem, recv_sem):
    rep = lax.axis_index("rep")
    me = lax.axis_index("seq")
    base, place = me // 4 * 4, me % 4
    rows = r_ref.shape[0]
    cols = h_ref.shape[1]
    peers = [base + (place ^ n) for n in (2, 3, 1)]
    meet([(rep, who) for who in peers])

    def block(who):
        return h_ref.at[pl.ds(pl.multiple_of((who % 4) * rows, 16), rows), :]

    def spot(who):
        return r_ref.at[:, pl.ds(pl.multiple_of((who % 4) * cols, LANES), cols)]

    copies = [
        send(block(who), spot(me), send_sem.at[n], recv_sem.at[n], (rep, who)) for n, who in enumerate(peers)
    ]
    for copy in copies:
        copy.start()
    local = pltpu.make_async_copy(block(me), spot(me), own_sem.at[0])
    local.start()
    local.wait()
    for n, who in enumerate(peers):
        send(block(who), spot(who), send_sem.at[n], recv_sem.at[n], (rep, who)).wait_recv()
    for copy in copies:
        copy.wait_send()


def frame_swap(values):
    dma = pltpu.SemaphoreType.DMA
    return pl.pallas_call(
        frame_swap_kernel,
        in_specs=[pl.BlockSpec(memory_space=pl.ANY)],
        out_specs=pl.BlockSpec(memory_space=pl.ANY),
        out_shape=jax.ShapeDtypeStruct((values.shape[0] // 4, values.shape[1] * 4), values.dtype),
        scratch_shapes=[dma((1,)), dma((3,)), dma((3,))],
        cost_estimate=pl.CostEstimate(flops=2_000_000_000, bytes_accessed=2_000_000, transcendentals=0),
        compiler_params=pltpu.CompilerParams(collective_id=3, has_side_effects=True),
        name="frame_swap",
    )(values)


def reduce_kernel(
    reps, count, gi_ref, go_ref, dn_ref, xs_ref, sv_ref, oi_ref, oo_ref, od_ref, so_ref,
    li_ref, ri_ref, rb_ref, zi_ref, qi_ref, lo_ref, ro_ref, rc_ref, zo_ref, qo_ref, ld_ref, bd_ref, hd_ref,
    load_sem, one_send, one_recv, on_send, on_recv, near_send, near_recv, past_send, past_recv, two_send, two_recv, three_send, three_recv, tok_send, tok_recv,
    head_send, head_recv, vec_ref, one_ref, two_ref, sum_ref, small_one, small_got, small_two, small_end,
):
    rep = lax.axis_index("rep")
    me = lax.axis_index("seq")
    chip, core = me // 2, me % 2
    base, place = me // 4 * 4, me % 4
    sibling = chip * 2 + 1 - core
    partner = (chip ^ 1) * 2 + core
    rep_ids = [(rep + k) % reps for k in range(1, reps)]
    seq_ids = [(me + k) % count for k in range(1, count)]
    part = li_ref.shape[2]
    rows = part * reps
    halves = lo_ref.shape[0]
    frames = count // 4
    cols = gi_ref.shape[1] // 3
    width = cols * 4
    tokens = od_ref.shape[0]
    meet([(r, me) for r in rep_ids] + [(rep, s) for s in seq_ids])
    waits = []

    def push(src, dst, send_sem, recv_sem, peer):
        copy = send(src, dst, send_sem, recv_sem, peer)
        copy.start()
        waits.append(copy)

    def arrived(dst, send_sem, recv_sem):
        send(dst, dst, send_sem, recv_sem, (rep, sibling)).wait_recv()

    def quarter(ref, who, r):
        return ref.at[pl.ds(pl.multiple_of(who * rows + r * part, 16), part), :]

    def token_rows(who):
        return dn_ref.at[pl.ds(pl.multiple_of(EDGE + (who % 4) * tokens, 16), tokens), :]

    ahead = send(
        dn_ref.at[pl.ds(EDGE - HEADER, HEADER), :], hd_ref.at[place], head_send.at[0], head_recv.at[place],
        (rep, lax.rem(base + count - 1, count)),
    )

    @pl.when(me >= 4)
    def _():
        ahead.start()

    push(token_rows(partner ^ 1), bd_ref.at[0], tok_send.at[0], tok_recv.at[0], (rep, sibling))
    push(token_rows(sibling), bd_ref.at[1], tok_send.at[1], tok_recv.at[1], (rep, sibling))
    loads = [
        pltpu.make_async_copy(token_rows(partner), ld_ref.at[0], load_sem.at[0]),
        pltpu.make_async_copy(token_rows(me), ld_ref.at[1], load_sem.at[1]),
    ]
    for copy in loads:
        copy.start()
    order = seq_ids + [me]
    near = [rep ^ 1, rep ^ 2]
    past = [rep ^ 2, rep ^ 1]
    blocks = [(go_ref, h, lo_ref.at[h], ro_ref.at[h], rc_ref.at[h]) for h in range(halves)]
    blocks += [(gi_ref, who, li_ref.at[n], ri_ref.at[n], rb_ref.at[n]) for n, who in enumerate(order)]
    for n, (grad, row, _, got, _) in enumerate(blocks):
        for m, r in enumerate((near[n % 2], rep ^ 3)):
            push(quarter(grad, row, r), got.at[m], one_send.at[n, m], one_recv.at[n, m], (near[n % 2], me))
    own = [
        pltpu.make_async_copy(quarter(grad, row, r), held.at[m], load_sem.at[2 + 2 * n + m])
        for n, (grad, row, held, _, _) in enumerate(blocks)
        for m, r in enumerate((rep, past[n % 2]))
    ]
    for copy in own:
        copy.start()

    loads[0].wait()
    arrived(bd_ref.at[0], tok_send.at[0], tok_recv.at[0])
    wide = jnp.float32
    ld_ref[0] = (ld_ref[0].astype(wide) + bd_ref[0].astype(wide)).astype(jnp.bfloat16)
    push(ld_ref.at[0], bd_ref.at[2], tok_send.at[2], tok_recv.at[2], (rep, partner))

    def pass_on(n):
        _, _, held, got, last = blocks[n]
        own[2 * n + 1].wait()
        arrived(got.at[1], one_send.at[n, 1], one_recv.at[n, 1])
        held[1] = (held[1].astype(wide) + got[1].astype(wide)).astype(jnp.bfloat16)
        push(held.at[1], last, on_send.at[n], on_recv.at[n], (past[n % 2], me))

    def finish(n):
        _, _, held, got, last = blocks[n]
        own[2 * n].wait()
        arrived(got.at[0], one_send.at[n, 0], one_recv.at[n, 0])
        arrived(last, on_send.at[n], on_recv.at[n])
        held[0] = (held[0].astype(wide) + got[0].astype(wide) + last[...].astype(wide)).astype(jnp.bfloat16)
        if n < halves:
            owner = place * halves + n

            @pl.when(owner == me)
            def _():
                zo_ref[me // 4] = lo_ref[n, 0]

            @pl.when(owner != me)
            def _():
                shipped(n).start()
        elif n < halves + count - 1:
            k = n - halves
            push(li_ref.at[k, 0], zi_ref.at[me], two_send.at[k], two_recv.at[me], (rep, order[k]))
        else:
            zi_ref[me] = li_ref[count - 1, 0]

    def shipped(h):
        return send(
            lo_ref.at[h, 0], zo_ref.at[me // 4], two_send.at[count + h], two_recv.at[count + me // 4],
            (rep, place * halves + h),
        )

    for n in range(len(blocks) + 2):
        if n < len(blocks):
            pass_on(n)
        if n >= 2:
            finish(n - 2)

    loads[1].wait()
    arrived(bd_ref.at[1], tok_send.at[1], tok_recv.at[1])
    arrived(bd_ref.at[2], tok_send.at[2], tok_recv.at[2])
    od_ref[...] = ld_ref[1].astype(wide) + bd_ref[1].astype(wide) + bd_ref[2].astype(wide)

    @pl.when((place == 3) & (me < count - 4))
    def _():
        total = od_ref[tokens - HEADER :, :]
        for v in range(4):
            arrived(hd_ref.at[v], head_send.at[0], head_recv.at[v])
            total = total + hd_ref[v].astype(wide)
        od_ref[tokens - HEADER :, :] = total

    @pl.when(me >= 4)
    def _():
        ahead.wait_send()

    gain_rows = width // LANES
    first = jnp.sum(od_ref[...] * xs_ref[...], axis=0, keepdims=True)
    vec_ref[...] = sv_ref[...]
    for k in range(gain_rows):
        vec_ref[k : k + 1, :] = first[:, k * LANES : (k + 1) * LANES]
    for m, r in enumerate(rep_ids):
        push(vec_ref, one_ref.at[rep], small_one.at[m], small_got.at[rep], (r, me))
    one_ref[rep] = vec_ref[...]

    for f in range(frames):
        source = f * 4 + me // halves

        @pl.when(source != me)
        def _():
            arrived(zo_ref.at[f], two_send.at[count], two_recv.at[count + f])

    total = zo_ref[0].astype(wide)
    for f in range(1, frames):
        total = total + zo_ref[f].astype(wide)
    qo_ref[...] = total.astype(jnp.bfloat16)
    for m, r in enumerate(rep_ids):
        push(qo_ref, oo_ref.at[pl.ds(pl.multiple_of(rep * part, 16), part), :], three_send.at[0, m], three_recv.at[0, m], (r, me))
    for m, r in enumerate(rep_ids):
        arrived(one_ref.at[r], small_one.at[m], small_got.at[r])
    total = one_ref[0]
    for r in range(1, reps):
        total = total + one_ref[r]
    sum_ref[...] = total
    two_ref[me] = total
    for m, s in enumerate(seq_ids):
        push(sum_ref, two_ref.at[me], small_two.at[m], small_end.at[me], (rep, s))
    for n, who in enumerate(seq_ids):
        arrived(zi_ref.at[who], two_send.at[n], two_recv.at[who])
    for u in range(4):
        total = zi_ref[u].astype(wide)
        for f in range(1, frames):
            total = total + zi_ref[f * 4 + u].astype(wide)
        for t in range(3):
            qi_ref[:, t * width + u * cols : t * width + (u + 1) * cols] = total[:, t * cols : (t + 1) * cols].astype(
                jnp.bfloat16
            )
    wing = 3 * width // 2

    def shard(r, k):
        return oi_ref.at[pl.ds(pl.multiple_of(r * part, 16), part), pl.ds(k * wing, wing)]

    for k in range(2):
        mine = qi_ref.at[:, pl.ds(k * wing, wing)]
        push(mine, shard(rep, k), near_send.at[k], near_recv.at[k], (near[k], me))
        push(mine, shard(rep, k), past_send.at[k, 0], past_recv.at[k, 0], (past[k], me))
    for k in range(2):
        got = shard(near[k], k)
        arrived(got, near_send.at[k], near_recv.at[k])
        push(got, got, past_send.at[k, 1], past_recv.at[k, 1], (past[k], me))
    final = [
        pltpu.make_async_copy(qo_ref, oo_ref.at[pl.ds(pl.multiple_of(rep * part, 16), part), :], load_sem.at[0]),
        pltpu.make_async_copy(qi_ref, oi_ref.at[pl.ds(pl.multiple_of(rep * part, 16), part), :], load_sem.at[1]),
    ]
    for copy in final:
        copy.start()
    for h in range(halves):
        owner = place * halves + h

        @pl.when(owner != me)
        def _():
            shipped(h).wait_send()

    for m, s in enumerate(seq_ids):
        arrived(two_ref.at[s], small_two.at[m], small_end.at[s])
    total = two_ref[0]
    for s in range(1, count):
        total = total + two_ref[s]
    so_ref[...] = total
    for copy in final:
        copy.wait()
    for m in range(reps - 1):
        r = (rep + reps - 1 - m) % reps
        arrived(oo_ref.at[pl.ds(pl.multiple_of(r * part, 16), part), :], three_send.at[0, m], three_recv.at[0, m])
    for k in range(2):
        arrived(shard(past[k], k), past_send.at[k, 0], past_recv.at[k, 0])
        arrived(shard(rep ^ 3, k), past_send.at[k, 1], past_recv.at[k, 1])
    for copy in waits:
        copy.wait_send()


def reduce_weights(grad_in, grad_out, tokens, scaled, small, reps, count):
    width = grad_out.shape[1]
    own = grad_in.shape[1]
    rows = width // count
    part = rows // reps
    halves = grad_out.shape[0] // rows
    frames = count // 4
    each = (tokens.shape[0] - 2 * EDGE) // 4
    dma = pltpu.SemaphoreType.DMA
    low = jnp.bfloat16
    hbm = pl.BlockSpec(memory_space=pl.ANY)
    vmem = pl.BlockSpec(memory_space=pltpu.VMEM)
    lines = small.shape[0]
    return pl.pallas_call(
        functools.partial(reduce_kernel, reps, count),
        in_specs=[hbm] * 3 + [vmem] * 2,
        out_specs=[hbm, hbm, vmem, vmem],
        out_shape=[
            jax.ShapeDtypeStruct((rows, 3 * width), low),
            jax.ShapeDtypeStruct((rows, width), low),
            jax.ShapeDtypeStruct((each, width), jnp.float32),
            jax.ShapeDtypeStruct((lines, LANES), jnp.float32),
        ],
        scratch_shapes=[
            pltpu.VMEM((count, 2, part, own), low), pltpu.VMEM((count, 2, part, own), low),
            pltpu.VMEM((count, part, own), low), pltpu.VMEM((count, part, own), low), pltpu.VMEM((part, 3 * width), low),
            pltpu.VMEM((halves, 2, part, width), low), pltpu.VMEM((halves, 2, part, width), low),
            pltpu.VMEM((halves, part, width), low),
            pltpu.VMEM((frames, part, width), low), pltpu.VMEM((part, width), low),
            pltpu.VMEM((2, each, width), low), pltpu.VMEM((3, each, width), low),
            pltpu.VMEM((4, HEADER, width), low),
            dma((2 + 2 * (count + halves),)), dma((count + halves, 2)), dma((count + halves, 2)), dma((count + halves,)),
            dma((count + halves,)),
            dma((2,)), dma((2,)), dma((2, 2)), dma((2, 2)),
            dma((count + halves,)), dma((count + frames,)), dma((1, reps - 1)), dma((1, reps - 1)), dma((3,)), dma((3,)),
            dma((1,)), dma((4,)),
            pltpu.VMEM((lines, LANES), jnp.float32), pltpu.VMEM((reps, lines, LANES), jnp.float32),
            pltpu.VMEM((count, lines, LANES), jnp.float32), pltpu.VMEM((lines, LANES), jnp.float32),
            dma((reps - 1,)), dma((reps,)), dma((count - 1,)), dma((count,)),
        ],
        cost_estimate=pl.CostEstimate(flops=2_000_000_000, bytes_accessed=20_000_000, transcendentals=0),
        compiler_params=pltpu.CompilerParams(collective_id=5, has_side_effects=True, vmem_limit_bytes=40 << 20),
        name="reduce_weights",
    )(grad_in, grad_out, tokens, scaled, small)


def rms_scale(values):
    return lax.rsqrt(jnp.mean(values * values, axis=-1, keepdims=True) + EPS)


def norm_back(grad_out, values, inv_scale, gain):
    scaled_grad = grad_out * gain
    inner = jnp.mean(scaled_grad * values, axis=-1, keepdims=True)
    return inv_scale * scaled_grad - values * inv_scale**3 * inner


def pad_heads(values, dim):
    shaped = values.reshape(values.shape[:-1] + (-1, dim))
    shaped = jnp.pad(shaped, [(0, 0)] * (shaped.ndim - 1) + [(0, LANES - dim)])
    return shaped.reshape(values.shape[:-1] + (-1,))


def cut_heads(values, dim):
    shaped = values.reshape(values.shape[:-1] + (-1, LANES))[..., :dim]
    return shaped.reshape(values.shape[:-1] + (-1,))


def on_device(
    inputs, segment_ids, valid_mask, input_weight, output_weight, conv_kernel, head_mix, first_gain, second_gain,
    group_gain, gate_weight, up_weight, down_weight, cotangent,
):
    tokens, width = inputs.shape[1:]
    heads, taps, span = conv_kernel.shape
    dim = width // heads
    scale = dim ** (-0.5)
    count = lax.axis_size("seq")
    team = FRAME // tokens
    own_heads = heads // team
    own_width = own_heads * dim
    own_pairs = own_heads // 2
    groups = [[g * team + i for i in range(team)] for g in range(count // team)]
    seq_rank = lax.axis_index("seq")
    place = seq_rank % team
    frame_first = (seq_rank // team) * FRAME
    row_first = seq_rank * tokens
    contract_rows = (((0,), (0,)), ((), ()))

    resid_in = inputs[0].astype(jnp.float32)
    grad_out = cotangent[0].astype(jnp.float32)
    row_valid = lax.dynamic_slice_in_dim(valid_mask[0], row_first, tokens).astype(jnp.float32)[:, None]
    ahead = lambda values: jnp.pad(values, (HEADER, 0))
    codes = make_codes(
        lax.dynamic_slice_in_dim(ahead(segment_ids[0]), frame_first, FRAME + HEADER),
        lax.dynamic_slice_in_dim(ahead(valid_mask[0]), frame_first, FRAME + HEADER),
    )
    own_kernel = lax.dynamic_slice_in_dim(conv_kernel, place * own_heads, own_heads)
    own_mix = lax.dynamic_slice_in_dim(head_mix, place * own_pairs, own_pairs).reshape(own_pairs, 4)
    own_gain = pad_heads(lax.dynamic_slice_in_dim(group_gain, place * own_width, own_width)[None], dim)
    toep, toep_split = split_toeplitz(toeplitz(own_kernel, scale))

    reps = lax.axis_size("rep")
    direct = team == 4 and reps == 4 and (width // count) % (16 * reps) == 0
    first_scale = rms_scale(resid_in)
    normed_in = (resid_in * first_scale * first_gain).astype(jnp.bfloat16)
    if direct:
        own_input, normed_frame = gather_weight(input_weight, normed_in, reps, count)
    else:
        full_input = lax.all_gather(input_weight, "seq", axis=0, tiled=True)
        own_input = lax.dynamic_slice_in_dim(full_input.reshape(width, 3, width), place * own_width, own_width, axis=2)
        own_input = own_input.reshape(width, 3 * own_width)
        normed_frame = lax.all_gather(normed_in, "seq", axis=0, tiled=True, axis_index_groups=groups)
        ends = lax.all_gather(normed_in[tokens - HEADER :], "seq", axis=0)
        last = jnp.maximum(seq_rank // team * team - 1, 0)
        end = jnp.where(frame_first > 0, lax.dynamic_index_in_dim(ends, last, keepdims=False), 0)
        lead = jnp.zeros((EDGE - HEADER, width), jnp.bfloat16)
        normed_frame = jnp.concatenate([lead, end, normed_frame, jnp.zeros((EDGE, width), jnp.bfloat16)], axis=0)
    dmlp = (row_valid * grad_out).astype(jnp.bfloat16)
    own_input, output_weight, dmlp = lax.optimization_barrier((own_input, output_weight, dmlp))
    full_output = lax.all_gather(output_weight, "seq", axis=0, tiled=True)
    own_input = pad_heads(own_input, dim)
    proj = jnp.dot(normed_frame, own_input, preferred_element_type=jnp.float32).astype(jnp.bfloat16)
    dmlp_all = lax.all_gather(dmlp, "seq", axis=0, tiled=True)
    normed_own, att, prob = attention_forward(proj, toep_split, codes, own_gain, own_mix, dim, taps)
    normed_own, full_output = lax.optimization_barrier((normed_own, full_output))
    normed_own = cut_heads(normed_own, dim)

    def to_rows(values):
        moved = lax.all_to_all(
            values.reshape(team, tokens, own_width), "seq", 0, 0, tiled=True, axis_index_groups=groups
        )
        return moved.transpose(1, 0, 2).reshape(tokens, width)

    normed = frame_swap(normed_own) if direct else to_rows(normed_own)
    branch = jnp.dot(normed, full_output, preferred_element_type=jnp.float32)
    resid = resid_in + row_valid * branch
    second_scale = rms_scale(resid)
    normed_mid = (resid * second_scale * second_gain).astype(jnp.bfloat16)
    normed_mid, dmlp_all = lax.optimization_barrier((normed_mid, dmlp_all))
    inputs_all = lax.all_gather(normed_mid, "seq", axis=0, tiled=True)
    gate = jnp.dot(inputs_all, gate_weight, preferred_element_type=jnp.float32)
    up_proj = jnp.dot(inputs_all, up_weight, preferred_element_type=jnp.float32)
    dhidden = jnp.dot(dmlp_all, down_weight.T, preferred_element_type=jnp.float32)
    sigmoid_gate = jax.nn.sigmoid(gate)
    gate_grad = (dhidden * up_proj * sigmoid_gate * (1.0 + gate * (1.0 - sigmoid_gate))).astype(jnp.bfloat16)
    up_grad = (dhidden * gate * sigmoid_gate).astype(jnp.bfloat16)
    hidden = (jax.nn.silu(gate) * up_proj).astype(jnp.bfloat16)
    dmid_part = (
        jnp.dot(gate_grad, gate_weight.T, preferred_element_type=jnp.float32)
        + jnp.dot(up_grad, up_weight.T, preferred_element_type=jnp.float32)
    ).astype(jnp.bfloat16)
    gate_grad, up_grad, hidden, dmid_part = lax.optimization_barrier((gate_grad, up_grad, hidden, dmid_part))
    dmid_low = lax.psum_scatter(dmid_part, "seq", scatter_dimension=0, tiled=True)
    mlp_part = jnp.dot(hidden, down_weight, preferred_element_type=jnp.float32).astype(jnp.bfloat16)
    mlp_grads = [
        lax.dot_general(left, right, contract_rows, preferred_element_type=jnp.float32).astype(jnp.bfloat16)
        for left, right in ((inputs_all, gate_grad), (inputs_all, up_grad), (hidden, dmlp_all))
    ]
    dmid_low, mlp_part, mlp_grads = lax.optimization_barrier((dmid_low, mlp_part, mlp_grads))
    mlp_low = lax.psum_scatter(mlp_part, "seq", scatter_dimension=0, tiled=True)
    mlp_grads = [lax.psum(value, "rep") for value in mlp_grads]
    dmid = dmid_low.astype(jnp.float32)
    second_part = jnp.sum(dmid * resid * second_scale, axis=0)
    dresid = grad_out + norm_back(dmid, resid, second_scale, second_gain)
    dbranch = (row_valid * dresid).astype(jnp.bfloat16)
    if direct:
        dbranch_frame = frame_gather(dbranch)
    else:
        dbranch_frame = lax.all_gather(dbranch, "seq", axis=0, tiled=True, axis_index_groups=groups)
    own_output = lax.dynamic_slice_in_dim(full_output, place * own_width, own_width, axis=0)
    dnormed_own = lax.dot_general(dbranch_frame, own_output, NT, preferred_element_type=jnp.float32)
    own_output_grad = lax.dot_general(normed_own, dbranch_frame, contract_rows, preferred_element_type=jnp.float32)
    own_output_grad = own_output_grad.astype(jnp.bfloat16)
    dq, dk, dv, dtoep, dmix, dgain = attention_backward(
        proj, toep, codes, prob, att, pad_heads(dnormed_own, dim), own_gain, own_mix, dim, taps, span
    )
    dproj = jnp.concatenate([dq, dk, dv], axis=1)
    own_input_grad = lax.dot_general(normed_frame, dproj, contract_rows, preferred_element_type=jnp.float32)
    own_input_grad = cut_heads(own_input_grad.astype(jnp.bfloat16), dim)
    dnormin_part = lax.dot_general(dproj, own_input, NT, preferred_element_type=jnp.float32).astype(jnp.bfloat16)
    def spread(values, size):
        empty = jnp.zeros((size,) + values.shape[1:], jnp.float32)
        return lax.dynamic_update_slice_in_dim(empty, values, place * values.shape[0], 0)

    kernel_part = spread(tap_grads(dtoep, taps, span, scale), heads)
    mix_part = spread(jnp.sum(dmix[:, :4], axis=-1).reshape(own_pairs, 2, 2), heads // 2)
    group_part = spread(cut_heads(dgain, dim)[0], width)
    parts = (kernel_part, mix_part, second_part, group_part)
    if direct:
        flat = jnp.concatenate([jnp.zeros((width,), jnp.float32)] + [value.reshape(-1) for value in parts])
        size = -(-flat.shape[0] // (8 * LANES)) * 8 * LANES
        small = jnp.pad(flat, (0, size - flat.shape[0])).reshape(-1, LANES)
        grad_input_w, grad_output_w, dnormin, small = reduce_weights(
            own_input_grad, own_output_grad, dnormin_part, resid_in * first_scale, small, reps, count
        )
        flat = small.reshape(-1)
        grad_first, others, start = flat[:width], [], width
        for value in parts:
            others.append(flat[start : start + value.size].reshape(value.shape))
            start += value.size
    else:
        dnormin = lax.psum_scatter(
            dnormin_part[EDGE : EDGE + FRAME], "seq", scatter_dimension=0, tiled=True, axis_index_groups=groups
        ).astype(jnp.float32)
        starts = lax.all_gather(dnormin_part[EDGE - HEADER : EDGE], "seq", axis=0).astype(jnp.float32)
        later = lax.dynamic_slice_in_dim(
            jnp.pad(starts, ((0, team), (0, 0), (0, 0))), (seq_rank // team + 1) * team, team
        ).sum(axis=0)
        later = jnp.where(place == team - 1, later, 0.0)
        dnormin = dnormin + jnp.pad(later, ((tokens - HEADER, 0), (0, 0)))
        pieces = lax.all_to_all(own_input_grad.reshape(count, width // count, 3 * own_width), "seq", 0, 0, tiled=True)
        pieces = pieces.reshape(count // team, team, width // count, 3, own_width).astype(jnp.float32).sum(axis=0)
        grad_input_w = pieces.transpose(1, 2, 0, 3).reshape(width // count, 3 * width)
        spots = jnp.zeros((width, width), jnp.bfloat16)
        spots = lax.dynamic_update_slice_in_dim(spots, own_output_grad, place * own_width, 0)
        grad_output_w = lax.psum_scatter(spots, "seq", scatter_dimension=0, tiled=True)
        grad_input_w, grad_output_w = [
            lax.psum(value.astype(jnp.bfloat16), "rep") for value in (grad_input_w, grad_output_w)
        ]
    dnormin, mlp_low, mlp_grads = lax.optimization_barrier((dnormin, mlp_low, mlp_grads))
    result = resid + row_valid * mlp_low.astype(jnp.float32)
    if not direct:
        first_part = jnp.sum(dnormin * resid_in * first_scale, axis=0)
        grad_first, others = lax.psum((first_part, parts), ("rep", "seq"))
    grad_in = dresid + norm_back(dnormin, resid_in, first_scale, first_gain)

    grad_kernel, grad_mix, grad_second, grad_group = others
    grads = [value.astype(jnp.float32) for value in (grad_input_w, grad_output_w, *mlp_grads)]
    return (
        result.astype(jnp.bfloat16)[None], grad_in.astype(jnp.bfloat16)[None], grads[0], grads[1], grad_kernel,
        grad_mix, grad_first, grad_second, grad_group, grads[2], grads[3], grads[4],
    )


def solution(mesh):
    in_specs = (
        P("rep", "seq", None), P("rep", None), P("rep", None), P("seq", None), P("seq", None), P(), P(), P(), P(), P(),
        P(None, "seq"), P(None, "seq"), P("seq", None), P("rep", "seq", None),
    )
    out_specs = (
        P("rep", "seq", None), P("rep", "seq", None), P("seq", None), P("seq", None), P(), P(), P(), P(), P(),
        P(None, "seq"), P(None, "seq"), P("seq", None),
    )
    return jax.shard_map(on_device, mesh=mesh, in_specs=in_specs, out_specs=out_specs, check_vma=False)
```

```python
import functools
import jax
import jax.numpy as jnp
from jax import lax
from jax.experimental import pallas as pl
from jax.experimental.pallas import tpu as pltpu
from jax.sharding import PartitionSpec as P

FRAME = 1024


EPS = 1e-06
LANES = 128
ROWS = 256
EDGE = 64
HEADER = 16
NEG = -1e30
PROB = jnp.float32

NT = (((1,), (1,)), ((), ()))
NN = (((1,), (0,)), ((), ()))


def dot(a, b, dims=NN):
    return lax.dot_general(a, b, dims, preferred_element_type=jnp.float32)


def toeplitz(kernel, scale):
    heads, taps, span = kernel.shape
    shape = (heads, 2 * LANES, taps * LANES)
    lane = lax.broadcasted_iota(jnp.int32, shape, 2)
    tap = lax.broadcasted_iota(jnp.int32, shape, 1)
    diff = lane % LANES + EDGE + span // 2 - tap
    total = jnp.zeros(shape, jnp.float32)
    for b in range(span):
        weight = jnp.repeat(kernel[:, :, b] * scale, LANES, axis=1)[:, None, :]
        total = total + jnp.where(diff == b, weight, 0.0)
    return total


def split_toeplitz(full):
    kept = lax.reduce_precision(full, exponent_bits=8, mantissa_bits=7)
    high = kept.astype(jnp.bfloat16)
    low = (full - kept).astype(jnp.bfloat16)
    return high, jnp.concatenate([high, high, low], axis=1)


def tap_grads(sums, taps, span, scale):
    shaped = sums.reshape(sums.shape[0], 16, taps, LANES).sum(axis=-1)
    return shaped[:, :span].transpose(0, 2, 1) * scale


def lane_mask(dim):
    return lax.broadcasted_iota(jnp.int32, (ROWS, LANES), 1) < dim


def group_stats(att, dim):
    mean = jnp.sum(att, axis=-1, keepdims=True) / dim
    centred = jnp.where(lane_mask(dim), att - mean, 0.0)
    var = jnp.sum(centred * centred, axis=-1, keepdims=True) / dim
    inv = lax.rsqrt(var + EPS)
    return centred * inv, inv


def widen(sources, targets, dim, pairs):
    pair = pl.program_id(0)
    for source, target in zip(sources, targets):
        for h in range(2):
            target[:, h * LANES + dim : (h + 1) * LANES] = jnp.zeros((target.shape[0], LANES - dim), target.dtype)
        for p in range(pairs):

            @pl.when(pair == p)
            def _():
                for h in range(2):
                    left = (2 * p + h) * dim
                    target[:, h * LANES : h * LANES + dim] = source[:, left : left + dim]


def place_head(target, rows, left, h, value, dim, pairs):
    pair = pl.program_id(0)
    for p in range(pairs):

        @pl.when(pair == p)
        def _():
            at = left + (2 * p + h) * dim
            target[rows, at : at + dim] = value[:, :dim].astype(target.dtype)


def forward_kernel(
    dim, taps, pairs, qs_ref, ks_ref, vs_ref, t_ref, rowc_ref, colp_ref, colc_ref, gain_ref, mix_ref,
    normed_ref, att_ref, prob_ref, lm_ref, lo_ref, p_ref, cv_ref, mx_ref, sm_ref, acc_ref, q_ref, k_ref, v_ref,
):
    step = pl.program_id(1)

    @pl.when(step == 0)
    def _():
        widen((qs_ref, ks_ref, vs_ref), (q_ref, k_ref, v_ref), dim, pairs)

    first = step * ROWS
    top = pl.multiple_of(first + EDGE - HEADER, 16)
    tall = ROWS + HEADER
    codes = rowc_ref[pl.ds(top, tall), :]
    ipos = first - HEADER + lax.broadcasted_iota(jnp.int32, (tall, LANES), 0)
    lane = lax.broadcasted_iota(jnp.int32, (tall, LANES), 1)
    live = codes[HEADER:] >= 0

    def logits(c, carry):
        at = pl.multiple_of(c * LANES, LANES)
        keep = (codes == colp_ref[:, pl.ds(at, LANES)]) & (at - EDGE + lane <= ipos)
        for h in range(2):
            cols = slice(h * LANES, (h + 1) * LANES)
            raw = dot(q_ref[pl.ds(top, tall), cols], k_ref[pl.ds(at, LANES), cols], NT)
            raw = jnp.where(keep, raw, 0.0)
            high = raw.astype(jnp.bfloat16)
            lm_ref[h, :, pl.ds(at, LANES)] = high
            lo_ref[h, :, pl.ds(at, LANES)] = (raw - high.astype(jnp.float32)).astype(jnp.bfloat16)
        return carry

    lax.fori_loop(0, 2 * step + 3, logits, 0)
    mx_ref[...] = jnp.full(mx_ref.shape, NEG, jnp.float32)

    def convolve(c, carry):
        for n in range(2):
            convolve_block(pl.multiple_of((2 * c + n) * LANES, LANES))
        return carry

    def convolve_block(at):
        keep = (codes[HEADER:] == colc_ref[:, pl.ds(at, LANES)]) & (at + lane[HEADER:] <= ipos[HEADER:])
        for h in range(2):
            high = lm_ref[h, :, pl.ds(at, 2 * LANES)]
            p_ref[h] = dot(jnp.concatenate([high, lo_ref[h, :, pl.ds(at, 2 * LANES)], high], axis=1), t_ref[h])
            conv = p_ref[h, HEADER:, :LANES]
            for a in range(1, taps):
                conv = conv + p_ref[h, HEADER - a : tall - a, a * LANES : (a + 1) * LANES]
            conv = jnp.where(keep, conv, NEG)
            cv_ref[h, :, pl.ds(at, LANES)] = conv
            mx_ref[h] = jnp.maximum(mx_ref[h], conv)

    lax.fori_loop(0, step + 1, convolve, 0)
    sm_ref[...] = jnp.zeros(sm_ref.shape, jnp.float32)
    for h in range(2):
        peak = jnp.max(mx_ref[h], axis=-1, keepdims=True)
        mx_ref[h] = jnp.where(live, jnp.broadcast_to(peak, (ROWS, LANES)), 0.0)

    def exponents(c, carry):
        for h in range(2):
            total = sm_ref[h]
            for n in range(2):
                at = pl.multiple_of((2 * c + n) * LANES, LANES)
                value = jnp.exp(cv_ref[h, :, pl.ds(at, LANES)] - mx_ref[h])
                cv_ref[h, :, pl.ds(at, LANES)] = value
                total = total + value
            sm_ref[h] = total
        return carry

    lax.fori_loop(0, step + 1, exponents, 0)
    for h in range(2):
        total = jnp.sum(sm_ref[h], axis=-1, keepdims=True)
        total = jnp.where(live, jnp.broadcast_to(total, (ROWS, LANES)), 1.0)
        sm_ref[h] = 1.0 / total
    acc_ref[...] = jnp.zeros(acc_ref.shape, jnp.float32)
    pair = pl.program_id(0)
    mix = [[mix_ref[pair, 2 * g + h] for h in range(2)] for g in range(2)]

    def mixing(c, carry):
        at = pl.multiple_of(c * 2 * LANES, 2 * LANES)
        mixed = [[], []]
        for n in range(2):
            spot = pl.ds(pl.multiple_of(at + n * LANES, LANES), LANES)
            prob = [cv_ref[h, :, spot] * sm_ref[h] for h in range(2)]
            for g in range(2):
                prob_ref[g, :, spot] = prob[g].astype(prob_ref.dtype)
                mixed[g].append((mix[g][0] * prob[0] + mix[g][1] * prob[1]).astype(jnp.bfloat16))
        for g in range(2):
            cols = slice(g * LANES, (g + 1) * LANES)
            value = v_ref[pl.ds(pl.multiple_of(at + EDGE, 16), 2 * LANES), cols]
            acc_ref[g] += dot(jnp.concatenate(mixed[g], axis=1), value)
        return carry

    lax.fori_loop(0, step + 1, mixing, 0)
    for g in range(2):
        att = acc_ref[g]
        att_ref[:, g * LANES : (g + 1) * LANES] = att
        unit, _ = group_stats(att, dim)
        normed = unit * gain_ref[0:1, g * LANES : (g + 1) * LANES]
        place_head(normed_ref, pl.ds(pl.multiple_of(first, ROWS), ROWS), 0, g, normed, dim, pairs)


def backward_kernel(
    dim, taps, span, pairs, qs_ref, ks_ref, vs_ref, t_ref, rowc_ref, colp_ref, colt_ref, rowt_ref, prob_ref, att_ref, dns_ref,
    gain_ref, mix_ref, dproj_ref, taps_ref, dmix_ref, dgain_ref,
    dp_ref, dc_ref, dl_ref, lt_ref, dkt_ref, dvt_ref, datt_ref, dattt_ref, qt_ref, rs_ref, dqa_ref, dm_ref, ahead_ref, g_ref, q_ref, k_ref, v_ref, dn_ref,
):
    pair = pl.program_id(0)
    turn = pl.program_id(1)
    step = pl.num_programs(1) - 1 - turn
    first = pl.multiple_of(step * ROWS, ROWS)
    own = pl.multiple_of(first + EDGE, 16)
    codes = rowc_ref[pl.ds(own, ROWS), :]
    ipos = first + lax.broadcasted_iota(jnp.int32, (ROWS, LANES), 0)
    lane = lax.broadcasted_iota(jnp.int32, (ROWS, LANES), 1)
    blocks = 2 * step + 2
    mix = [[mix_ref[pair, 2 * g + h] for h in range(2)] for g in range(2)]

    @pl.when(turn == 0)
    def _():
        dc_ref[...] = jnp.zeros(dc_ref.shape, jnp.float32)
        dkt_ref[...] = jnp.zeros(dkt_ref.shape, jnp.float32)
        dvt_ref[...] = jnp.zeros(dvt_ref.shape, jnp.float32)
        g_ref[...] = jnp.zeros(g_ref.shape, jnp.float32)
        dmix_ref[...] = jnp.zeros(dmix_ref.shape, jnp.float32)
        dgain_ref[...] = jnp.zeros(dgain_ref.shape, jnp.float32)
        widen((qs_ref, ks_ref, vs_ref), (q_ref, k_ref, v_ref), dim, pairs)

        @pl.when(pair == 0)
        def _():
            for rows in (slice(0, EDGE), slice(dproj_ref.shape[0] - EDGE, dproj_ref.shape[0])):
                dproj_ref[rows, :] = jnp.zeros((EDGE, dproj_ref.shape[1]), jnp.bfloat16)

    widen((dns_ref,), (dn_ref,), dim, pairs)

    @pl.when(turn > 0)
    def _():
        for h in range(2):
            dc_ref[h, ROWS:, :] = dc_ref[h, :8, :]

    for g in range(2):
        cols = slice(g * LANES, (g + 1) * LANES)
        unit, inv = group_stats(att_ref[:, cols], dim)
        grad = dn_ref[:, cols]
        dgain_ref[0:1, cols] += jnp.sum(grad * unit, axis=0, keepdims=True)
        scaled = grad * gain_ref[0:1, cols]
        mean = jnp.sum(scaled, axis=-1, keepdims=True) / dim
        inner = jnp.sum(scaled * unit, axis=-1, keepdims=True) / dim
        datt = inv * (scaled - mean - unit * inner)
        datt = jnp.where(lane_mask(dim), datt, 0.0)
        high = datt.astype(jnp.bfloat16)
        datt_ref[g, :, :LANES] = high
        datt_ref[g, :, LANES:] = (datt - high.astype(jnp.float32)).astype(jnp.bfloat16)
        dattt_ref[g] = datt.T.astype(jnp.bfloat16)
        qt_ref[g] = q_ref[pl.ds(own, ROWS), cols].astype(jnp.float32).T.astype(jnp.bfloat16)
    rs_ref[...] = jnp.zeros(rs_ref.shape, jnp.float32)
    dm_ref[...] = jnp.zeros(dm_ref.shape, jnp.float32)

    def probs(c, carry):
        for n in range(2):
            probs_block(pl.multiple_of((2 * c + n) * LANES, LANES))
        return carry

    def probs_block(at):
        prob = [prob_ref[h, :, pl.ds(at, LANES)].astype(jnp.float32) for h in range(2)]
        dmixed = []
        for g in range(2):
            cols = slice(g * LANES, (g + 1) * LANES)
            value = v_ref[pl.ds(at + EDGE, LANES), cols]
            dmixed.append(dot(datt_ref[g], jnp.concatenate([value, value], axis=1), NT))
            mixed = (mix[g][0] * prob[0] + mix[g][1] * prob[1]).astype(jnp.bfloat16)
            dvt_ref[g, :, pl.ds(at, LANES)] += dot(dattt_ref[g], mixed)
            for h in range(2):
                dm_ref[2 * g + h] += dmixed[g] * prob[h]
        for h in range(2):
            dprob = mix[0][h] * dmixed[0] + mix[1][h] * dmixed[1]
            dp_ref[h, :, pl.ds(at, LANES)] = dprob
            rs_ref[h] += prob[h] * dprob

    lax.fori_loop(0, step + 1, probs, 0)
    for h in range(2):
        rs_ref[h] = jnp.broadcast_to(jnp.sum(rs_ref[h], axis=-1, keepdims=True), (ROWS, LANES))
    for n in range(4):
        dmix_ref[0, n : n + 1, :] += jnp.sum(dm_ref[n], axis=0, keepdims=True)

    tlane = lax.broadcasted_iota(jnp.int32, (LANES, ROWS), 1)
    trow = lax.broadcasted_iota(jnp.int32, (LANES, ROWS), 0)

    def transposed_logits(c, carry):
        at = pl.multiple_of(c * LANES, LANES)
        wide = jnp.concatenate([colt_ref[pl.ds(at, LANES), :]] * 2, axis=1)
        keep = (wide == rowt_ref[:, pl.ds(first, ROWS)]) & (at - EDGE + trow <= first + tlane)
        for h in range(2):
            cols = slice(h * LANES, (h + 1) * LANES)
            raw = dot(k_ref[pl.ds(at, LANES), cols], q_ref[pl.ds(own, ROWS), cols], NT)
            lt_ref[h, pl.ds(at, LANES), :] = jnp.where(keep, raw, 0.0).astype(jnp.bfloat16)
            dl_ref[h, :, pl.ds(at, LANES)] = jnp.zeros((ROWS, LANES), jnp.float32)
        return carry

    lax.fori_loop(0, blocks + 1, transposed_logits, 0)

    def convolve(c, carry):
        for n in range(2):
            convolve_block(pl.multiple_of((2 * c + n) * LANES, LANES))
        return carry

    def convolve_block(at):
        for h in range(2):
            prob = prob_ref[h, :, pl.ds(at, LANES)].astype(jnp.float32)
            dc_ref[h, :ROWS, pl.ds(at, LANES)] = prob * (dp_ref[h, :, pl.ds(at, LANES)] - rs_ref[h])
            shifted = jnp.concatenate(
                [dc_ref[h, a : a + ROWS, pl.ds(at, LANES)].astype(jnp.bfloat16) for a in range(taps)], axis=1
            )
            g_ref[h] += dot(lt_ref[h, pl.ds(at, 2 * LANES), :], shifted)
            dl_ref[h, :, pl.ds(at, 2 * LANES)] += dot(shifted, t_ref[h], NT)

    lax.fori_loop(0, step + 1, convolve, 0)
    dqa_ref[...] = jnp.zeros(dqa_ref.shape, jnp.float32)

    def logits(c, carry):
        at = pl.multiple_of(c * LANES, LANES)
        keep = (codes == colp_ref[:, pl.ds(at, LANES)]) & (at - EDGE + lane <= ipos)
        for h in range(2):
            cols = slice(h * LANES, (h + 1) * LANES)
            dl = jnp.where(keep, dl_ref[h, :, pl.ds(at, LANES)], 0.0).astype(jnp.bfloat16)
            dqa_ref[h] += dot(dl, k_ref[pl.ds(at, LANES), cols])
            dkt_ref[h, :, pl.ds(at, LANES)] += dot(qt_ref[h], dl)
        return carry

    lax.fori_loop(0, blocks + 1, logits, 0)
    for h in range(2):
        place_head(dproj_ref, pl.ds(own, ROWS), 0, h, dqa_ref[h], dim, pairs)

    @pl.when(step == 0)
    def _():
        head = slice(EDGE - HEADER, EDGE)
        wide = (HEADER, 2 * LANES)
        keep = jnp.concatenate([rowc_ref[head, :]] * 2, axis=1) == colp_ref[:, : 2 * LANES]
        keep = keep & (
            lax.broadcasted_iota(jnp.int32, wide, 1) - EDGE <= lax.broadcasted_iota(jnp.int32, wide, 0) - HEADER
        )
        for h in range(2):
            cols = slice(h * LANES, (h + 1) * LANES)
            ahead_ref[:HEADER, :] = jnp.zeros((HEADER, LANES), jnp.float32)
            ahead_ref[HEADER:, :] = dc_ref[h, :HEADER, :LANES]
            shifted = jnp.concatenate(
                [ahead_ref[a : a + HEADER, :].astype(jnp.bfloat16) for a in range(taps)], axis=1
            )
            near = k_ref[: 2 * LANES, cols]
            query = q_ref[head, cols]
            raw = jnp.where(keep, dot(query, near, NT), 0.0)
            g_ref[h] += dot(raw.T.astype(jnp.bfloat16), shifted)
            dl = jnp.where(keep, dot(shifted, t_ref[h], NT), 0.0).astype(jnp.bfloat16)
            place_head(dproj_ref, head, 0, h, dot(dl, near), dim, pairs)
            dkt_ref[h, :, : 2 * LANES] += dot(query.astype(jnp.float32).T.astype(jnp.bfloat16), dl)
            every = slice(0, dkt_ref.shape[2])
            place_head(dproj_ref, every, 2 * pairs * dim, h, dkt_ref[h].T, dim, pairs)
            inner = slice(EDGE, EDGE + dvt_ref.shape[2])
            place_head(dproj_ref, inner, 4 * pairs * dim, h, dvt_ref[h].T, dim, pairs)
        shape = (2 * LANES, taps * LANES)
        lanes = lax.broadcasted_iota(jnp.int32, shape, 1) & (LANES - 1)
        diff = lanes + (EDGE + span // 2) - lax.broadcasted_iota(jnp.int32, shape, 0)

        def diagonals(b, carry):
            for h in range(2):
                part = jnp.where(diff == b, g_ref[h], 0.0)
                taps_ref[h, pl.ds(b, 1), :] = jnp.sum(part, axis=0, keepdims=True)
            return carry

        lax.fori_loop(0, span, diagonals, 0)


def attention_forward(proj, toep, codes, gain, mix, dim, taps):
    tall = proj.shape[0]
    frame = tall - 2 * EDGE
    pairs = mix.shape[0]
    steps = frame // ROWS
    whole = lambda off: pl.BlockSpec((tall, 2 * pairs * dim), lambda p, r: (0, off))
    wide = pairs * 2 * LANES
    return pl.pallas_call(
        functools.partial(forward_kernel, dim, taps, mix.shape[0]),
        grid=(pairs, steps),
        in_specs=[
            whole(0), whole(1), whole(2),
            pl.BlockSpec((2, 6 * LANES, taps * LANES), lambda p, r: (p, 0, 0)),
            pl.BlockSpec((tall, LANES), lambda p, r: (0, 0)),
            pl.BlockSpec((1, tall), lambda p, r: (0, 0)),
            pl.BlockSpec((1, frame), lambda p, r: (0, 0)),
            pl.BlockSpec((1, 2 * LANES), lambda p, r: (0, p)),
            pl.BlockSpec(memory_space=pltpu.SMEM),
        ],
        out_specs=[
            pl.BlockSpec((frame, 2 * pairs * dim), lambda p, r: (0, 0)),
            pl.BlockSpec((ROWS, 2 * LANES), lambda p, r: (r, p)),
            pl.BlockSpec((2, ROWS, frame), lambda p, r: (p, r, 0)),
        ],
        out_shape=[
            jax.ShapeDtypeStruct((frame, 2 * pairs * dim), jnp.bfloat16),
            jax.ShapeDtypeStruct((frame, wide), jnp.float32),
            jax.ShapeDtypeStruct((2 * pairs, frame, frame), PROB),
        ],
        scratch_shapes=[
            pltpu.VMEM((2, ROWS + HEADER, tall), jnp.bfloat16),
            pltpu.VMEM((2, ROWS + HEADER, tall), jnp.bfloat16),
            pltpu.VMEM((2, ROWS + HEADER, taps * LANES), jnp.float32),
            pltpu.VMEM((2, ROWS, frame), jnp.float32),
            pltpu.VMEM((2, ROWS, LANES), jnp.float32),
            pltpu.VMEM((2, ROWS, LANES), jnp.float32),
            pltpu.VMEM((2, ROWS, LANES), jnp.float32),
            pltpu.VMEM((tall, 2 * LANES), jnp.bfloat16),
            pltpu.VMEM((tall, 2 * LANES), jnp.bfloat16),
            pltpu.VMEM((tall, 2 * LANES), jnp.bfloat16),
        ],
        cost_estimate=pl.CostEstimate(flops=10_000_000_000, bytes_accessed=40_000_000, transcendentals=0),
        compiler_params=pltpu.CompilerParams(vmem_limit_bytes=48 << 20),
        name="attend",
    )(proj, proj, proj, toep, codes["row"], codes["colp"], codes["col"], gain, mix)


def attention_backward(proj, toep, codes, prob, att, dnormed, gain, mix, dim, taps, span):
    tall = proj.shape[0]
    frame = tall - 2 * EDGE
    pairs = mix.shape[0]
    steps = frame // ROWS
    whole = lambda off: pl.BlockSpec((tall, 2 * pairs * dim), lambda p, r: (0, off))
    wide = pairs * 2 * LANES
    back = lambda r: steps - 1 - r
    return pl.pallas_call(
        functools.partial(backward_kernel, dim, taps, span, mix.shape[0]),
        grid=(pairs, steps),
        in_specs=[
            whole(0), whole(1), whole(2),
            pl.BlockSpec((2, 2 * LANES, taps * LANES), lambda p, r: (p, 0, 0)),
            pl.BlockSpec((tall, LANES), lambda p, r: (0, 0)),
            pl.BlockSpec((1, tall), lambda p, r: (0, 0)),
            pl.BlockSpec((tall, LANES), lambda p, r: (0, 0)),
            pl.BlockSpec((1, frame), lambda p, r: (0, 0)),
            pl.BlockSpec((2, ROWS, frame), lambda p, r: (p, back(r), 0)),
            pl.BlockSpec((ROWS, 2 * LANES), lambda p, r: (back(r), p)),
            pl.BlockSpec((ROWS, 2 * pairs * dim), lambda p, r: (back(r), 0)),
            pl.BlockSpec((1, 2 * LANES), lambda p, r: (0, p)),
            pl.BlockSpec(memory_space=pltpu.SMEM),
        ],
        out_specs=[
            pl.BlockSpec((tall, 6 * pairs * dim), lambda p, r: (0, 0)),
            pl.BlockSpec((2, 16, taps * LANES), lambda p, r: (p, 0, 0)),
            pl.BlockSpec((1, 8, LANES), lambda p, r: (p, 0, 0)),
            pl.BlockSpec((1, 2 * LANES), lambda p, r: (0, p)),
        ],
        out_shape=[
            jax.ShapeDtypeStruct((tall, 6 * pairs * dim), jnp.bfloat16),
            jax.ShapeDtypeStruct((2 * pairs, 16, taps * LANES), jnp.float32),
            jax.ShapeDtypeStruct((pairs, 8, LANES), jnp.float32),
            jax.ShapeDtypeStruct((1, wide), jnp.float32),
        ],
        scratch_shapes=[
            pltpu.VMEM((2, ROWS, frame), jnp.float32),
            pltpu.VMEM((2, ROWS + 8, frame), jnp.float32),
            pltpu.VMEM((2, ROWS, tall), jnp.float32),
            pltpu.VMEM((2, tall, ROWS), jnp.bfloat16),
            pltpu.VMEM((2, LANES, tall), jnp.float32),
            pltpu.VMEM((2, LANES, frame), jnp.float32),
            pltpu.VMEM((2, ROWS, 2 * LANES), jnp.bfloat16),
            pltpu.VMEM((2, LANES, ROWS), jnp.bfloat16),
            pltpu.VMEM((2, LANES, ROWS), jnp.bfloat16),
            pltpu.VMEM((2, ROWS, LANES), jnp.float32),
            pltpu.VMEM((2, ROWS, LANES), jnp.float32),
            pltpu.VMEM((4, ROWS, LANES), jnp.float32),
            pltpu.VMEM((2 * HEADER, LANES), jnp.float32),
            pltpu.VMEM((2, 2 * LANES, taps * LANES), jnp.float32),
            pltpu.VMEM((tall, 2 * LANES), jnp.bfloat16),
            pltpu.VMEM((tall, 2 * LANES), jnp.bfloat16),
            pltpu.VMEM((tall, 2 * LANES), jnp.bfloat16),
            pltpu.VMEM((ROWS, 2 * LANES), jnp.float32),
        ],
        cost_estimate=pl.CostEstimate(flops=10_000_000_000, bytes_accessed=40_000_000, transcendentals=0),
        compiler_params=pltpu.CompilerParams(vmem_limit_bytes=48 << 20),
        name="attend_back",
    )(proj, proj, proj, toep, codes["row"], codes["colp"], codes["colt"], codes["rowt"], prob, att, dnormed, gain, mix)


def make_codes(segment, valid):
    row = jnp.where(valid > 0, segment, -1)
    col = jnp.where(valid > 0, segment, -2)
    rowp = jnp.pad(row, (EDGE - HEADER, EDGE), constant_values=-1)
    colp = jnp.pad(col, (EDGE - HEADER, EDGE), constant_values=-2)
    tall = rowp.shape[0]
    return {
        "row": jnp.broadcast_to(rowp[:, None], (tall, LANES)),
        "colt": jnp.broadcast_to(colp[:, None], (tall, LANES)),
        "colp": colp[None],
        "col": col[None, HEADER:],
        "rowt": row[None, HEADER:],
    }


MESH = pl.DeviceIdType.MESH
TOKENS_AFTER = 2


def meet(peers):
    barrier = pltpu.get_barrier_semaphore()
    for peer in peers:
        pl.semaphore_signal(barrier, inc=1, device_id=peer, device_id_type=MESH)
    pl.semaphore_wait(barrier, len(peers))


def send(src, dst, send_sem, recv_sem, peer):
    return pltpu.make_async_remote_copy(
        src_ref=src, dst_ref=dst, send_sem=send_sem, recv_sem=recv_sem, device_id=peer, device_id_type=MESH
    )


def gather_kernel(
    reps, count, w_ref, x_ref, z_ref, wc_ref, f_ref, own_sem, side_send, side_recv, far_send, far_recv, rep_send, rep_recv,
    tok_send, tok_recv, head_send, head_recv,
):
    rep = lax.axis_index("rep")
    me = lax.axis_index("seq")
    chips = count // 2
    chip, core = me // 2, me % 2
    rows = w_ref.shape[0]
    part = rows // reps
    full = w_ref.shape[1] // 3
    cols = wc_ref.shape[1] // 3
    tokens = x_ref.shape[0]
    place = me % 4
    sibling = chip * 2 + 1 - core
    far_ids = [((chip + k) % chips) * 2 + e for k in range(1, chips) for e in range(2)]
    rep_ids = [(rep + k) % reps for k in range(1, reps)]
    at = lambda r, s: (r, s)
    meet([at(rep, s) for s in far_ids + [sibling]] + [at(r, me) for r in rep_ids])

    def source(first, size, who, t):
        left = pl.multiple_of(t * full + (who % 4) * cols, LANES)
        return w_ref.at[pl.ds(first, size), pl.ds(left, cols)]

    def target(first, size, t):
        return wc_ref.at[pl.ds(first, size), pl.ds(t * cols, cols)]

    def spot(who, r):
        return pl.multiple_of(who * rows + r * part, 16)

    def token_rows(who, half):
        return f_ref.at[pl.ds(pl.multiple_of(EDGE + (who % 4) * tokens + half * (tokens // 2), 16), tokens // 2), :]

    waits = []
    quarter = pl.multiple_of(rep * part, 16)
    for n, who in enumerate(far_ids):
        for t in range(3):
            copy = send(
                source(quarter, part, who, t), target(spot(me, rep), part, t), far_send.at[n, t], far_recv.at[me, t],
                at(rep, who),
            )
            copy.start()
            waits.append(copy)
    for t in range(3):
        copy = send(
            source(0, rows, sibling, t), target(spot(me, 0), rows, t), side_send.at[t], side_recv.at[t], at(rep, sibling)
        )
        copy.start()
        waits.append(copy)
    local = [
        pltpu.make_async_copy(source(0, rows, me, t), target(spot(me, 0), rows, t), own_sem.at[t]) for t in range(3)
    ]
    lead = EDGE - HEADER
    local.append(pltpu.make_async_copy(z_ref.at[pl.ds(0, lead), :], f_ref.at[pl.ds(0, lead), :], own_sem.at[4]))
    local.append(
        pltpu.make_async_copy(z_ref, f_ref.at[pl.ds(f_ref.shape[0] - EDGE, EDGE), :], own_sem.at[5])
    )
    local.append(pltpu.make_async_copy(
        x_ref, f_ref.at[pl.ds(pl.multiple_of(EDGE + place * tokens, 16), tokens), :], own_sem.at[3]
    ))
    for copy in local:
        copy.start()
    def send_tokens():
        partner = (chip ^ 1) * 2 + core
        for half in range(2):
            mine = x_ref.at[pl.ds(half * (tokens // 2), tokens // 2), :]
            copy = send(mine, token_rows(me, half), tok_send.at[0, half], tok_recv.at[0, half], at(rep, partner))
            copy.start()
            waits.append(copy)
            copy = send(mine, token_rows(me, half), tok_send.at[1, half], tok_recv.at[1, half], at(rep, sibling))
            copy.start()
            waits.append(copy)

    head = f_ref.at[pl.ds(lead, HEADER), :]
    fill = pltpu.make_async_copy(z_ref.at[pl.ds(0, HEADER), :], head, own_sem.at[6])
    sends_on = (place == 3) & (me < count - 4)
    after = [
        send(x_ref.at[pl.ds(tokens - HEADER, HEADER), :], head, head_send.at[v], head_recv.at[0],
             at(rep, lax.rem(me + 1 + v, count)))
        for v in range(4)
    ]
    partner = (chip ^ 1) * 2 + core
    for n, who in enumerate(far_ids):
        if n == min(TOKENS_AFTER, len(far_ids) - 1):
            send_tokens()

            @pl.when(sends_on)
            def _():
                for copy in after:
                    copy.start()

            @pl.when(me < 4)
            def _():
                fill.start()

        for t in range(3):
            got = target(spot(who, rep), part, t)
            send(got, got, far_send.at[n, t], far_recv.at[who, t], at(rep, who)).wait_recv()
        block = wc_ref.at[pl.ds(spot(who, rep), part), :]
        for m, r in enumerate(rep_ids):
            copy = send(block, block, rep_send.at[n, m], rep_recv.at[n, m], at(r, me))
            copy.start()
            waits.append(copy)
    for half in range(2):
        got = token_rows(partner, half)
        send(got, got, tok_send.at[0, half], tok_recv.at[0, half], at(rep, partner)).wait_recv()
        copy = send(got, got, tok_send.at[2, half], tok_recv.at[2, half], at(rep, sibling))
        copy.start()
        waits.append(copy)
    for copy in local:
        copy.wait()

    @pl.when(me < 4)
    def _():
        fill.wait()

    @pl.when(me >= 4)
    def _():
        after[0].wait_recv()

    @pl.when(sends_on)
    def _():
        for copy in after:
            copy.wait_send()

    for t in range(3):
        got = target(spot(sibling, 0), rows, t)
        send(got, got, side_send.at[t], side_recv.at[t], at(rep, sibling)).wait_recv()
    for half in range(2):
        for kind, who in ((1, sibling), (2, partner ^ 1)):
            got = token_rows(who, half)
            send(got, got, tok_send.at[kind, half], tok_recv.at[kind, half], at(rep, sibling)).wait_recv()
    for n, who in enumerate(far_ids):
        for m in range(reps - 1):
            block = wc_ref.at[pl.ds(spot(who, (rep + reps - 1 - m) % reps), part), :]
            send(block, block, rep_send.at[n, m], rep_recv.at[n, m], at(rep_ids[m], me)).wait_recv()
    for copy in waits:
        copy.wait_send()


def gather_weight(weight, tokens, reps, count):
    rows, full = weight.shape
    own = full // 4
    far = count - 2
    dma = pltpu.SemaphoreType.DMA
    return pl.pallas_call(
        functools.partial(gather_kernel, reps, count),
        in_specs=[pl.BlockSpec(memory_space=pl.ANY)] * 3,
        out_specs=[pl.BlockSpec(memory_space=pl.ANY)] * 2,
        out_shape=[
            jax.ShapeDtypeStruct((rows * count, own), weight.dtype),
            jax.ShapeDtypeStruct((tokens.shape[0] * 4 + 2 * EDGE, tokens.shape[1]), tokens.dtype),
        ],
        scratch_shapes=[
            dma((7,)), dma((3,)), dma((3,)), dma((far, 3)), dma((count, 3)), dma((far, reps - 1)), dma((far, reps - 1)),
            dma((3, 2)), dma((3, 2)), dma((4,)), dma((1,)),
        ],
        cost_estimate=pl.CostEstimate(flops=2_000_000_000, bytes_accessed=20_000_000, transcendentals=0),
        compiler_params=pltpu.CompilerParams(collective_id=1, has_side_effects=True),
        name="gather_weight",
    )(weight, tokens, jnp.zeros((EDGE, tokens.shape[1]), tokens.dtype))


def frame_gather_kernel(x_ref, f_ref, own_sem, send_sem, recv_sem):
    rep = lax.axis_index("rep")
    me = lax.axis_index("seq")
    chip, core = me // 2, me % 2
    half_rows = x_ref.shape[0] // 2
    sibling = (rep, chip * 2 + 1 - core)
    partner = (rep, (chip ^ 1) * 2 + core)
    meet([sibling, partner])

    def rows(who, half):
        return f_ref.at[pl.ds(pl.multiple_of((who % 4) * 2 * half_rows + half * half_rows, 16), half_rows), :]

    waits = []

    def push(src, dst, kind, half, peer):
        copy = send(src, dst, send_sem.at[kind, half], recv_sem.at[kind, half], peer)
        copy.start()
        waits.append(copy)

    for half in range(2):
        push(x_ref.at[pl.ds(half * half_rows, half_rows), :], rows(me, half), 0, half, partner)
    for half in range(2):
        push(x_ref.at[pl.ds(half * half_rows, half_rows), :], rows(me, half), 1, half, sibling)
    local = pltpu.make_async_copy(
        x_ref, f_ref.at[pl.ds(pl.multiple_of((me % 4) * 2 * half_rows, 16), 2 * half_rows), :], own_sem.at[0]
    )
    local.start()

    def arrived(kind, half, who):
        got = rows(who, half)
        send(got, got, send_sem.at[kind, half], recv_sem.at[kind, half], sibling).wait_recv()
        return got

    for half in range(2):
        got = arrived(0, half, partner[1])
        push(got, got, 2, half, sibling)
    local.wait()
    for half in range(2):
        arrived(1, half, sibling[1])
        arrived(2, half, partner[1] ^ 1)
    for copy in waits:
        copy.wait_send()


def frame_gather(values):
    dma = pltpu.SemaphoreType.DMA
    return pl.pallas_call(
        frame_gather_kernel,
        in_specs=[pl.BlockSpec(memory_space=pl.ANY)],
        out_specs=pl.BlockSpec(memory_space=pl.ANY),
        out_shape=jax.ShapeDtypeStruct((values.shape[0] * 4, values.shape[1]), values.dtype),
        scratch_shapes=[dma((1,)), dma((3, 2)), dma((3, 2))],
        cost_estimate=pl.CostEstimate(flops=2_000_000_000, bytes_accessed=8_000_000, transcendentals=0),
        compiler_params=pltpu.CompilerParams(collective_id=2, has_side_effects=True),
        name="frame_gather",
    )(values)


def frame_swap_kernel(h_ref, r_ref, own_sem, send_sem, recv_sem):
    rep = lax.axis_index("rep")
    me = lax.axis_index("seq")
    base, place = me // 4 * 4, me % 4
    rows = r_ref.shape[0]
    cols = h_ref.shape[1]
    peers = [base + (place ^ n) for n in (2, 3, 1)]
    meet([(rep, who) for who in peers])

    def block(who):
        return h_ref.at[pl.ds(pl.multiple_of((who % 4) * rows, 16), rows), :]

    def spot(who):
        return r_ref.at[:, pl.ds(pl.multiple_of((who % 4) * cols, LANES), cols)]

    copies = [
        send(block(who), spot(me), send_sem.at[n], recv_sem.at[n], (rep, who)) for n, who in enumerate(peers)
    ]
    for copy in copies:
        copy.start()
    local = pltpu.make_async_copy(block(me), spot(me), own_sem.at[0])
    local.start()
    local.wait()
    for n, who in enumerate(peers):
        send(block(who), spot(who), send_sem.at[n], recv_sem.at[n], (rep, who)).wait_recv()
    for copy in copies:
        copy.wait_send()


def frame_swap(values):
    dma = pltpu.SemaphoreType.DMA
    return pl.pallas_call(
        frame_swap_kernel,
        in_specs=[pl.BlockSpec(memory_space=pl.ANY)],
        out_specs=pl.BlockSpec(memory_space=pl.ANY),
        out_shape=jax.ShapeDtypeStruct((values.shape[0] // 4, values.shape[1] * 4), values.dtype),
        scratch_shapes=[dma((1,)), dma((3,)), dma((3,))],
        cost_estimate=pl.CostEstimate(flops=2_000_000_000, bytes_accessed=2_000_000, transcendentals=0),
        compiler_params=pltpu.CompilerParams(collective_id=3, has_side_effects=True),
        name="frame_swap",
    )(values)


def reduce_kernel(
    reps, count, gi_ref, go_ref, dn_ref, xs_ref, sv_ref, oi_ref, oo_ref, od_ref, so_ref,
    li_ref, ri_ref, rb_ref, zi_ref, qi_ref, lo_ref, ro_ref, rc_ref, zo_ref, qo_ref, ld_ref, bd_ref, hd_ref,
    load_sem, one_send, one_recv, on_send, on_recv, near_send, near_recv, past_send, past_recv, two_send, two_recv, three_send, three_recv, tok_send, tok_recv,
    head_send, head_recv, vec_ref, one_ref, two_ref, sum_ref, small_one, small_got, small_two, small_end,
):
    rep = lax.axis_index("rep")
    me = lax.axis_index("seq")
    chip, core = me // 2, me % 2
    base, place = me // 4 * 4, me % 4
    sibling = chip * 2 + 1 - core
    partner = (chip ^ 1) * 2 + core
    rep_ids = [(rep + k) % reps for k in range(1, reps)]
    seq_ids = [(me + k) % count for k in range(1, count)]
    part = li_ref.shape[2]
    rows = part * reps
    halves = lo_ref.shape[0]
    frames = count // 4
    cols = gi_ref.shape[1] // 3
    width = cols * 4
    tokens = od_ref.shape[0]
    meet([(r, me) for r in rep_ids] + [(rep, s) for s in seq_ids])
    waits = []

    def push(src, dst, send_sem, recv_sem, peer):
        copy = send(src, dst, send_sem, recv_sem, peer)
        copy.start()
        waits.append(copy)

    def arrived(dst, send_sem, recv_sem):
        send(dst, dst, send_sem, recv_sem, (rep, sibling)).wait_recv()

    def quarter(ref, who, r):
        return ref.at[pl.ds(pl.multiple_of(who * rows + r * part, 16), part), :]

    def token_rows(who):
        return dn_ref.at[pl.ds(pl.multiple_of(EDGE + (who % 4) * tokens, 16), tokens), :]

    ahead = send(
        dn_ref.at[pl.ds(EDGE - HEADER, HEADER), :], hd_ref.at[place], head_send.at[0], head_recv.at[place],
        (rep, lax.rem(base + count - 1, count)),
    )

    @pl.when(me >= 4)
    def _():
        ahead.start()

    push(token_rows(partner ^ 1), bd_ref.at[0], tok_send.at[0], tok_recv.at[0], (rep, sibling))
    push(token_rows(sibling), bd_ref.at[1], tok_send.at[1], tok_recv.at[1], (rep, sibling))
    loads = [
        pltpu.make_async_copy(token_rows(partner), ld_ref.at[0], load_sem.at[0]),
        pltpu.make_async_copy(token_rows(me), ld_ref.at[1], load_sem.at[1]),
    ]
    for copy in loads:
        copy.start()
    order = seq_ids + [me]
    near = [rep ^ 1, rep ^ 2]
    past = [rep ^ 2, rep ^ 1]
    blocks = [(go_ref, h, lo_ref.at[h], ro_ref.at[h], rc_ref.at[h]) for h in range(halves)]
    blocks += [(gi_ref, who, li_ref.at[n], ri_ref.at[n], rb_ref.at[n]) for n, who in enumerate(order)]
    for n, (grad, row, _, got, _) in enumerate(blocks):
        for m, r in enumerate((near[n % 2], rep ^ 3)):
            push(quarter(grad, row, r), got.at[m], one_send.at[n, m], one_recv.at[n, m], (near[n % 2], me))
    own = [
        pltpu.make_async_copy(quarter(grad, row, r), held.at[m], load_sem.at[2 + 2 * n + m])
        for n, (grad, row, held, _, _) in enumerate(blocks)
        for m, r in enumerate((rep, past[n % 2]))
    ]
    for copy in own:
        copy.start()

    loads[0].wait()
    arrived(bd_ref.at[0], tok_send.at[0], tok_recv.at[0])
    wide = jnp.float32
    ld_ref[0] = (ld_ref[0].astype(wide) + bd_ref[0].astype(wide)).astype(jnp.bfloat16)
    push(ld_ref.at[0], bd_ref.at[2], tok_send.at[2], tok_recv.at[2], (rep, partner))

    def pass_on(n):
        _, _, held, got, last = blocks[n]
        own[2 * n + 1].wait()
        arrived(got.at[1], one_send.at[n, 1], one_recv.at[n, 1])
        held[1] = (held[1].astype(wide) + got[1].astype(wide)).astype(jnp.bfloat16)
        push(held.at[1], last, on_send.at[n], on_recv.at[n], (past[n % 2], me))

    def finish(n):
        _, _, held, got, last = blocks[n]
        own[2 * n].wait()
        arrived(got.at[0], one_send.at[n, 0], one_recv.at[n, 0])
        arrived(last, on_send.at[n], on_recv.at[n])
        held[0] = (held[0].astype(wide) + got[0].astype(wide) + last[...].astype(wide)).astype(jnp.bfloat16)
        if n < halves:
            owner = place * halves + n

            @pl.when(owner == me)
            def _():
                zo_ref[me // 4] = lo_ref[n, 0]

            @pl.when(owner != me)
            def _():
                shipped(n).start()
        elif n < halves + count - 1:
            k = n - halves
            push(li_ref.at[k, 0], zi_ref.at[me], two_send.at[k], two_recv.at[me], (rep, order[k]))
        else:
            zi_ref[me] = li_ref[count - 1, 0]

    def shipped(h):
        return send(
            lo_ref.at[h, 0], zo_ref.at[me // 4], two_send.at[count + h], two_recv.at[count + me // 4],
            (rep, place * halves + h),
        )

    for n in range(len(blocks) + 2):
        if n < len(blocks):
            pass_on(n)
        if n >= 2:
            finish(n - 2)

    loads[1].wait()
    arrived(bd_ref.at[1], tok_send.at[1], tok_recv.at[1])
    arrived(bd_ref.at[2], tok_send.at[2], tok_recv.at[2])
    od_ref[...] = ld_ref[1].astype(wide) + bd_ref[1].astype(wide) + bd_ref[2].astype(wide)

    @pl.when((place == 3) & (me < count - 4))
    def _():
        total = od_ref[tokens - HEADER :, :]
        for v in range(4):
            arrived(hd_ref.at[v], head_send.at[0], head_recv.at[v])
            total = total + hd_ref[v].astype(wide)
        od_ref[tokens - HEADER :, :] = total

    @pl.when(me >= 4)
    def _():
        ahead.wait_send()

    gain_rows = width // LANES
    first = jnp.sum(od_ref[...] * xs_ref[...], axis=0, keepdims=True)
    vec_ref[...] = sv_ref[...]
    for k in range(gain_rows):
        vec_ref[k : k + 1, :] = first[:, k * LANES : (k + 1) * LANES]
    for m, r in enumerate(rep_ids):
        push(vec_ref, one_ref.at[rep], small_one.at[m], small_got.at[rep], (r, me))
    one_ref[rep] = vec_ref[...]

    for f in range(frames):
        source = f * 4 + me // halves

        @pl.when(source != me)
        def _():
            arrived(zo_ref.at[f], two_send.at[count], two_recv.at[count + f])

    total = zo_ref[0].astype(wide)
    for f in range(1, frames):
        total = total + zo_ref[f].astype(wide)
    qo_ref[...] = total.astype(jnp.bfloat16)
    for m, r in enumerate(rep_ids):
        push(qo_ref, oo_ref.at[pl.ds(pl.multiple_of(rep * part, 16), part), :], three_send.at[0, m], three_recv.at[0, m], (r, me))
    for m, r in enumerate(rep_ids):
        arrived(one_ref.at[r], small_one.at[m], small_got.at[r])
    total = one_ref[0]
    for r in range(1, reps):
        total = total + one_ref[r]
    sum_ref[...] = total
    two_ref[me] = total
    for m, s in enumerate(seq_ids):
        push(sum_ref, two_ref.at[me], small_two.at[m], small_end.at[me], (rep, s))
    for n, who in enumerate(seq_ids):
        arrived(zi_ref.at[who], two_send.at[n], two_recv.at[who])
    for u in range(4):
        total = zi_ref[u].astype(wide)
        for f in range(1, frames):
            total = total + zi_ref[f * 4 + u].astype(wide)
        for t in range(3):
            qi_ref[:, t * width + u * cols : t * width + (u + 1) * cols] = total[:, t * cols : (t + 1) * cols].astype(
                jnp.bfloat16
            )
    wing = 3 * width // 2

    def shard(r, k):
        return oi_ref.at[pl.ds(pl.multiple_of(r * part, 16), part), pl.ds(k * wing, wing)]

    for k in range(2):
        mine = qi_ref.at[:, pl.ds(k * wing, wing)]
        push(mine, shard(rep, k), near_send.at[k], near_recv.at[k], (near[k], me))
        push(mine, shard(rep, k), past_send.at[k, 0], past_recv.at[k, 0], (past[k], me))
    for k in range(2):
        got = shard(near[k], k)
        arrived(got, near_send.at[k], near_recv.at[k])
        push(got, got, past_send.at[k, 1], past_recv.at[k, 1], (past[k], me))
    final = [
        pltpu.make_async_copy(qo_ref, oo_ref.at[pl.ds(pl.multiple_of(rep * part, 16), part), :], load_sem.at[0]),
        pltpu.make_async_copy(qi_ref, oi_ref.at[pl.ds(pl.multiple_of(rep * part, 16), part), :], load_sem.at[1]),
    ]
    for copy in final:
        copy.start()
    for h in range(halves):
        owner = place * halves + h

        @pl.when(owner != me)
        def _():
            shipped(h).wait_send()

    for m, s in enumerate(seq_ids):
        arrived(two_ref.at[s], small_two.at[m], small_end.at[s])
    total = two_ref[0]
    for s in range(1, count):
        total = total + two_ref[s]
    so_ref[...] = total
    for copy in final:
        copy.wait()
    for m in range(reps - 1):
        r = (rep + reps - 1 - m) % reps
        arrived(oo_ref.at[pl.ds(pl.multiple_of(r * part, 16), part), :], three_send.at[0, m], three_recv.at[0, m])
    for k in range(2):
        arrived(shard(past[k], k), past_send.at[k, 0], past_recv.at[k, 0])
        arrived(shard(rep ^ 3, k), past_send.at[k, 1], past_recv.at[k, 1])
    for copy in waits:
        copy.wait_send()


def reduce_weights(grad_in, grad_out, tokens, scaled, small, reps, count):
    width = grad_out.shape[1]
    own = grad_in.shape[1]
    rows = width // count
    part = rows // reps
    halves = grad_out.shape[0] // rows
    frames = count // 4
    each = (tokens.shape[0] - 2 * EDGE) // 4
    dma = pltpu.SemaphoreType.DMA
    low = jnp.bfloat16
    hbm = pl.BlockSpec(memory_space=pl.ANY)
    vmem = pl.BlockSpec(memory_space=pltpu.VMEM)
    lines = small.shape[0]
    return pl.pallas_call(
        functools.partial(reduce_kernel, reps, count),
        in_specs=[hbm] * 3 + [vmem] * 2,
        out_specs=[hbm, hbm, vmem, vmem],
        out_shape=[
            jax.ShapeDtypeStruct((rows, 3 * width), low),
            jax.ShapeDtypeStruct((rows, width), low),
            jax.ShapeDtypeStruct((each, width), jnp.float32),
            jax.ShapeDtypeStruct((lines, LANES), jnp.float32),
        ],
        scratch_shapes=[
            pltpu.VMEM((count, 2, part, own), low), pltpu.VMEM((count, 2, part, own), low),
            pltpu.VMEM((count, part, own), low), pltpu.VMEM((count, part, own), low), pltpu.VMEM((part, 3 * width), low),
            pltpu.VMEM((halves, 2, part, width), low), pltpu.VMEM((halves, 2, part, width), low),
            pltpu.VMEM((halves, part, width), low),
            pltpu.VMEM((frames, part, width), low), pltpu.VMEM((part, width), low),
            pltpu.VMEM((2, each, width), low), pltpu.VMEM((3, each, width), low),
            pltpu.VMEM((4, HEADER, width), low),
            dma((2 + 2 * (count + halves),)), dma((count + halves, 2)), dma((count + halves, 2)), dma((count + halves,)),
            dma((count + halves,)),
            dma((2,)), dma((2,)), dma((2, 2)), dma((2, 2)),
            dma((count + halves,)), dma((count + frames,)), dma((1, reps - 1)), dma((1, reps - 1)), dma((3,)), dma((3,)),
            dma((1,)), dma((4,)),
            pltpu.VMEM((lines, LANES), jnp.float32), pltpu.VMEM((reps, lines, LANES), jnp.float32),
            pltpu.VMEM((count, lines, LANES), jnp.float32), pltpu.VMEM((lines, LANES), jnp.float32),
            dma((reps - 1,)), dma((reps,)), dma((count - 1,)), dma((count,)),
        ],
        cost_estimate=pl.CostEstimate(flops=2_000_000_000, bytes_accessed=20_000_000, transcendentals=0),
        compiler_params=pltpu.CompilerParams(collective_id=5, has_side_effects=True, vmem_limit_bytes=40 << 20),
        name="reduce_weights",
    )(grad_in, grad_out, tokens, scaled, small)


def rep_sum_kernel(
    g_refs, o_ref, held, got, last, load_sem, one_send, one_recv, on_send, on_recv
):
    rep = lax.axis_index("rep")
    me = lax.axis_index("seq")
    near = [rep ^ 1, rep ^ 2]
    past = [rep ^ 2, rep ^ 1]
    meet([(r, me) for r in near])
    waits = []

    def push(src, dst, send_sem, recv_sem, peer):
        copy = send(src, dst, send_sem, recv_sem, peer)
        copy.start()
        waits.append(copy)

    def arrived(dst, send_sem, recv_sem):
        send(dst, dst, send_sem, recv_sem, (near[0], me)).wait_recv()

    blocks = [(k, s) for k in range(3) for s in range(2)]

    def rows(n, r):
        k, s = blocks[n]
        size = last[k].shape[1]
        return g_refs[k].at[pl.ds(pl.multiple_of(r * 2 * size + s * size, 16), size), :]

    for n, (k, s) in enumerate(blocks):
        for m, r in enumerate((near[s], rep ^ 3)):
            push(rows(n, r), got[k].at[s, m], one_send.at[n, m], one_recv.at[n, m], (near[s], me))
    own = [
        pltpu.make_async_copy(rows(n, r), held[k].at[s, m], load_sem.at[2 * n + m])
        for n, (k, s) in enumerate(blocks)
        for m, r in enumerate((rep, past[s]))
    ]
    for copy in own:
        copy.start()
    wide = jnp.float32
    for n in range(len(blocks) + 2):
        if n < len(blocks):
            k, s = blocks[n]
            own[2 * n + 1].wait()
            arrived(got[k].at[s, 1], one_send.at[n, 1], one_recv.at[n, 1])
            held[k][s, 1] = (held[k][s, 1].astype(wide) + got[k][s, 1].astype(wide)).astype(jnp.bfloat16)
            push(held[k].at[s, 1], last[k].at[s], on_send.at[n], on_recv.at[n], (past[s], me))
        if n >= 2:
            k, s = blocks[n - 2]
            size = last[k].shape[1]
            own[2 * n - 4].wait()
            arrived(got[k].at[s, 0], one_send.at[n - 2, 0], one_recv.at[n - 2, 0])
            arrived(last[k].at[s], on_send.at[n - 2], on_recv.at[n - 2])
            total = held[k][s, 0].astype(wide) + got[k][s, 0].astype(wide) + last[k][s].astype(wide)
            total = total.astype(jnp.bfloat16)
            lanes = last[0].shape[2]
            if k < 2:
                o_ref[s * size : (s + 1) * size, k * lanes : (k + 1) * lanes] = total
            else:
                for j in range(total.shape[1] // lanes):
                    first = (2 * j + s) * size
                    o_ref[first : first + size, 2 * lanes :] = total[:, j * lanes : (j + 1) * lanes]
    for copy in waits:
        copy.wait_send()


def rep_sum(arrays):
    dma = pltpu.SemaphoreType.DMA
    shapes = [(value.shape[0] // 4, value.shape[1]) for value in arrays]
    low = jnp.bfloat16

    def body(*refs):
        rep_sum_kernel(refs[:3], refs[3], refs[4:7], refs[7:10], refs[10:13], *refs[13:])

    return pl.pallas_call(
        body,
        in_specs=[pl.BlockSpec(memory_space=pl.ANY)] * 3,
        out_specs=pl.BlockSpec(memory_space=pltpu.VMEM),
        out_shape=jax.ShapeDtypeStruct((shapes[0][0], 3 * shapes[0][1]), low),
        scratch_shapes=[pltpu.VMEM((2, 2, rows // 2, cols), low) for rows, cols in shapes]
        + [pltpu.VMEM((2, 2, rows // 2, cols), low) for rows, cols in shapes]
        + [pltpu.VMEM((2, rows // 2, cols), low) for rows, cols in shapes]
        + [dma((12,)), dma((6, 2)), dma((6, 2)), dma((6,)), dma((6,))],
        cost_estimate=pl.CostEstimate(flops=2_000_000_000, bytes_accessed=20_000_000, transcendentals=0),
        compiler_params=pltpu.CompilerParams(collective_id=6, has_side_effects=True, vmem_limit_bytes=32 << 20),
        name="rep_sum",
    )(*arrays)


def rms_scale(values):
    return lax.rsqrt(jnp.mean(values * values, axis=-1, keepdims=True) + EPS)


def norm_back(grad_out, values, inv_scale, gain):
    scaled_grad = grad_out * gain
    inner = jnp.mean(scaled_grad * values, axis=-1, keepdims=True)
    return inv_scale * scaled_grad - values * inv_scale**3 * inner


def pad_heads(values, dim):
    shaped = values.reshape(values.shape[:-1] + (-1, dim))
    shaped = jnp.pad(shaped, [(0, 0)] * (shaped.ndim - 1) + [(0, LANES - dim)])
    return shaped.reshape(values.shape[:-1] + (-1,))


def cut_heads(values, dim):
    shaped = values.reshape(values.shape[:-1] + (-1, LANES))[..., :dim]
    return shaped.reshape(values.shape[:-1] + (-1,))


def on_device(
    inputs, segment_ids, valid_mask, input_weight, output_weight, conv_kernel, head_mix, first_gain, second_gain,
    group_gain, gate_weight, up_weight, down_weight, cotangent,
):
    tokens, width = inputs.shape[1:]
    heads, taps, span = conv_kernel.shape
    dim = width // heads
    scale = dim ** (-0.5)
    count = lax.axis_size("seq")
    team = FRAME // tokens
    own_heads = heads // team
    own_width = own_heads * dim
    own_pairs = own_heads // 2
    groups = [[g * team + i for i in range(team)] for g in range(count // team)]
    seq_rank = lax.axis_index("seq")
    place = seq_rank % team
    frame_first = (seq_rank // team) * FRAME
    row_first = seq_rank * tokens
    contract_rows = (((0,), (0,)), ((), ()))

    resid_in = inputs[0].astype(jnp.float32)
    grad_out = cotangent[0].astype(jnp.float32)
    row_valid = lax.dynamic_slice_in_dim(valid_mask[0], row_first, tokens).astype(jnp.float32)[:, None]
    ahead = lambda values: jnp.pad(values, (HEADER, 0))
    codes = make_codes(
        lax.dynamic_slice_in_dim(ahead(segment_ids[0]), frame_first, FRAME + HEADER),
        lax.dynamic_slice_in_dim(ahead(valid_mask[0]), frame_first, FRAME + HEADER),
    )
    own_kernel = lax.dynamic_slice_in_dim(conv_kernel, place * own_heads, own_heads)
    own_mix = lax.dynamic_slice_in_dim(head_mix, place * own_pairs, own_pairs).reshape(own_pairs, 4)
    own_gain = pad_heads(lax.dynamic_slice_in_dim(group_gain, place * own_width, own_width)[None], dim)
    toep, toep_split = split_toeplitz(toeplitz(own_kernel, scale))

    reps = lax.axis_size("rep")
    direct = team == 4 and reps == 4 and down_weight.shape[0] * 3 == width and (width // count) % (16 * reps) == 0
    first_scale = rms_scale(resid_in)
    normed_in = (resid_in * first_scale * first_gain).astype(jnp.bfloat16)
    if direct:
        own_input, normed_frame = gather_weight(input_weight, normed_in, reps, count)
    else:
        full_input = lax.all_gather(input_weight, "seq", axis=0, tiled=True)
        own_input = lax.dynamic_slice_in_dim(full_input.reshape(width, 3, width), place * own_width, own_width, axis=2)
        own_input = own_input.reshape(width, 3 * own_width)
        normed_frame = lax.all_gather(normed_in, "seq", axis=0, tiled=True, axis_index_groups=groups)
        ends = lax.all_gather(normed_in[tokens - HEADER :], "seq", axis=0)
        last = jnp.maximum(seq_rank // team * team - 1, 0)
        end = jnp.where(frame_first > 0, lax.dynamic_index_in_dim(ends, last, keepdims=False), 0)
        lead = jnp.zeros((EDGE - HEADER, width), jnp.bfloat16)
        normed_frame = jnp.concatenate([lead, end, normed_frame, jnp.zeros((EDGE, width), jnp.bfloat16)], axis=0)
    dmlp = (row_valid * grad_out).astype(jnp.bfloat16)
    own_input, output_weight, dmlp = lax.optimization_barrier((own_input, output_weight, dmlp))
    full_output = lax.all_gather(output_weight, "seq", axis=0, tiled=True)
    proj = jnp.dot(normed_frame, own_input, preferred_element_type=jnp.float32).astype(jnp.bfloat16)
    dmlp_all = lax.all_gather(dmlp, "seq", axis=0, tiled=True)
    normed_own, att, prob = attention_forward(proj, toep_split, codes, own_gain, own_mix, dim, taps)
    normed_own, full_output = lax.optimization_barrier((normed_own, full_output))

    def to_rows(values):
        moved = lax.all_to_all(
            values.reshape(team, tokens, own_width), "seq", 0, 0, tiled=True, axis_index_groups=groups
        )
        return moved.transpose(1, 0, 2).reshape(tokens, width)

    normed = frame_swap(normed_own) if direct else to_rows(normed_own)
    branch = jnp.dot(normed, full_output, preferred_element_type=jnp.float32)
    resid = resid_in + row_valid * branch
    second_scale = rms_scale(resid)
    normed_mid = (resid * second_scale * second_gain).astype(jnp.bfloat16)
    normed_mid, dmlp_all = lax.optimization_barrier((normed_mid, dmlp_all))
    inputs_all = lax.all_gather(normed_mid, "seq", axis=0, tiled=True)
    gate = jnp.dot(inputs_all, gate_weight, preferred_element_type=jnp.float32)
    up_proj = jnp.dot(inputs_all, up_weight, preferred_element_type=jnp.float32)
    dhidden = jnp.dot(dmlp_all, down_weight.T, preferred_element_type=jnp.float32)
    sigmoid_gate = jax.nn.sigmoid(gate)
    gate_grad = (dhidden * up_proj * sigmoid_gate * (1.0 + gate * (1.0 - sigmoid_gate))).astype(jnp.bfloat16)
    up_grad = (dhidden * gate * sigmoid_gate).astype(jnp.bfloat16)
    hidden = (jax.nn.silu(gate) * up_proj).astype(jnp.bfloat16)
    dmid_part = (
        jnp.dot(gate_grad, gate_weight.T, preferred_element_type=jnp.float32)
        + jnp.dot(up_grad, up_weight.T, preferred_element_type=jnp.float32)
    ).astype(jnp.bfloat16)
    gate_grad, up_grad, hidden, dmid_part = lax.optimization_barrier((gate_grad, up_grad, hidden, dmid_part))
    dmid_low = lax.psum_scatter(dmid_part, "seq", scatter_dimension=0, tiled=True)
    mlp_part = jnp.dot(hidden, down_weight, preferred_element_type=jnp.float32).astype(jnp.bfloat16)
    mlp_grads = [
        lax.dot_general(left, right, contract_rows, preferred_element_type=jnp.float32).astype(jnp.bfloat16)
        for left, right in ((inputs_all, gate_grad), (inputs_all, up_grad), (hidden, dmlp_all))
    ]
    if direct:
        mlp_grads = rep_sum(mlp_grads)
    dmid_low, mlp_part, mlp_grads = lax.optimization_barrier((dmid_low, mlp_part, mlp_grads))
    mlp_low = lax.psum_scatter(mlp_part, "seq", scatter_dimension=0, tiled=True)
    if direct:
        packed = lax.all_gather(mlp_grads, "rep", axis=0)
    else:
        mlp_grads = [lax.psum(value, "rep") for value in mlp_grads]
    dmid = dmid_low.astype(jnp.float32)
    second_part = jnp.sum(dmid * resid * second_scale, axis=0)
    dresid = grad_out + norm_back(dmid, resid, second_scale, second_gain)
    dbranch = (row_valid * dresid).astype(jnp.bfloat16)
    if direct:
        dbranch_frame = frame_gather(dbranch)
    else:
        dbranch_frame = lax.all_gather(dbranch, "seq", axis=0, tiled=True, axis_index_groups=groups)
    own_output = lax.dynamic_slice_in_dim(full_output, place * own_width, own_width, axis=0)
    dnormed_own = lax.dot_general(dbranch_frame, own_output, NT, preferred_element_type=jnp.float32)
    own_output_grad = lax.dot_general(normed_own, dbranch_frame, contract_rows, preferred_element_type=jnp.float32)
    own_output_grad = own_output_grad.astype(jnp.bfloat16)
    dproj, dtoep, dmix, dgain = attention_backward(
        proj, toep, codes, prob, att, dnormed_own, own_gain, own_mix, dim, taps, span
    )
    own_input_grad = lax.dot_general(normed_frame, dproj, contract_rows, preferred_element_type=jnp.float32)
    own_input_grad = own_input_grad.astype(jnp.bfloat16)
    dnormin_part = lax.dot_general(dproj, own_input, NT, preferred_element_type=jnp.float32).astype(jnp.bfloat16)
    def spread(values, size):
        empty = jnp.zeros((size,) + values.shape[1:], jnp.float32)
        return lax.dynamic_update_slice_in_dim(empty, values, place * values.shape[0], 0)

    kernel_part = spread(tap_grads(dtoep, taps, span, scale), heads)
    mix_part = spread(jnp.sum(dmix[:, :4], axis=-1).reshape(own_pairs, 2, 2), heads // 2)
    group_part = spread(cut_heads(dgain, dim)[0], width)
    parts = (kernel_part, mix_part, second_part, group_part)
    if direct:
        flat = jnp.concatenate([jnp.zeros((width,), jnp.float32)] + [value.reshape(-1) for value in parts])
        size = -(-flat.shape[0] // (8 * LANES)) * 8 * LANES
        small = jnp.pad(flat, (0, size - flat.shape[0])).reshape(-1, LANES)
        grad_input_w, grad_output_w, dnormin, small = reduce_weights(
            own_input_grad, own_output_grad, dnormin_part, resid_in * first_scale, small, reps, count
        )
        flat = small.reshape(-1)
        grad_first, others, start = flat[:width], [], width
        for value in parts:
            others.append(flat[start : start + value.size].reshape(value.shape))
            start += value.size
    else:
        dnormin = lax.psum_scatter(
            dnormin_part[EDGE : EDGE + FRAME], "seq", scatter_dimension=0, tiled=True, axis_index_groups=groups
        ).astype(jnp.float32)
        starts = lax.all_gather(dnormin_part[EDGE - HEADER : EDGE], "seq", axis=0).astype(jnp.float32)
        later = lax.dynamic_slice_in_dim(
            jnp.pad(starts, ((0, team), (0, 0), (0, 0))), (seq_rank // team + 1) * team, team
        ).sum(axis=0)
        later = jnp.where(place == team - 1, later, 0.0)
        dnormin = dnormin + jnp.pad(later, ((tokens - HEADER, 0), (0, 0)))
        pieces = lax.all_to_all(own_input_grad.reshape(count, width // count, 3 * own_width), "seq", 0, 0, tiled=True)
        pieces = pieces.reshape(count // team, team, width // count, 3, own_width).astype(jnp.float32).sum(axis=0)
        grad_input_w = pieces.transpose(1, 2, 0, 3).reshape(width // count, 3 * width)
        spots = jnp.zeros((width, width), jnp.bfloat16)
        spots = lax.dynamic_update_slice_in_dim(spots, own_output_grad, place * own_width, 0)
        grad_output_w = lax.psum_scatter(spots, "seq", scatter_dimension=0, tiled=True)
        grad_input_w, grad_output_w = [
            lax.psum(value.astype(jnp.bfloat16), "rep") for value in (grad_input_w, grad_output_w)
        ]
    dnormin, mlp_low, mlp_sums = lax.optimization_barrier((dnormin, mlp_low, packed if direct else mlp_grads))
    if direct:
        packed = mlp_sums
    else:
        mlp_grads = mlp_sums
    result = resid + row_valid * mlp_low.astype(jnp.float32)
    if not direct:
        first_part = jnp.sum(dnormin * resid_in * first_scale, axis=0)
        grad_first, others = lax.psum((first_part, parts), ("rep", "seq"))
    grad_in = dresid + norm_back(dnormin, resid_in, first_scale, first_gain)

    grad_kernel, grad_mix, grad_second, grad_group = others
    if direct:
        units = down_weight.shape[0]
        mlp_grads = [
            packed[:, :, :units].reshape(width, units),
            packed[:, :, units : 2 * units].reshape(width, units),
            packed[:, :, 2 * units :].reshape(reps, 3, units // reps, units).transpose(0, 2, 1, 3).reshape(units, width),
        ]
    grads = [value.astype(jnp.float32) for value in (grad_input_w, grad_output_w, *mlp_grads)]
    return (
        result.astype(jnp.bfloat16)[None], grad_in.astype(jnp.bfloat16)[None], grads[0], grads[1], grad_kernel,
        grad_mix, grad_first, grad_second, grad_group, grads[2], grads[3], grads[4],
    )


def solution(mesh):
    in_specs = (
        P("rep", "seq", None), P("rep", None), P("rep", None), P("seq", None), P("seq", None), P(), P(), P(), P(), P(),
        P(None, "seq"), P(None, "seq"), P("seq", None), P("rep", "seq", None),
    )
    out_specs = (
        P("rep", "seq", None), P("rep", "seq", None), P("seq", None), P("seq", None), P(), P(), P(), P(), P(),
        P(None, "seq"), P(None, "seq"), P("seq", None),
    )
    return jax.shard_map(on_device, mesh=mesh, in_specs=in_specs, out_specs=out_specs, check_vma=False)
```

```python
import functools
import jax
import jax.numpy as jnp
from jax import lax
from jax.experimental import pallas as pl
from jax.experimental.pallas import tpu as pltpu
from jax.sharding import PartitionSpec as P

FRAME = 1024


EPS = 1e-06
LANES = 128
ROWS = 256
EDGE = 64
HEADER = 16
NEG = -1e30
PROB = jnp.float32

NT = (((1,), (1,)), ((), ()))
NN = (((1,), (0,)), ((), ()))


def dot(a, b, dims=NN):
    return lax.dot_general(a, b, dims, preferred_element_type=jnp.float32)


def toeplitz(kernel, scale):
    heads, taps, span = kernel.shape
    shape = (heads, 2 * LANES, taps * LANES)
    lane = lax.broadcasted_iota(jnp.int32, shape, 2)
    tap = lax.broadcasted_iota(jnp.int32, shape, 1)
    diff = lane % LANES + EDGE + span // 2 - tap
    total = jnp.zeros(shape, jnp.float32)
    for b in range(span):
        weight = jnp.repeat(kernel[:, :, b] * scale, LANES, axis=1)[:, None, :]
        total = total + jnp.where(diff == b, weight, 0.0)
    return total


def split_toeplitz(full):
    kept = lax.reduce_precision(full, exponent_bits=8, mantissa_bits=7)
    high = kept.astype(jnp.bfloat16)
    low = (full - kept).astype(jnp.bfloat16)
    return high, jnp.concatenate([high, high, low], axis=1)


def tap_grads(sums, taps, span, scale):
    shaped = sums.reshape(sums.shape[0], 16, taps, LANES).sum(axis=-1)
    return shaped[:, :span].transpose(0, 2, 1) * scale


def lane_mask(dim):
    return lax.broadcasted_iota(jnp.int32, (ROWS, LANES), 1) < dim


def group_stats(att, dim):
    mean = jnp.sum(att, axis=-1, keepdims=True) / dim
    centred = jnp.where(lane_mask(dim), att - mean, 0.0)
    var = jnp.sum(centred * centred, axis=-1, keepdims=True) / dim
    inv = lax.rsqrt(var + EPS)
    return centred * inv, inv


def widen(sources, targets, dim, pairs):
    pair = pl.program_id(0)
    for source, target in zip(sources, targets):
        for h in range(2):
            target[:, h * LANES + dim : (h + 1) * LANES] = jnp.zeros((target.shape[0], LANES - dim), target.dtype)
        for p in range(pairs):

            @pl.when(pair == p)
            def _():
                for h in range(2):
                    left = (2 * p + h) * dim
                    target[:, h * LANES : h * LANES + dim] = source[:, left : left + dim]


def place_head(target, rows, left, h, value, dim, pairs):
    pair = pl.program_id(0)
    for p in range(pairs):

        @pl.when(pair == p)
        def _():
            at = left + (2 * p + h) * dim
            target[rows, at : at + dim] = value[:, :dim].astype(target.dtype)


def forward_kernel(
    dim, taps, pairs, qs_ref, ks_ref, vs_ref, t_ref, rowc_ref, colp_ref, colc_ref, gain_ref, mix_ref,
    normed_ref, att_ref, prob_ref, lm_ref, lo_ref, p_ref, cv_ref, mx_ref, sm_ref, acc_ref, q_ref, k_ref, v_ref,
):
    step = pl.program_id(1)

    @pl.when(step == 0)
    def _():
        widen((qs_ref, ks_ref, vs_ref), (q_ref, k_ref, v_ref), dim, pairs)

    first = step * ROWS
    top = pl.multiple_of(first + EDGE - HEADER, 16)
    tall = ROWS + HEADER
    codes = rowc_ref[pl.ds(top, tall), :]
    ipos = first - HEADER + lax.broadcasted_iota(jnp.int32, (tall, LANES), 0)
    lane = lax.broadcasted_iota(jnp.int32, (tall, LANES), 1)
    live = codes[HEADER:] >= 0

    def logits(c, carry):
        at = pl.multiple_of(c * LANES, LANES)
        keep = (codes == colp_ref[:, pl.ds(at, LANES)]) & (at - EDGE + lane <= ipos)
        for h in range(2):
            cols = slice(h * LANES, (h + 1) * LANES)
            raw = dot(q_ref[pl.ds(top, tall), cols], k_ref[pl.ds(at, LANES), cols], NT)
            raw = jnp.where(keep, raw, 0.0)
            high = raw.astype(jnp.bfloat16)
            lm_ref[h, :, pl.ds(at, LANES)] = high
            lo_ref[h, :, pl.ds(at, LANES)] = (raw - high.astype(jnp.float32)).astype(jnp.bfloat16)
        return carry

    lax.fori_loop(0, 2 * step + 3, logits, 0)
    mx_ref[...] = jnp.full(mx_ref.shape, NEG, jnp.float32)

    def convolve(c, carry):
        for n in range(2):
            convolve_block(pl.multiple_of((2 * c + n) * LANES, LANES))
        return carry

    def convolve_block(at):
        keep = (codes[HEADER:] == colc_ref[:, pl.ds(at, LANES)]) & (at + lane[HEADER:] <= ipos[HEADER:])
        for h in range(2):
            high = lm_ref[h, :, pl.ds(at, 2 * LANES)]
            p_ref[h] = dot(jnp.concatenate([high, lo_ref[h, :, pl.ds(at, 2 * LANES)], high], axis=1), t_ref[h])
            conv = p_ref[h, HEADER:, :LANES]
            for a in range(1, taps):
                conv = conv + p_ref[h, HEADER - a : tall - a, a * LANES : (a + 1) * LANES]
            conv = jnp.where(keep, conv, NEG)
            cv_ref[h, :, pl.ds(at, LANES)] = conv
            mx_ref[h] = jnp.maximum(mx_ref[h], conv)

    lax.fori_loop(0, step + 1, convolve, 0)
    sm_ref[...] = jnp.zeros(sm_ref.shape, jnp.float32)
    for h in range(2):
        peak = jnp.max(mx_ref[h], axis=-1, keepdims=True)
        mx_ref[h] = jnp.where(live, jnp.broadcast_to(peak, (ROWS, LANES)), 0.0)

    def exponents(c, carry):
        for h in range(2):
            total = sm_ref[h]
            for n in range(2):
                at = pl.multiple_of((2 * c + n) * LANES, LANES)
                value = jnp.exp(cv_ref[h, :, pl.ds(at, LANES)] - mx_ref[h])
                cv_ref[h, :, pl.ds(at, LANES)] = value
                total = total + value
            sm_ref[h] = total
        return carry

    lax.fori_loop(0, step + 1, exponents, 0)
    for h in range(2):
        total = jnp.sum(sm_ref[h], axis=-1, keepdims=True)
        total = jnp.where(live, jnp.broadcast_to(total, (ROWS, LANES)), 1.0)
        sm_ref[h] = 1.0 / total
    acc_ref[...] = jnp.zeros(acc_ref.shape, jnp.float32)
    pair = pl.program_id(0)
    mix = [[mix_ref[pair, 2 * g + h] for h in range(2)] for g in range(2)]

    def mixing(c, carry):
        at = pl.multiple_of(c * 2 * LANES, 2 * LANES)
        mixed = [[], []]
        for n in range(2):
            spot = pl.ds(pl.multiple_of(at + n * LANES, LANES), LANES)
            prob = [cv_ref[h, :, spot] * sm_ref[h] for h in range(2)]
            for g in range(2):
                prob_ref[g, :, spot] = prob[g].astype(prob_ref.dtype)
                mixed[g].append((mix[g][0] * prob[0] + mix[g][1] * prob[1]).astype(jnp.bfloat16))
        for g in range(2):
            cols = slice(g * LANES, (g + 1) * LANES)
            value = v_ref[pl.ds(pl.multiple_of(at + EDGE, 16), 2 * LANES), cols]
            acc_ref[g] += dot(jnp.concatenate(mixed[g], axis=1), value)
        return carry

    lax.fori_loop(0, step + 1, mixing, 0)
    for g in range(2):
        att = acc_ref[g]
        att_ref[:, g * LANES : (g + 1) * LANES] = att
        unit, _ = group_stats(att, dim)
        normed = unit * gain_ref[0:1, g * LANES : (g + 1) * LANES]
        place_head(normed_ref, pl.ds(pl.multiple_of(first, ROWS), ROWS), 0, g, normed, dim, pairs)


def backward_kernel(
    dim, taps, span, pairs, qs_ref, ks_ref, vs_ref, t_ref, rowc_ref, colp_ref, colt_ref, rowt_ref, prob_ref, att_ref, dns_ref,
    gain_ref, mix_ref, dproj_ref, taps_ref, dmix_ref, dgain_ref,
    dp_ref, dc_ref, dl_ref, lt_ref, dkt_ref, dvt_ref, datt_ref, dattt_ref, qt_ref, rs_ref, dqa_ref, dm_ref, ahead_ref, g_ref, q_ref, k_ref, v_ref, dn_ref,
):
    pair = pl.program_id(0)
    turn = pl.program_id(1)
    step = pl.num_programs(1) - 1 - turn
    first = pl.multiple_of(step * ROWS, ROWS)
    own = pl.multiple_of(first + EDGE, 16)
    codes = rowc_ref[pl.ds(own, ROWS), :]
    ipos = first + lax.broadcasted_iota(jnp.int32, (ROWS, LANES), 0)
    lane = lax.broadcasted_iota(jnp.int32, (ROWS, LANES), 1)
    blocks = 2 * step + 2
    mix = [[mix_ref[pair, 2 * g + h] for h in range(2)] for g in range(2)]

    @pl.when(turn == 0)
    def _():
        dc_ref[...] = jnp.zeros(dc_ref.shape, jnp.float32)
        dkt_ref[...] = jnp.zeros(dkt_ref.shape, jnp.float32)
        dvt_ref[...] = jnp.zeros(dvt_ref.shape, jnp.float32)
        g_ref[...] = jnp.zeros(g_ref.shape, jnp.float32)
        dmix_ref[...] = jnp.zeros(dmix_ref.shape, jnp.float32)
        dgain_ref[...] = jnp.zeros(dgain_ref.shape, jnp.float32)
        widen((qs_ref, ks_ref, vs_ref), (q_ref, k_ref, v_ref), dim, pairs)

        @pl.when(pair == 0)
        def _():
            for rows in (slice(0, EDGE), slice(dproj_ref.shape[0] - EDGE, dproj_ref.shape[0])):
                dproj_ref[rows, :] = jnp.zeros((EDGE, dproj_ref.shape[1]), jnp.bfloat16)

    widen((dns_ref,), (dn_ref,), dim, pairs)

    @pl.when(turn > 0)
    def _():
        for h in range(2):
            dc_ref[h, ROWS:, :] = dc_ref[h, :8, :]

    for g in range(2):
        cols = slice(g * LANES, (g + 1) * LANES)
        unit, inv = group_stats(att_ref[:, cols], dim)
        grad = dn_ref[:, cols]
        dgain_ref[0:1, cols] += jnp.sum(grad * unit, axis=0, keepdims=True)
        scaled = grad * gain_ref[0:1, cols]
        mean = jnp.sum(scaled, axis=-1, keepdims=True) / dim
        inner = jnp.sum(scaled * unit, axis=-1, keepdims=True) / dim
        datt = inv * (scaled - mean - unit * inner)
        datt = jnp.where(lane_mask(dim), datt, 0.0)
        high = datt.astype(jnp.bfloat16)
        datt_ref[g, :, :LANES] = high
        datt_ref[g, :, LANES:] = (datt - high.astype(jnp.float32)).astype(jnp.bfloat16)
        dattt_ref[g] = datt.T.astype(jnp.bfloat16)
        qt_ref[g] = q_ref[pl.ds(own, ROWS), cols].astype(jnp.float32).T.astype(jnp.bfloat16)
    rs_ref[...] = jnp.zeros(rs_ref.shape, jnp.float32)
    dm_ref[...] = jnp.zeros(dm_ref.shape, jnp.float32)

    def probs(c, carry):
        for n in range(2):
            probs_block(pl.multiple_of((2 * c + n) * LANES, LANES))
        return carry

    def probs_block(at):
        prob = [prob_ref[h, :, pl.ds(at, LANES)].astype(jnp.float32) for h in range(2)]
        dmixed = []
        for g in range(2):
            cols = slice(g * LANES, (g + 1) * LANES)
            value = v_ref[pl.ds(at + EDGE, LANES), cols]
            dmixed.append(dot(datt_ref[g], jnp.concatenate([value, value], axis=1), NT))
            mixed = (mix[g][0] * prob[0] + mix[g][1] * prob[1]).astype(jnp.bfloat16)
            dvt_ref[g, :, pl.ds(at, LANES)] += dot(dattt_ref[g], mixed)
            for h in range(2):
                dm_ref[2 * g + h] += dmixed[g] * prob[h]
        for h in range(2):
            dprob = mix[0][h] * dmixed[0] + mix[1][h] * dmixed[1]
            dp_ref[h, :, pl.ds(at, LANES)] = dprob
            rs_ref[h] += prob[h] * dprob

    lax.fori_loop(0, step + 1, probs, 0)
    for h in range(2):
        rs_ref[h] = jnp.broadcast_to(jnp.sum(rs_ref[h], axis=-1, keepdims=True), (ROWS, LANES))
    for n in range(4):
        dmix_ref[0, n : n + 1, :] += jnp.sum(dm_ref[n], axis=0, keepdims=True)

    tlane = lax.broadcasted_iota(jnp.int32, (LANES, ROWS), 1)
    trow = lax.broadcasted_iota(jnp.int32, (LANES, ROWS), 0)

    def transposed_logits(c, carry):
        at = pl.multiple_of(c * LANES, LANES)
        wide = jnp.concatenate([colt_ref[pl.ds(at, LANES), :]] * 2, axis=1)
        keep = (wide == rowt_ref[:, pl.ds(first, ROWS)]) & (at - EDGE + trow <= first + tlane)
        for h in range(2):
            cols = slice(h * LANES, (h + 1) * LANES)
            raw = dot(k_ref[pl.ds(at, LANES), cols], q_ref[pl.ds(own, ROWS), cols], NT)
            lt_ref[h, pl.ds(at, LANES), :] = jnp.where(keep, raw, 0.0).astype(jnp.bfloat16)
            dl_ref[h, :, pl.ds(at, LANES)] = jnp.zeros((ROWS, LANES), jnp.float32)
        return carry

    lax.fori_loop(0, blocks + 1, transposed_logits, 0)

    def convolve(c, carry):
        for n in range(2):
            convolve_block(pl.multiple_of((2 * c + n) * LANES, LANES))
        return carry

    def convolve_block(at):
        for h in range(2):
            prob = prob_ref[h, :, pl.ds(at, LANES)].astype(jnp.float32)
            dc_ref[h, :ROWS, pl.ds(at, LANES)] = prob * (dp_ref[h, :, pl.ds(at, LANES)] - rs_ref[h])
            shifted = jnp.concatenate(
                [dc_ref[h, a : a + ROWS, pl.ds(at, LANES)].astype(jnp.bfloat16) for a in range(taps)], axis=1
            )
            g_ref[h] += dot(lt_ref[h, pl.ds(at, 2 * LANES), :], shifted)
            dl_ref[h, :, pl.ds(at, 2 * LANES)] += dot(shifted, t_ref[h], NT)

    lax.fori_loop(0, step + 1, convolve, 0)
    dqa_ref[...] = jnp.zeros(dqa_ref.shape, jnp.float32)

    def logits(c, carry):
        at = pl.multiple_of(c * LANES, LANES)
        keep = (codes == colp_ref[:, pl.ds(at, LANES)]) & (at - EDGE + lane <= ipos)
        for h in range(2):
            cols = slice(h * LANES, (h + 1) * LANES)
            dl = jnp.where(keep, dl_ref[h, :, pl.ds(at, LANES)], 0.0).astype(jnp.bfloat16)
            dqa_ref[h] += dot(dl, k_ref[pl.ds(at, LANES), cols])
            dkt_ref[h, :, pl.ds(at, LANES)] += dot(qt_ref[h], dl)
        return carry

    lax.fori_loop(0, blocks + 1, logits, 0)
    for h in range(2):
        place_head(dproj_ref, pl.ds(own, ROWS), 0, h, dqa_ref[h], dim, pairs)

    @pl.when(step == 0)
    def _():
        head = slice(EDGE - HEADER, EDGE)
        wide = (HEADER, 2 * LANES)
        keep = jnp.concatenate([rowc_ref[head, :]] * 2, axis=1) == colp_ref[:, : 2 * LANES]
        keep = keep & (
            lax.broadcasted_iota(jnp.int32, wide, 1) - EDGE <= lax.broadcasted_iota(jnp.int32, wide, 0) - HEADER
        )
        for h in range(2):
            cols = slice(h * LANES, (h + 1) * LANES)
            ahead_ref[:HEADER, :] = jnp.zeros((HEADER, LANES), jnp.float32)
            ahead_ref[HEADER:, :] = dc_ref[h, :HEADER, :LANES]
            shifted = jnp.concatenate(
                [ahead_ref[a : a + HEADER, :].astype(jnp.bfloat16) for a in range(taps)], axis=1
            )
            near = k_ref[: 2 * LANES, cols]
            query = q_ref[head, cols]
            raw = jnp.where(keep, dot(query, near, NT), 0.0)
            g_ref[h] += dot(raw.T.astype(jnp.bfloat16), shifted)
            dl = jnp.where(keep, dot(shifted, t_ref[h], NT), 0.0).astype(jnp.bfloat16)
            place_head(dproj_ref, head, 0, h, dot(dl, near), dim, pairs)
            dkt_ref[h, :, : 2 * LANES] += dot(query.astype(jnp.float32).T.astype(jnp.bfloat16), dl)
            every = slice(0, dkt_ref.shape[2])
            place_head(dproj_ref, every, 2 * pairs * dim, h, dkt_ref[h].T, dim, pairs)
            inner = slice(EDGE, EDGE + dvt_ref.shape[2])
            place_head(dproj_ref, inner, 4 * pairs * dim, h, dvt_ref[h].T, dim, pairs)
        shape = (2 * LANES, taps * LANES)
        lanes = lax.broadcasted_iota(jnp.int32, shape, 1) & (LANES - 1)
        diff = lanes + (EDGE + span // 2) - lax.broadcasted_iota(jnp.int32, shape, 0)

        def diagonals(b, carry):
            for h in range(2):
                part = jnp.where(diff == b, g_ref[h], 0.0)
                taps_ref[h, pl.ds(b, 1), :] = jnp.sum(part, axis=0, keepdims=True)
            return carry

        lax.fori_loop(0, span, diagonals, 0)


def attention_forward(proj, toep, codes, gain, mix, dim, taps):
    tall = proj.shape[0]
    frame = tall - 2 * EDGE
    pairs = mix.shape[0]
    steps = frame // ROWS
    whole = lambda off: pl.BlockSpec((tall, 2 * pairs * dim), lambda p, r: (0, off))
    wide = pairs * 2 * LANES
    return pl.pallas_call(
        functools.partial(forward_kernel, dim, taps, mix.shape[0]),
        grid=(pairs, steps),
        in_specs=[
            whole(0), whole(1), whole(2),
            pl.BlockSpec((2, 6 * LANES, taps * LANES), lambda p, r: (p, 0, 0)),
            pl.BlockSpec((tall, LANES), lambda p, r: (0, 0)),
            pl.BlockSpec((1, tall), lambda p, r: (0, 0)),
            pl.BlockSpec((1, frame), lambda p, r: (0, 0)),
            pl.BlockSpec((1, 2 * LANES), lambda p, r: (0, p)),
            pl.BlockSpec(memory_space=pltpu.SMEM),
        ],
        out_specs=[
            pl.BlockSpec((frame, 2 * pairs * dim), lambda p, r: (0, 0)),
            pl.BlockSpec((ROWS, 2 * LANES), lambda p, r: (r, p)),
            pl.BlockSpec((2, ROWS, frame), lambda p, r: (p, r, 0)),
        ],
        out_shape=[
            jax.ShapeDtypeStruct((frame, 2 * pairs * dim), jnp.bfloat16),
            jax.ShapeDtypeStruct((frame, wide), jnp.float32),
            jax.ShapeDtypeStruct((2 * pairs, frame, frame), PROB),
        ],
        scratch_shapes=[
            pltpu.VMEM((2, ROWS + HEADER, tall), jnp.bfloat16),
            pltpu.VMEM((2, ROWS + HEADER, tall), jnp.bfloat16),
            pltpu.VMEM((2, ROWS + HEADER, taps * LANES), jnp.float32),
            pltpu.VMEM((2, ROWS, frame), jnp.float32),
            pltpu.VMEM((2, ROWS, LANES), jnp.float32),
            pltpu.VMEM((2, ROWS, LANES), jnp.float32),
            pltpu.VMEM((2, ROWS, LANES), jnp.float32),
            pltpu.VMEM((tall, 2 * LANES), jnp.bfloat16),
            pltpu.VMEM((tall, 2 * LANES), jnp.bfloat16),
            pltpu.VMEM((tall, 2 * LANES), jnp.bfloat16),
        ],
        cost_estimate=pl.CostEstimate(flops=10_000_000_000, bytes_accessed=40_000_000, transcendentals=0),
        compiler_params=pltpu.CompilerParams(vmem_limit_bytes=48 << 20),
        name="attend",
    )(proj, proj, proj, toep, codes["row"], codes["colp"], codes["col"], gain, mix)


def attention_backward(proj, toep, codes, prob, att, dnormed, gain, mix, dim, taps, span):
    tall = proj.shape[0]
    frame = tall - 2 * EDGE
    pairs = mix.shape[0]
    steps = frame // ROWS
    whole = lambda off: pl.BlockSpec((tall, 2 * pairs * dim), lambda p, r: (0, off))
    wide = pairs * 2 * LANES
    back = lambda r: steps - 1 - r
    return pl.pallas_call(
        functools.partial(backward_kernel, dim, taps, span, mix.shape[0]),
        grid=(pairs, steps),
        in_specs=[
            whole(0), whole(1), whole(2),
            pl.BlockSpec((2, 2 * LANES, taps * LANES), lambda p, r: (p, 0, 0)),
            pl.BlockSpec((tall, LANES), lambda p, r: (0, 0)),
            pl.BlockSpec((1, tall), lambda p, r: (0, 0)),
            pl.BlockSpec((tall, LANES), lambda p, r: (0, 0)),
            pl.BlockSpec((1, frame), lambda p, r: (0, 0)),
            pl.BlockSpec((2, ROWS, frame), lambda p, r: (p, back(r), 0)),
            pl.BlockSpec((ROWS, 2 * LANES), lambda p, r: (back(r), p)),
            pl.BlockSpec((ROWS, 2 * pairs * dim), lambda p, r: (back(r), 0)),
            pl.BlockSpec((1, 2 * LANES), lambda p, r: (0, p)),
            pl.BlockSpec(memory_space=pltpu.SMEM),
        ],
        out_specs=[
            pl.BlockSpec((tall, 6 * pairs * dim), lambda p, r: (0, 0)),
            pl.BlockSpec((2, 16, taps * LANES), lambda p, r: (p, 0, 0)),
            pl.BlockSpec((1, 8, LANES), lambda p, r: (p, 0, 0)),
            pl.BlockSpec((1, 2 * LANES), lambda p, r: (0, p)),
        ],
        out_shape=[
            jax.ShapeDtypeStruct((tall, 6 * pairs * dim), jnp.bfloat16),
            jax.ShapeDtypeStruct((2 * pairs, 16, taps * LANES), jnp.float32),
            jax.ShapeDtypeStruct((pairs, 8, LANES), jnp.float32),
            jax.ShapeDtypeStruct((1, wide), jnp.float32),
        ],
        scratch_shapes=[
            pltpu.VMEM((2, ROWS, frame), jnp.float32),
            pltpu.VMEM((2, ROWS + 8, frame), jnp.float32),
            pltpu.VMEM((2, ROWS, tall), jnp.float32),
            pltpu.VMEM((2, tall, ROWS), jnp.bfloat16),
            pltpu.VMEM((2, LANES, tall), jnp.float32),
            pltpu.VMEM((2, LANES, frame), jnp.float32),
            pltpu.VMEM((2, ROWS, 2 * LANES), jnp.bfloat16),
            pltpu.VMEM((2, LANES, ROWS), jnp.bfloat16),
            pltpu.VMEM((2, LANES, ROWS), jnp.bfloat16),
            pltpu.VMEM((2, ROWS, LANES), jnp.float32),
            pltpu.VMEM((2, ROWS, LANES), jnp.float32),
            pltpu.VMEM((4, ROWS, LANES), jnp.float32),
            pltpu.VMEM((2 * HEADER, LANES), jnp.float32),
            pltpu.VMEM((2, 2 * LANES, taps * LANES), jnp.float32),
            pltpu.VMEM((tall, 2 * LANES), jnp.bfloat16),
            pltpu.VMEM((tall, 2 * LANES), jnp.bfloat16),
            pltpu.VMEM((tall, 2 * LANES), jnp.bfloat16),
            pltpu.VMEM((ROWS, 2 * LANES), jnp.float32),
        ],
        cost_estimate=pl.CostEstimate(flops=10_000_000_000, bytes_accessed=40_000_000, transcendentals=0),
        compiler_params=pltpu.CompilerParams(vmem_limit_bytes=48 << 20),
        name="attend_back",
    )(proj, proj, proj, toep, codes["row"], codes["colp"], codes["colt"], codes["rowt"], prob, att, dnormed, gain, mix)


def make_codes(segment, valid):
    row = jnp.where(valid > 0, segment, -1)
    col = jnp.where(valid > 0, segment, -2)
    rowp = jnp.pad(row, (EDGE - HEADER, EDGE), constant_values=-1)
    colp = jnp.pad(col, (EDGE - HEADER, EDGE), constant_values=-2)
    tall = rowp.shape[0]
    return {
        "row": jnp.broadcast_to(rowp[:, None], (tall, LANES)),
        "colt": jnp.broadcast_to(colp[:, None], (tall, LANES)),
        "colp": colp[None],
        "col": col[None, HEADER:],
        "rowt": row[None, HEADER:],
    }


MESH = pl.DeviceIdType.MESH
TOKENS_AFTER = 2


def meet(peers):
    barrier = pltpu.get_barrier_semaphore()
    for peer in peers:
        pl.semaphore_signal(barrier, inc=1, device_id=peer, device_id_type=MESH)
    pl.semaphore_wait(barrier, len(peers))


def send(src, dst, send_sem, recv_sem, peer):
    return pltpu.make_async_remote_copy(
        src_ref=src, dst_ref=dst, send_sem=send_sem, recv_sem=recv_sem, device_id=peer, device_id_type=MESH
    )


def gather_kernel(
    reps, count, w_ref, x_ref, z_ref, wc_ref, f_ref, own_sem, side_send, side_recv, far_send, far_recv, rep_send, rep_recv,
    tok_send, tok_recv, head_send, head_recv,
):
    rep = lax.axis_index("rep")
    me = lax.axis_index("seq")
    chips = count // 2
    chip, core = me // 2, me % 2
    rows = w_ref.shape[0]
    part = rows // reps
    full = w_ref.shape[1] // 3
    cols = wc_ref.shape[1] // 3
    tokens = x_ref.shape[0]
    place = me % 4
    sibling = chip * 2 + 1 - core
    far_ids = [((chip + k) % chips) * 2 + e for k in range(1, chips) for e in range(2)]
    rep_ids = [(rep + k) % reps for k in range(1, reps)]
    at = lambda r, s: (r, s)
    meet([at(rep, s) for s in far_ids + [sibling]] + [at(r, me) for r in rep_ids])

    def source(first, size, who, t):
        left = pl.multiple_of(t * full + (who % 4) * cols, LANES)
        return w_ref.at[pl.ds(first, size), pl.ds(left, cols)]

    def target(first, size, t):
        return wc_ref.at[pl.ds(first, size), pl.ds(t * cols, cols)]

    def spot(who, r):
        return pl.multiple_of(who * rows + r * part, 16)

    def token_rows(who, half):
        return f_ref.at[pl.ds(pl.multiple_of(EDGE + (who % 4) * tokens + half * (tokens // 2), 16), tokens // 2), :]

    waits = []
    quarter = pl.multiple_of(rep * part, 16)
    for n, who in enumerate(far_ids):
        for t in range(3):
            copy = send(
                source(quarter, part, who, t), target(spot(me, rep), part, t), far_send.at[n, t], far_recv.at[me, t],
                at(rep, who),
            )
            copy.start()
            waits.append(copy)
    for t in range(3):
        copy = send(
            source(0, rows, sibling, t), target(spot(me, 0), rows, t), side_send.at[t], side_recv.at[t], at(rep, sibling)
        )
        copy.start()
        waits.append(copy)
    local = [
        pltpu.make_async_copy(source(0, rows, me, t), target(spot(me, 0), rows, t), own_sem.at[t]) for t in range(3)
    ]
    lead = EDGE - HEADER
    local.append(pltpu.make_async_copy(z_ref.at[pl.ds(0, lead), :], f_ref.at[pl.ds(0, lead), :], own_sem.at[4]))
    local.append(
        pltpu.make_async_copy(z_ref, f_ref.at[pl.ds(f_ref.shape[0] - EDGE, EDGE), :], own_sem.at[5])
    )
    local.append(pltpu.make_async_copy(
        x_ref, f_ref.at[pl.ds(pl.multiple_of(EDGE + place * tokens, 16), tokens), :], own_sem.at[3]
    ))
    for copy in local:
        copy.start()
    def send_tokens():
        partner = (chip ^ 1) * 2 + core
        for half in range(2):
            mine = x_ref.at[pl.ds(half * (tokens // 2), tokens // 2), :]
            copy = send(mine, token_rows(me, half), tok_send.at[0, half], tok_recv.at[0, half], at(rep, partner))
            copy.start()
            waits.append(copy)
            copy = send(mine, token_rows(me, half), tok_send.at[1, half], tok_recv.at[1, half], at(rep, sibling))
            copy.start()
            waits.append(copy)

    head = f_ref.at[pl.ds(lead, HEADER), :]
    fill = pltpu.make_async_copy(z_ref.at[pl.ds(0, HEADER), :], head, own_sem.at[6])
    sends_on = (place == 3) & (me < count - 4)
    after = [
        send(x_ref.at[pl.ds(tokens - HEADER, HEADER), :], head, head_send.at[v], head_recv.at[0],
             at(rep, lax.rem(me + 1 + v, count)))
        for v in range(4)
    ]
    partner = (chip ^ 1) * 2 + core
    for n, who in enumerate(far_ids):
        if n == min(TOKENS_AFTER, len(far_ids) - 1):
            send_tokens()

            @pl.when(sends_on)
            def _():
                for copy in after:
                    copy.start()

            @pl.when(me < 4)
            def _():
                fill.start()

        for t in range(3):
            got = target(spot(who, rep), part, t)
            send(got, got, far_send.at[n, t], far_recv.at[who, t], at(rep, who)).wait_recv()
        block = wc_ref.at[pl.ds(spot(who, rep), part), :]
        for m, r in enumerate(rep_ids):
            copy = send(block, block, rep_send.at[n, m], rep_recv.at[n, m], at(r, me))
            copy.start()
            waits.append(copy)
    for half in range(2):
        got = token_rows(partner, half)
        send(got, got, tok_send.at[0, half], tok_recv.at[0, half], at(rep, partner)).wait_recv()
        copy = send(got, got, tok_send.at[2, half], tok_recv.at[2, half], at(rep, sibling))
        copy.start()
        waits.append(copy)
    for copy in local:
        copy.wait()

    @pl.when(me < 4)
    def _():
        fill.wait()

    @pl.when(me >= 4)
    def _():
        after[0].wait_recv()

    @pl.when(sends_on)
    def _():
        for copy in after:
            copy.wait_send()

    for t in range(3):
        got = target(spot(sibling, 0), rows, t)
        send(got, got, side_send.at[t], side_recv.at[t], at(rep, sibling)).wait_recv()
    for half in range(2):
        for kind, who in ((1, sibling), (2, partner ^ 1)):
            got = token_rows(who, half)
            send(got, got, tok_send.at[kind, half], tok_recv.at[kind, half], at(rep, sibling)).wait_recv()
    for n, who in enumerate(far_ids):
        for m in range(reps - 1):
            block = wc_ref.at[pl.ds(spot(who, (rep + reps - 1 - m) % reps), part), :]
            send(block, block, rep_send.at[n, m], rep_recv.at[n, m], at(rep_ids[m], me)).wait_recv()
    for copy in waits:
        copy.wait_send()


def gather_weight(weight, tokens, reps, count):
    rows, full = weight.shape
    own = full // 4
    far = count - 2
    dma = pltpu.SemaphoreType.DMA
    return pl.pallas_call(
        functools.partial(gather_kernel, reps, count),
        in_specs=[pl.BlockSpec(memory_space=pl.ANY)] * 3,
        out_specs=[pl.BlockSpec(memory_space=pl.ANY)] * 2,
        out_shape=[
            jax.ShapeDtypeStruct((rows * count, own), weight.dtype),
            jax.ShapeDtypeStruct((tokens.shape[0] * 4 + 2 * EDGE, tokens.shape[1]), tokens.dtype),
        ],
        scratch_shapes=[
            dma((7,)), dma((3,)), dma((3,)), dma((far, 3)), dma((count, 3)), dma((far, reps - 1)), dma((far, reps - 1)),
            dma((3, 2)), dma((3, 2)), dma((4,)), dma((1,)),
        ],
        cost_estimate=pl.CostEstimate(flops=2_000_000_000, bytes_accessed=20_000_000, transcendentals=0),
        compiler_params=pltpu.CompilerParams(collective_id=1, has_side_effects=True),
        name="gather_weight",
    )(weight, tokens, jnp.zeros((EDGE, tokens.shape[1]), tokens.dtype))


def frame_gather_kernel(x_ref, f_ref, own_sem, send_sem, recv_sem):
    rep = lax.axis_index("rep")
    me = lax.axis_index("seq")
    chip, core = me // 2, me % 2
    half_rows = x_ref.shape[0] // 2
    sibling = (rep, chip * 2 + 1 - core)
    partner = (rep, (chip ^ 1) * 2 + core)
    meet([sibling, partner])

    def rows(who, half):
        return f_ref.at[pl.ds(pl.multiple_of((who % 4) * 2 * half_rows + half * half_rows, 16), half_rows), :]

    waits = []

    def push(src, dst, kind, half, peer):
        copy = send(src, dst, send_sem.at[kind, half], recv_sem.at[kind, half], peer)
        copy.start()
        waits.append(copy)

    for half in range(2):
        push(x_ref.at[pl.ds(half * half_rows, half_rows), :], rows(me, half), 0, half, partner)
    for half in range(2):
        push(x_ref.at[pl.ds(half * half_rows, half_rows), :], rows(me, half), 1, half, sibling)
    local = pltpu.make_async_copy(
        x_ref, f_ref.at[pl.ds(pl.multiple_of((me % 4) * 2 * half_rows, 16), 2 * half_rows), :], own_sem.at[0]
    )
    local.start()

    def arrived(kind, half, who):
        got = rows(who, half)
        send(got, got, send_sem.at[kind, half], recv_sem.at[kind, half], sibling).wait_recv()
        return got

    for half in range(2):
        got = arrived(0, half, partner[1])
        push(got, got, 2, half, sibling)
    local.wait()
    for half in range(2):
        arrived(1, half, sibling[1])
        arrived(2, half, partner[1] ^ 1)
    for copy in waits:
        copy.wait_send()


def frame_gather(values):
    dma = pltpu.SemaphoreType.DMA
    return pl.pallas_call(
        frame_gather_kernel,
        in_specs=[pl.BlockSpec(memory_space=pl.ANY)],
        out_specs=pl.BlockSpec(memory_space=pl.ANY),
        out_shape=jax.ShapeDtypeStruct((values.shape[0] * 4, values.shape[1]), values.dtype),
        scratch_shapes=[dma((1,)), dma((3, 2)), dma((3, 2))],
        cost_estimate=pl.CostEstimate(flops=2_000_000_000, bytes_accessed=8_000_000, transcendentals=0),
        compiler_params=pltpu.CompilerParams(collective_id=2, has_side_effects=True),
        name="frame_gather",
    )(values)


def frame_swap_kernel(h_ref, r_ref, own_sem, send_sem, recv_sem):
    rep = lax.axis_index("rep")
    me = lax.axis_index("seq")
    base, place = me // 4 * 4, me % 4
    rows = r_ref.shape[0]
    cols = h_ref.shape[1]
    peers = [base + (place ^ n) for n in (2, 3, 1)]
    meet([(rep, who) for who in peers])

    def block(who):
        return h_ref.at[pl.ds(pl.multiple_of((who % 4) * rows, 16), rows), :]

    def spot(who):
        return r_ref.at[:, pl.ds(pl.multiple_of((who % 4) * cols, LANES), cols)]

    copies = [
        send(block(who), spot(me), send_sem.at[n], recv_sem.at[n], (rep, who)) for n, who in enumerate(peers)
    ]
    for copy in copies:
        copy.start()
    local = pltpu.make_async_copy(block(me), spot(me), own_sem.at[0])
    local.start()
    local.wait()
    for n, who in enumerate(peers):
        send(block(who), spot(who), send_sem.at[n], recv_sem.at[n], (rep, who)).wait_recv()
    for copy in copies:
        copy.wait_send()


def frame_swap(values):
    dma = pltpu.SemaphoreType.DMA
    return pl.pallas_call(
        frame_swap_kernel,
        in_specs=[pl.BlockSpec(memory_space=pl.ANY)],
        out_specs=pl.BlockSpec(memory_space=pl.ANY),
        out_shape=jax.ShapeDtypeStruct((values.shape[0] // 4, values.shape[1] * 4), values.dtype),
        scratch_shapes=[dma((1,)), dma((3,)), dma((3,))],
        cost_estimate=pl.CostEstimate(flops=2_000_000_000, bytes_accessed=2_000_000, transcendentals=0),
        compiler_params=pltpu.CompilerParams(collective_id=3, has_side_effects=True),
        name="frame_swap",
    )(values)


def reduce_kernel(
    reps, count, gi_ref, go_ref, dn_ref, xs_ref, sv_ref, oi_ref, oo_ref, od_ref, so_ref,
    li_ref, ri_ref, rb_ref, zi_ref, qi_ref, lo_ref, ro_ref, rc_ref, zo_ref, qo_ref, ld_ref, bd_ref, hd_ref,
    load_sem, one_send, one_recv, on_send, on_recv, near_send, near_recv, past_send, past_recv, two_send, two_recv, three_send, three_recv, tok_send, tok_recv,
    head_send, head_recv, vec_ref, one_ref, two_ref, sum_ref, small_one, small_got, small_two, small_end,
):
    rep = lax.axis_index("rep")
    me = lax.axis_index("seq")
    chip, core = me // 2, me % 2
    base, place = me // 4 * 4, me % 4
    sibling = chip * 2 + 1 - core
    partner = (chip ^ 1) * 2 + core
    rep_ids = [(rep + k) % reps for k in range(1, reps)]
    seq_ids = [(me + k) % count for k in range(1, count)]
    part = li_ref.shape[2]
    rows = part * reps
    halves = lo_ref.shape[0]
    frames = count // 4
    cols = gi_ref.shape[1] // 3
    width = cols * 4
    tokens = od_ref.shape[0]
    meet([(r, me) for r in rep_ids] + [(rep, s) for s in seq_ids])
    waits = []

    def push(src, dst, send_sem, recv_sem, peer):
        copy = send(src, dst, send_sem, recv_sem, peer)
        copy.start()
        waits.append(copy)

    def arrived(dst, send_sem, recv_sem):
        send(dst, dst, send_sem, recv_sem, (rep, sibling)).wait_recv()

    def quarter(ref, who, r):
        return ref.at[pl.ds(pl.multiple_of(who * rows + r * part, 16), part), :]

    def token_rows(who):
        return dn_ref.at[pl.ds(pl.multiple_of(EDGE + (who % 4) * tokens, 16), tokens), :]

    ahead = send(
        dn_ref.at[pl.ds(EDGE - HEADER, HEADER), :], hd_ref.at[place], head_send.at[0], head_recv.at[place],
        (rep, lax.rem(base + count - 1, count)),
    )

    @pl.when(me >= 4)
    def _():
        ahead.start()

    push(token_rows(partner ^ 1), bd_ref.at[0], tok_send.at[0], tok_recv.at[0], (rep, sibling))
    push(token_rows(sibling), bd_ref.at[1], tok_send.at[1], tok_recv.at[1], (rep, sibling))
    loads = [
        pltpu.make_async_copy(token_rows(partner), ld_ref.at[0], load_sem.at[0]),
        pltpu.make_async_copy(token_rows(me), ld_ref.at[1], load_sem.at[1]),
    ]
    for copy in loads:
        copy.start()
    order = seq_ids + [me]
    near = [rep ^ 1, rep ^ 2]
    past = [rep ^ 2, rep ^ 1]
    blocks = [(go_ref, h, lo_ref.at[h], ro_ref.at[h], rc_ref.at[h]) for h in range(halves)]
    blocks += [(gi_ref, who, li_ref.at[n], ri_ref.at[n], rb_ref.at[n]) for n, who in enumerate(order)]
    for n, (grad, row, _, got, _) in enumerate(blocks):
        for m, r in enumerate((near[n % 2], rep ^ 3)):
            push(quarter(grad, row, r), got.at[m], one_send.at[n, m], one_recv.at[n, m], (near[n % 2], me))
    own = [
        pltpu.make_async_copy(quarter(grad, row, r), held.at[m], load_sem.at[2 + 2 * n + m])
        for n, (grad, row, held, _, _) in enumerate(blocks)
        for m, r in enumerate((rep, past[n % 2]))
    ]
    for copy in own:
        copy.start()

    loads[0].wait()
    arrived(bd_ref.at[0], tok_send.at[0], tok_recv.at[0])
    wide = jnp.float32
    ld_ref[0] = (ld_ref[0].astype(wide) + bd_ref[0].astype(wide)).astype(jnp.bfloat16)
    push(ld_ref.at[0], bd_ref.at[2], tok_send.at[2], tok_recv.at[2], (rep, partner))

    def pass_on(n):
        _, _, held, got, last = blocks[n]
        own[2 * n + 1].wait()
        arrived(got.at[1], one_send.at[n, 1], one_recv.at[n, 1])
        held[1] = (held[1].astype(wide) + got[1].astype(wide)).astype(jnp.bfloat16)
        push(held.at[1], last, on_send.at[n], on_recv.at[n], (past[n % 2], me))

    def finish(n):
        _, _, held, got, last = blocks[n]
        own[2 * n].wait()
        arrived(got.at[0], one_send.at[n, 0], one_recv.at[n, 0])
        arrived(last, on_send.at[n], on_recv.at[n])
        held[0] = (held[0].astype(wide) + got[0].astype(wide) + last[...].astype(wide)).astype(jnp.bfloat16)
        if n < halves:
            owner = place * halves + n

            @pl.when(owner == me)
            def _():
                zo_ref[me // 4] = lo_ref[n, 0]

            @pl.when(owner != me)
            def _():
                shipped(n).start()
        elif n < halves + count - 1:
            k = n - halves
            push(li_ref.at[k, 0], zi_ref.at[me], two_send.at[k], two_recv.at[me], (rep, order[k]))
        else:
            zi_ref[me] = li_ref[count - 1, 0]

    def shipped(h):
        return send(
            lo_ref.at[h, 0], zo_ref.at[me // 4], two_send.at[count + h], two_recv.at[count + me // 4],
            (rep, place * halves + h),
        )

    for n in range(len(blocks) + 2):
        if n < len(blocks):
            pass_on(n)
        if n >= 2:
            finish(n - 2)

    loads[1].wait()
    arrived(bd_ref.at[1], tok_send.at[1], tok_recv.at[1])
    arrived(bd_ref.at[2], tok_send.at[2], tok_recv.at[2])
    od_ref[...] = ld_ref[1].astype(wide) + bd_ref[1].astype(wide) + bd_ref[2].astype(wide)

    @pl.when((place == 3) & (me < count - 4))
    def _():
        total = od_ref[tokens - HEADER :, :]
        for v in range(4):
            arrived(hd_ref.at[v], head_send.at[0], head_recv.at[v])
            total = total + hd_ref[v].astype(wide)
        od_ref[tokens - HEADER :, :] = total

    @pl.when(me >= 4)
    def _():
        ahead.wait_send()

    gain_rows = width // LANES
    first = jnp.sum(od_ref[...] * xs_ref[...], axis=0, keepdims=True)
    vec_ref[...] = sv_ref[...]
    for k in range(gain_rows):
        vec_ref[k : k + 1, :] = first[:, k * LANES : (k + 1) * LANES]
    for m, r in enumerate(rep_ids):
        push(vec_ref, one_ref.at[rep], small_one.at[m], small_got.at[rep], (r, me))
    one_ref[rep] = vec_ref[...]

    for f in range(frames):
        source = f * 4 + me // halves

        @pl.when(source != me)
        def _():
            arrived(zo_ref.at[f], two_send.at[count], two_recv.at[count + f])

    total = zo_ref[0].astype(wide)
    for f in range(1, frames):
        total = total + zo_ref[f].astype(wide)
    qo_ref[...] = total.astype(jnp.bfloat16)
    for m, r in enumerate(rep_ids):
        push(qo_ref, oo_ref.at[pl.ds(pl.multiple_of(rep * part, 16), part), :], three_send.at[0, m], three_recv.at[0, m], (r, me))
    for m, r in enumerate(rep_ids):
        arrived(one_ref.at[r], small_one.at[m], small_got.at[r])
    total = one_ref[0]
    for r in range(1, reps):
        total = total + one_ref[r]
    sum_ref[...] = total
    two_ref[me] = total
    for m, s in enumerate(seq_ids):
        push(sum_ref, two_ref.at[me], small_two.at[m], small_end.at[me], (rep, s))
    for n, who in enumerate(seq_ids):
        arrived(zi_ref.at[who], two_send.at[n], two_recv.at[who])
    for u in range(4):
        total = zi_ref[u].astype(wide)
        for f in range(1, frames):
            total = total + zi_ref[f * 4 + u].astype(wide)
        for t in range(3):
            qi_ref[:, t * width + u * cols : t * width + (u + 1) * cols] = total[:, t * cols : (t + 1) * cols].astype(
                jnp.bfloat16
            )
    wing = 3 * width // 2

    def shard(r, k):
        return oi_ref.at[pl.ds(pl.multiple_of(r * part, 16), part), pl.ds(k * wing, wing)]

    for k in range(2):
        mine = qi_ref.at[:, pl.ds(k * wing, wing)]
        push(mine, shard(rep, k), near_send.at[k], near_recv.at[k], (near[k], me))
        push(mine, shard(rep, k), past_send.at[k, 0], past_recv.at[k, 0], (past[k], me))
    for k in range(2):
        got = shard(near[k], k)
        arrived(got, near_send.at[k], near_recv.at[k])
        push(got, got, past_send.at[k, 1], past_recv.at[k, 1], (past[k], me))
    final = [
        pltpu.make_async_copy(qo_ref, oo_ref.at[pl.ds(pl.multiple_of(rep * part, 16), part), :], load_sem.at[0]),
        pltpu.make_async_copy(qi_ref, oi_ref.at[pl.ds(pl.multiple_of(rep * part, 16), part), :], load_sem.at[1]),
    ]
    for copy in final:
        copy.start()
    for h in range(halves):
        owner = place * halves + h

        @pl.when(owner != me)
        def _():
            shipped(h).wait_send()

    for m, s in enumerate(seq_ids):
        arrived(two_ref.at[s], small_two.at[m], small_end.at[s])
    total = two_ref[0]
    for s in range(1, count):
        total = total + two_ref[s]
    so_ref[...] = total
    for copy in final:
        copy.wait()
    for m in range(reps - 1):
        r = (rep + reps - 1 - m) % reps
        arrived(oo_ref.at[pl.ds(pl.multiple_of(r * part, 16), part), :], three_send.at[0, m], three_recv.at[0, m])
    for k in range(2):
        arrived(shard(past[k], k), past_send.at[k, 0], past_recv.at[k, 0])
        arrived(shard(rep ^ 3, k), past_send.at[k, 1], past_recv.at[k, 1])
    for copy in waits:
        copy.wait_send()


def reduce_weights(grad_in, grad_out, tokens, scaled, small, reps, count):
    width = grad_out.shape[1]
    own = grad_in.shape[1]
    rows = width // count
    part = rows // reps
    halves = grad_out.shape[0] // rows
    frames = count // 4
    each = (tokens.shape[0] - 2 * EDGE) // 4
    dma = pltpu.SemaphoreType.DMA
    low = jnp.bfloat16
    hbm = pl.BlockSpec(memory_space=pl.ANY)
    vmem = pl.BlockSpec(memory_space=pltpu.VMEM)
    lines = small.shape[0]
    return pl.pallas_call(
        functools.partial(reduce_kernel, reps, count),
        in_specs=[hbm] * 3 + [vmem] * 2,
        out_specs=[hbm, hbm, vmem, vmem],
        out_shape=[
            jax.ShapeDtypeStruct((rows, 3 * width), low),
            jax.ShapeDtypeStruct((rows, width), low),
            jax.ShapeDtypeStruct((each, width), jnp.float32),
            jax.ShapeDtypeStruct((lines, LANES), jnp.float32),
        ],
        scratch_shapes=[
            pltpu.VMEM((count, 2, part, own), low), pltpu.VMEM((count, 2, part, own), low),
            pltpu.VMEM((count, part, own), low), pltpu.VMEM((count, part, own), low), pltpu.VMEM((part, 3 * width), low),
            pltpu.VMEM((halves, 2, part, width), low), pltpu.VMEM((halves, 2, part, width), low),
            pltpu.VMEM((halves, part, width), low),
            pltpu.VMEM((frames, part, width), low), pltpu.VMEM((part, width), low),
            pltpu.VMEM((2, each, width), low), pltpu.VMEM((3, each, width), low),
            pltpu.VMEM((4, HEADER, width), low),
            dma((2 + 2 * (count + halves),)), dma((count + halves, 2)), dma((count + halves, 2)), dma((count + halves,)),
            dma((count + halves,)),
            dma((2,)), dma((2,)), dma((2, 2)), dma((2, 2)),
            dma((count + halves,)), dma((count + frames,)), dma((1, reps - 1)), dma((1, reps - 1)), dma((3,)), dma((3,)),
            dma((1,)), dma((4,)),
            pltpu.VMEM((lines, LANES), jnp.float32), pltpu.VMEM((reps, lines, LANES), jnp.float32),
            pltpu.VMEM((count, lines, LANES), jnp.float32), pltpu.VMEM((lines, LANES), jnp.float32),
            dma((reps - 1,)), dma((reps,)), dma((count - 1,)), dma((count,)),
        ],
        cost_estimate=pl.CostEstimate(flops=2_000_000_000, bytes_accessed=20_000_000, transcendentals=0),
        compiler_params=pltpu.CompilerParams(collective_id=5, has_side_effects=True, vmem_limit_bytes=40 << 20),
        name="reduce_weights",
    )(grad_in, grad_out, tokens, scaled, small)


def rep_sum_kernel(
    g_refs, o_ref, held, got, last, load_sem, one_send, one_recv, on_send, on_recv
):
    rep = lax.axis_index("rep")
    me = lax.axis_index("seq")
    near = [rep ^ 1, rep ^ 2]
    past = [rep ^ 2, rep ^ 1]
    meet([(r, me) for r in near])
    waits = []

    def push(src, dst, send_sem, recv_sem, peer):
        copy = send(src, dst, send_sem, recv_sem, peer)
        copy.start()
        waits.append(copy)

    def arrived(dst, send_sem, recv_sem):
        send(dst, dst, send_sem, recv_sem, (near[0], me)).wait_recv()

    blocks = [(k, s) for k in range(3) for s in range(2)]

    def rows(n, r):
        k, s = blocks[n]
        size = last[k].shape[1]
        return g_refs[k].at[pl.ds(pl.multiple_of(r * 2 * size + s * size, 16), size), :]

    for n, (k, s) in enumerate(blocks):
        for m, r in enumerate((near[s], rep ^ 3)):
            push(rows(n, r), got[k].at[s, m], one_send.at[n, m], one_recv.at[n, m], (near[s], me))
    own = [
        pltpu.make_async_copy(rows(n, r), held[k].at[s, m], load_sem.at[2 * n + m])
        for n, (k, s) in enumerate(blocks)
        for m, r in enumerate((rep, past[s]))
    ]
    for copy in own:
        copy.start()
    wide = jnp.float32
    for n in range(len(blocks) + 2):
        if n < len(blocks):
            k, s = blocks[n]
            own[2 * n + 1].wait()
            arrived(got[k].at[s, 1], one_send.at[n, 1], one_recv.at[n, 1])
            held[k][s, 1] = (held[k][s, 1].astype(wide) + got[k][s, 1].astype(wide)).astype(jnp.bfloat16)
            push(held[k].at[s, 1], last[k].at[s], on_send.at[n], on_recv.at[n], (past[s], me))
        if n >= 2:
            k, s = blocks[n - 2]
            size = last[k].shape[1]
            own[2 * n - 4].wait()
            arrived(got[k].at[s, 0], one_send.at[n - 2, 0], one_recv.at[n - 2, 0])
            arrived(last[k].at[s], on_send.at[n - 2], on_recv.at[n - 2])
            total = held[k][s, 0].astype(wide) + got[k][s, 0].astype(wide) + last[k][s].astype(wide)
            total = total.astype(jnp.bfloat16)
            lanes = last[0].shape[2]
            if k < 2:
                o_ref[s * size : (s + 1) * size, k * lanes : (k + 1) * lanes] = total
            else:
                for j in range(total.shape[1] // lanes):
                    first = (2 * j + s) * size
                    o_ref[first : first + size, 2 * lanes :] = total[:, j * lanes : (j + 1) * lanes]
    for copy in waits:
        copy.wait_send()


def rep_sum(arrays):
    dma = pltpu.SemaphoreType.DMA
    shapes = [(value.shape[0] // 4, value.shape[1]) for value in arrays]
    low = jnp.bfloat16

    def body(*refs):
        rep_sum_kernel(refs[:3], refs[3], refs[4:7], refs[7:10], refs[10:13], *refs[13:])

    return pl.pallas_call(
        body,
        in_specs=[pl.BlockSpec(memory_space=pl.ANY)] * 3,
        out_specs=pl.BlockSpec(memory_space=pltpu.VMEM),
        out_shape=jax.ShapeDtypeStruct((shapes[0][0], 3 * shapes[0][1]), low),
        scratch_shapes=[pltpu.VMEM((2, 2, rows // 2, cols), low) for rows, cols in shapes]
        + [pltpu.VMEM((2, 2, rows // 2, cols), low) for rows, cols in shapes]
        + [pltpu.VMEM((2, rows // 2, cols), low) for rows, cols in shapes]
        + [dma((12,)), dma((6, 2)), dma((6, 2)), dma((6,)), dma((6,))],
        cost_estimate=pl.CostEstimate(flops=2_000_000_000, bytes_accessed=20_000_000, transcendentals=0),
        compiler_params=pltpu.CompilerParams(collective_id=6, has_side_effects=True, vmem_limit_bytes=32 << 20),
        name="rep_sum",
    )(*arrays)


def rms_scale(values):
    return lax.rsqrt(jnp.mean(values * values, axis=-1, keepdims=True) + EPS)


def norm_back(grad_out, values, inv_scale, gain):
    scaled_grad = grad_out * gain
    inner = jnp.mean(scaled_grad * values, axis=-1, keepdims=True)
    return inv_scale * scaled_grad - values * inv_scale**3 * inner


def pad_heads(values, dim):
    shaped = values.reshape(values.shape[:-1] + (-1, dim))
    shaped = jnp.pad(shaped, [(0, 0)] * (shaped.ndim - 1) + [(0, LANES - dim)])
    return shaped.reshape(values.shape[:-1] + (-1,))


def cut_heads(values, dim):
    shaped = values.reshape(values.shape[:-1] + (-1, LANES))[..., :dim]
    return shaped.reshape(values.shape[:-1] + (-1,))


def on_device(
    inputs, segment_ids, valid_mask, input_weight, output_weight, conv_kernel, head_mix, first_gain, second_gain,
    group_gain, gate_weight, up_weight, down_weight, cotangent,
):
    tokens, width = inputs.shape[1:]
    heads, taps, span = conv_kernel.shape
    dim = width // heads
    scale = dim ** (-0.5)
    count = lax.axis_size("seq")
    team = FRAME // tokens
    own_heads = heads // team
    own_width = own_heads * dim
    own_pairs = own_heads // 2
    groups = [[g * team + i for i in range(team)] for g in range(count // team)]
    seq_rank = lax.axis_index("seq")
    place = seq_rank % team
    frame_first = (seq_rank // team) * FRAME
    row_first = seq_rank * tokens
    contract_rows = (((0,), (0,)), ((), ()))

    resid_in = inputs[0].astype(jnp.float32)
    grad_out = cotangent[0].astype(jnp.float32)
    row_valid = lax.dynamic_slice_in_dim(valid_mask[0], row_first, tokens).astype(jnp.float32)[:, None]
    ahead = lambda values: jnp.pad(values, (HEADER, 0))
    codes = make_codes(
        lax.dynamic_slice_in_dim(ahead(segment_ids[0]), frame_first, FRAME + HEADER),
        lax.dynamic_slice_in_dim(ahead(valid_mask[0]), frame_first, FRAME + HEADER),
    )
    own_kernel = lax.dynamic_slice_in_dim(conv_kernel, place * own_heads, own_heads)
    own_mix = lax.dynamic_slice_in_dim(head_mix, place * own_pairs, own_pairs).reshape(own_pairs, 4)
    own_gain = pad_heads(lax.dynamic_slice_in_dim(group_gain, place * own_width, own_width)[None], dim)
    toep, toep_split = split_toeplitz(toeplitz(own_kernel, scale))

    reps = lax.axis_size("rep")
    direct = team == 4 and reps == 4 and down_weight.shape[0] * 3 == width and (width // count) % (16 * reps) == 0
    first_scale = rms_scale(resid_in)
    normed_in = (resid_in * first_scale * first_gain).astype(jnp.bfloat16)
    if direct:
        own_input, normed_frame = gather_weight(input_weight, normed_in, reps, count)
    else:
        full_input = lax.all_gather(input_weight, "seq", axis=0, tiled=True)
        own_input = lax.dynamic_slice_in_dim(full_input.reshape(width, 3, width), place * own_width, own_width, axis=2)
        own_input = own_input.reshape(width, 3 * own_width)
        normed_frame = lax.all_gather(normed_in, "seq", axis=0, tiled=True, axis_index_groups=groups)
        ends = lax.all_gather(normed_in[tokens - HEADER :], "seq", axis=0)
        last = jnp.maximum(seq_rank // team * team - 1, 0)
        end = jnp.where(frame_first > 0, lax.dynamic_index_in_dim(ends, last, keepdims=False), 0)
        lead = jnp.zeros((EDGE - HEADER, width), jnp.bfloat16)
        normed_frame = jnp.concatenate([lead, end, normed_frame, jnp.zeros((EDGE, width), jnp.bfloat16)], axis=0)
    dmlp = (row_valid * grad_out).astype(jnp.bfloat16)
    own_input, output_weight, dmlp = lax.optimization_barrier((own_input, output_weight, dmlp))
    full_output = lax.all_gather(output_weight, "seq", axis=0, tiled=True)
    proj = jnp.dot(normed_frame, own_input, preferred_element_type=jnp.float32).astype(jnp.bfloat16)
    dmlp_all = lax.all_gather(dmlp, "seq", axis=0, tiled=True)
    normed_own, att, prob = attention_forward(proj, toep_split, codes, own_gain, own_mix, dim, taps)
    normed_own, full_output = lax.optimization_barrier((normed_own, full_output))

    def to_rows(values):
        moved = lax.all_to_all(
            values.reshape(team, tokens, own_width), "seq", 0, 0, tiled=True, axis_index_groups=groups
        )
        return moved.transpose(1, 0, 2).reshape(tokens, width)

    normed = frame_swap(normed_own) if direct else to_rows(normed_own)
    branch = jnp.dot(normed, full_output, preferred_element_type=jnp.float32)
    resid = resid_in + row_valid * branch
    second_scale = rms_scale(resid)
    normed_mid = (resid * second_scale * second_gain).astype(jnp.bfloat16)
    normed_mid, dmlp_all = lax.optimization_barrier((normed_mid, dmlp_all))
    inputs_all = lax.all_gather(normed_mid, "seq", axis=0, tiled=True)
    gate = jnp.dot(inputs_all, gate_weight, preferred_element_type=jnp.float32)
    up_proj = jnp.dot(inputs_all, up_weight, preferred_element_type=jnp.float32)
    dhidden = jnp.dot(dmlp_all, down_weight.T, preferred_element_type=jnp.float32)
    sigmoid_gate = jax.nn.sigmoid(gate)
    gate_grad = (dhidden * up_proj * sigmoid_gate * (1.0 + gate * (1.0 - sigmoid_gate))).astype(jnp.bfloat16)
    up_grad = (dhidden * gate * sigmoid_gate).astype(jnp.bfloat16)
    hidden = (jax.nn.silu(gate) * up_proj).astype(jnp.bfloat16)
    dmid_part = (
        jnp.dot(gate_grad, gate_weight.T, preferred_element_type=jnp.float32)
        + jnp.dot(up_grad, up_weight.T, preferred_element_type=jnp.float32)
    ).astype(jnp.bfloat16)
    gate_grad, up_grad, hidden, dmid_part = lax.optimization_barrier((gate_grad, up_grad, hidden, dmid_part))
    dmid_low = lax.psum_scatter(dmid_part, "seq", scatter_dimension=0, tiled=True)
    mlp_part = jnp.dot(hidden, down_weight, preferred_element_type=jnp.float32).astype(jnp.bfloat16)
    mlp_grads = [
        lax.dot_general(left, right, contract_rows, preferred_element_type=jnp.float32).astype(jnp.bfloat16)
        for left, right in ((inputs_all, gate_grad), (inputs_all, up_grad), (hidden, dmlp_all))
    ]
    if direct:
        mlp_grads = rep_sum(mlp_grads)
    dmid_low, mlp_part, mlp_grads = lax.optimization_barrier((dmid_low, mlp_part, mlp_grads))
    mlp_low = lax.psum_scatter(mlp_part, "seq", scatter_dimension=0, tiled=True)
    if direct:
        packed = lax.all_gather(mlp_grads, "rep", axis=0)
    else:
        mlp_grads = [lax.psum(value, "rep") for value in mlp_grads]
    dmid = dmid_low.astype(jnp.float32)
    second_part = jnp.sum(dmid * resid * second_scale, axis=0)
    dresid = grad_out + norm_back(dmid, resid, second_scale, second_gain)
    dbranch = (row_valid * dresid).astype(jnp.bfloat16)
    if direct:
        dbranch_frame = frame_gather(dbranch)
    else:
        dbranch_frame = lax.all_gather(dbranch, "seq", axis=0, tiled=True, axis_index_groups=groups)
    own_output = lax.dynamic_slice_in_dim(full_output, place * own_width, own_width, axis=0)
    dnormed_own = lax.dot_general(dbranch_frame, own_output, NT, preferred_element_type=jnp.float32)
    own_output_grad = lax.dot_general(normed_own, dbranch_frame, contract_rows, preferred_element_type=jnp.float32)
    own_output_grad = own_output_grad.astype(jnp.bfloat16)
    dproj, dtoep, dmix, dgain = attention_backward(
        proj, toep, codes, prob, att, dnormed_own, own_gain, own_mix, dim, taps, span
    )
    own_input_grad = lax.dot_general(normed_frame, dproj, contract_rows, preferred_element_type=jnp.float32)
    own_input_grad = own_input_grad.astype(jnp.bfloat16)
    dnormin_part = lax.dot_general(dproj, own_input, NT, preferred_element_type=jnp.float32).astype(jnp.bfloat16)
    def spread(values, size):
        empty = jnp.zeros((size,) + values.shape[1:], jnp.float32)
        return lax.dynamic_update_slice_in_dim(empty, values, place * values.shape[0], 0)

    kernel_part = spread(tap_grads(dtoep, taps, span, scale), heads)
    mix_part = spread(jnp.sum(dmix[:, :4], axis=-1).reshape(own_pairs, 2, 2), heads // 2)
    group_part = spread(cut_heads(dgain, dim)[0], width)
    parts = (kernel_part, mix_part, second_part, group_part)
    if direct:
        lines = lambda value: jnp.pad(value.reshape(-1), (0, -value.size % LANES)).reshape(-1, LANES)
        small = jnp.concatenate([jnp.zeros((width // LANES, LANES), jnp.float32)] + [lines(value) for value in parts])
        small = jnp.pad(small, ((0, -small.shape[0] % 8), (0, 0)))
        grad_input_w, grad_output_w, dnormin, small = reduce_weights(
            own_input_grad, own_output_grad, dnormin_part, resid_in * first_scale, small, reps, count
        )
        grad_first, others, start = small[: width // LANES].reshape(-1), [], width // LANES
        for value in parts:
            size = -(-value.size // LANES)
            others.append(small[start : start + size].reshape(-1)[: value.size].reshape(value.shape))
            start += size
    else:
        dnormin = lax.psum_scatter(
            dnormin_part[EDGE : EDGE + FRAME], "seq", scatter_dimension=0, tiled=True, axis_index_groups=groups
        ).astype(jnp.float32)
        starts = lax.all_gather(dnormin_part[EDGE - HEADER : EDGE], "seq", axis=0).astype(jnp.float32)
        later = lax.dynamic_slice_in_dim(
            jnp.pad(starts, ((0, team), (0, 0), (0, 0))), (seq_rank // team + 1) * team, team
        ).sum(axis=0)
        later = jnp.where(place == team - 1, later, 0.0)
        dnormin = dnormin + jnp.pad(later, ((tokens - HEADER, 0), (0, 0)))
        pieces = lax.all_to_all(own_input_grad.reshape(count, width // count, 3 * own_width), "seq", 0, 0, tiled=True)
        pieces = pieces.reshape(count // team, team, width // count, 3, own_width).astype(jnp.float32).sum(axis=0)
        grad_input_w = pieces.transpose(1, 2, 0, 3).reshape(width // count, 3 * width)
        spots = jnp.zeros((width, width), jnp.bfloat16)
        spots = lax.dynamic_update_slice_in_dim(spots, own_output_grad, place * own_width, 0)
        grad_output_w = lax.psum_scatter(spots, "seq", scatter_dimension=0, tiled=True)
        grad_input_w, grad_output_w = [
            lax.psum(value.astype(jnp.bfloat16), "rep") for value in (grad_input_w, grad_output_w)
        ]
    dnormin, mlp_low, mlp_sums = lax.optimization_barrier((dnormin, mlp_low, packed if direct else mlp_grads))
    if direct:
        packed = mlp_sums
    else:
        mlp_grads = mlp_sums
    result = resid + row_valid * mlp_low.astype(jnp.float32)
    if not direct:
        first_part = jnp.sum(dnormin * resid_in * first_scale, axis=0)
        grad_first, others = lax.psum((first_part, parts), ("rep", "seq"))
    grad_in = dresid + norm_back(dnormin, resid_in, first_scale, first_gain)

    grad_kernel, grad_mix, grad_second, grad_group = others
    if direct:
        units = down_weight.shape[0]
        mlp_grads = [
            packed[:, :, :units].reshape(width, units),
            packed[:, :, units : 2 * units].reshape(width, units),
            packed[:, :, 2 * units :].reshape(reps, 3, units // reps, units).transpose(0, 2, 1, 3).reshape(units, width),
        ]
    grads = [value.astype(jnp.float32) for value in (grad_input_w, grad_output_w, *mlp_grads)]
    return (
        result.astype(jnp.bfloat16)[None], grad_in.astype(jnp.bfloat16)[None], grads[0], grads[1], grad_kernel,
        grad_mix, grad_first, grad_second, grad_group, grads[2], grads[3], grads[4],
    )


def solution(mesh):
    in_specs = (
        P("rep", "seq", None), P("rep", None), P("rep", None), P("seq", None), P("seq", None), P(), P(), P(), P(), P(),
        P(None, "seq"), P(None, "seq"), P("seq", None), P("rep", "seq", None),
    )
    out_specs = (
        P("rep", "seq", None), P("rep", "seq", None), P("seq", None), P("seq", None), P(), P(), P(), P(), P(),
        P(None, "seq"), P(None, "seq"), P("seq", None),
    )
    return jax.shard_map(on_device, mesh=mesh, in_specs=in_specs, out_specs=out_specs, check_vma=False)
```
